32 devices in a mesh: member: 2 (over x), patch: 8 (over z, y), feat: 2 (over core).
Axes of the slice: x: 2, y: 2, z: 4, core: 2. Of those that a mesh axis runs over, the one named last changes fastest.
Arguments:
- node_state: bfloat16 [81920, 512], P(('member', 'patch')), parts along dimension 0, may hold values from -6 to 6
- fine_tile: bfloat16 [320, 4, 128, 128], P('patch'), may hold values from -3 to 3
- coarse_tile: bfloat16 [320, 128, 160], P('patch'), may hold values from -3 to 3
- fine_index: int32 [320, 4], P('patch'), may hold values from 0 to 319, as said below
- coarse_index: int32 [320, 4], P('patch'), may hold values from 0 to 7
- node_degree: int32 [40960], P('patch'), may hold values from 4 to 12
- w_msg: bfloat16 [2, 512, 512], P(None, None, 'feat'), may hold values from -0.25 to 0.25
- w_in: bfloat16 [2, 1024, 512], P(None, None, 'feat'), may hold values from -0.1875 to 0.1875
- w_out: bfloat16 [2, 512, 512], P(None, 'feat'), may hold values from -0.25 to 0.25
Outputs:
- new_state: bfloat16 [81920, 512], P(('member', 'patch')), parts along dimension 0
The draws below stay inside these ranges and needn't reach their ends.
There are 2 independent parts, one for each index of `member`. The reference program is written for one: setup_inputs(seed, part) draws one part's arguments, and reference() takes and returns one part's arrays. A program takes and returns all parts, laid end to end along the dimension named above; an argument that names none is the same for every part. Nothing has to cross between parts.
Inputs may be any that keep to these rules, and one draw needn't show every extreme that they name: `fine_index`: slot 0 of row b is b itself; every entry of row b lies within 20 blocks of the block range of the patch that holds block b, and the rows of a patch's first and last blocks reach the farthest such block on the side of a neighbouring patch.
All inputs are finite; a program needn't handle non-finite values.
Results may differ from the reference program's by a relative error of at most 0.014.
Values may be sent and summed in bfloat16 or wider, within the bound.
No kernel may reach another device: no remote copies, remote signals or barrier semaphores. Data moves between devices by JAX's collectives and lax.ppermute only.
A program may use at most 192 MiB of HBM per device.

```python
import jax
import jax.numpy as jnp
from jax import lax

D = 512
NB_DEV = 40
BLK = 128
KB = 4
KC = 4
CN_DEV = 40
LAYERS = 2
HALO_BLK = 20
NBLK = 320
NODES = 40960
N_PATCH = 8
N_FEAT = 2


def draw_fine_index(key, part):
    total_blocks = NB_DEV * N_PATCH
    block_ids = jnp.arange(total_blocks, dtype=jnp.int32)
    owner = block_ids // NB_DEV
    lowest = jnp.maximum(owner * NB_DEV - HALO_BLK, 0)
    highest = jnp.minimum((owner + 1) * NB_DEV + HALO_BLK, total_blocks)
    raw = jax.random.randint(key, (total_blocks, KB), 0, 1 << 20, dtype=jnp.int32)
    links = lowest[:, None] + raw % (highest - lowest)[:, None]
    local_pos = block_ids % NB_DEV
    first_fix = jnp.where((local_pos == 0) & (owner > 0), owner * NB_DEV - HALO_BLK, links[:, 1])
    last_fix = jnp.where((local_pos == NB_DEV - 1) & (owner < N_PATCH - 1), (owner + 1) * NB_DEV + HALO_BLK - 1, first_fix)
    links = links.at[:, 0].set(block_ids)
    links = links.at[:, 1].set(last_fix)
    return links.astype(jnp.int32)


def plant(drawn, own_key, low, high):
    spot = [jax.random.randint(jax.random.fold_in(own_key, axis), (), 0, length) for axis, length in enumerate(drawn.shape)]
    widest = drawn.shape.index(max(drawn.shape))
    next_to = spot[:widest] + [(spot[widest] + 1) % drawn.shape[widest]] + spot[widest + 1:]
    return drawn.at[tuple(spot)].set(low).at[tuple(next_to)].set(high)


def steps_of(stream_key, shape, split, least, high):
    def one(dim, blocks):
        heights = jax.random.uniform(jax.random.fold_in(jax.random.fold_in(stream_key, 6), dim), (blocks,), jnp.float32, least / len(split), high / len(split))
        return jnp.repeat(jnp.exp(heights), shape[dim] // blocks).reshape((-1,) + (1,) * (len(shape) - dim - 1))

    gain = one(*split[0])
    for cut in split[1:]:
        gain = gain * one(*cut)
    return gain


def scatter_about(stream_key, dims, scale, most, pieces=(), held_as=jnp.bfloat16):
    factor_of = steps_of(stream_key, dims, pieces, -0.22, 0.18) if pieces else 1.0
    result = jax.random.normal(stream_key, dims, jnp.float32) * scale * factor_of
    return jnp.minimum(jnp.maximum(result, -most), most).astype(held_as)


def setup_inputs(seed: int = 0, part: int = 0) -> dict:
    key_of = jax.random.split(jax.random.key(seed), 10)
    part_splits = jax.random.split(jax.random.fold_in(key_of[9], part), 10)
    node_state = scatter_about(part_splits[0], (NODES, D), 1.0, 6.0, ((0, 8),))
    fine_tile = scatter_about(key_of[1], (NBLK, KB, BLK, BLK), 0.5, 3.0, ((0, 8),))
    coarse_tile = scatter_about(key_of[2], (NBLK, BLK, KC * CN_DEV), 0.5, 3.0, ((0, 8),))
    fine_index = draw_fine_index(jax.random.fold_in(key_of[9], 71), part)
    coarse_index = plant(jax.random.randint(key_of[4], (NBLK, KC), 0, N_PATCH), jax.random.fold_in(key_of[4], 1), 0, N_PATCH - 1).astype(jnp.int32)
    node_degree = plant(jax.random.randint(key_of[5], (NODES,), 4, 13), jax.random.fold_in(key_of[5], 1), 4, 12).astype(jnp.int32)
    w_msg = scatter_about(key_of[6], (LAYERS, D, D), D ** -0.5, 0.25, ((2, 2),))
    w_in = scatter_about(key_of[7], (LAYERS, 2 * D, D), (2 * D) ** -0.5, 0.1875, ((2, 2),))
    w_out = scatter_about(key_of[8], (LAYERS, D, D), D ** -0.5, 0.25, ((1, 2),))
    return dict(node_state=node_state, fine_tile=fine_tile, coarse_tile=coarse_tile, fine_index=fine_index, coarse_index=coarse_index, node_degree=node_degree, w_msg=w_msg, w_in=w_in, w_out=w_out)


def layer_norm(values):
    center = values - lax.optimization_barrier(jnp.mean(values, axis=-1, keepdims=True))
    spread = lax.optimization_barrier(jnp.mean(center * center, axis=-1, keepdims=True))
    return center * lax.rsqrt(spread + 1e-05)

def reference(node_state, fine_tile, coarse_tile, fine_index, coarse_index, node_degree, w_msg, w_in, w_out):
    state = node_state
    total_blocks = NB_DEV * N_PATCH
    half_hidden = D // N_FEAT
    for layer_pos in range(LAYERS):
        normed = layer_norm(state.astype(jnp.float32)).astype(jnp.bfloat16)
        message = jax.nn.silu(jnp.dot(normed, w_msg[layer_pos], preferred_element_type=jnp.float32)).astype(jnp.bfloat16)
        blocks = message.reshape(total_blocks, BLK, D)
        coarse_rows = message.reshape(N_PATCH, NB_DEV * BLK, D)[:, :CN_DEV, :]

        def one_block(item):
            tiles, links, coarse_weights, coarse_links = item
            chosen = blocks[links].astype(jnp.float32)
            summed = jnp.einsum('krs,ksd->rd', tiles.astype(jnp.float32), chosen)
            coarse_chosen = coarse_rows[coarse_links].reshape(KC * CN_DEV, D)
            return summed + jnp.dot(coarse_weights, coarse_chosen, preferred_element_type=jnp.float32)
        summed = lax.map(one_block, (fine_tile, fine_index, coarse_tile, coarse_index))
        aggregate = (summed.reshape(NODES, D) / node_degree[:, None].astype(jnp.float32)).astype(jnp.bfloat16)
        joined = layer_norm(jnp.concatenate([state.astype(jnp.float32), aggregate.astype(jnp.float32)], axis=1)).astype(jnp.bfloat16)
        hidden = jax.nn.silu(jnp.dot(joined, w_in[layer_pos], preferred_element_type=jnp.float32)).astype(jnp.bfloat16)
        update = jnp.zeros((NODES, D), jnp.float32)
        for piece_pos in range(N_FEAT):
            lower = piece_pos * half_hidden
            partial_sum = jnp.dot(hidden[:, lower:lower + half_hidden], w_out[layer_pos][lower:lower + half_hidden], preferred_element_type=jnp.float32)
            rounded = lax.optimization_barrier(partial_sum.astype(jnp.bfloat16))
            update = update + rounded.astype(jnp.float32)
        state = (state.astype(jnp.float32) + update).astype(jnp.bfloat16)
    return state
```

```python
import functools

import jax
import jax.numpy as jnp
from jax import lax
from jax.experimental import pallas as pl
from jax.experimental.pallas import tpu as pltpu
from jax.sharding import PartitionSpec as P

CN_DEV = 40
LAYERS = 2
HALO_BLK = 20
CHUNKS = 2
ROW_TILE = 256
BLOCK_STEP = 5
VMEM_BYTES = 56 << 20
F32 = jnp.float32
BF16 = jnp.bfloat16


def silu(v):
    return 0.5 * v * (1.0 + jnp.tanh(0.5 * v))


def dot(a, b):
    return jnp.dot(a, b, preferred_element_type=F32)


def normalize(parts):
    width = sum(part.shape[-1] for part in parts)
    mean = sum(jnp.sum(part, axis=-1, keepdims=True) for part in parts) / width
    center = [part - mean for part in parts]
    spread = sum(jnp.sum(part * part, axis=-1, keepdims=True) for part in center) / width
    scale = lax.rsqrt(spread + 1e-05)
    return [(part * scale).astype(BF16) for part in center]


def params():
    return pltpu.CompilerParams(vmem_limit_bytes=VMEM_BYTES)


def message_kernel(state_ref, weight_ref, out_ref):
    (normed,) = normalize([state_ref[...].astype(F32)])
    out_ref[...] = silu(dot(normed, weight_ref[...])).astype(BF16)


def message_call(state, weight, start, rows, tile):
    first = start // tile
    return pl.pallas_call(
        message_kernel,
        grid=(rows // tile,),
        in_specs=[
            pl.BlockSpec((tile, state.shape[1]), lambda i: (first + i, 0)),
            pl.BlockSpec(weight.shape, lambda i: (0, 0)),
        ],
        out_specs=pl.BlockSpec((tile, weight.shape[1]), lambda i: (i, 0)),
        out_shape=jax.ShapeDtypeStruct((rows, weight.shape[1]), BF16),
        compiler_params=params(),
        name="message",
    )(state, weight)


def aggregate_kernel(pieces, chunk, half, scal, *refs):
    piece_refs = refs[:pieces]
    coarse_ref, fine_ref, ctile_ref, degree_ref, send_ref, keep_ref, table, coarse_f32, sems = refs[pieces:]
    slot = pl.program_id(0)
    step = pl.program_id(1)
    copies = [
        pltpu.make_async_copy(ref, table.at[pl.ds(scal[1 + pos], ref.shape[0])], sems.at[pos])
        for pos, ref in enumerate(piece_refs)
    ]

    @pl.when((slot == 0) & (step == 0))
    def _():
        for copy in copies:
            copy.start()
        coarse_f32[...] = coarse_ref[...].astype(F32)
        for copy in copies:
            copy.wait()

    feat = scal[0]
    which = jnp.where(slot == 0, 1 - feat, feat)
    count, block, _ = ctile_ref.shape
    kinds = fine_ref.shape[1]
    first = which * half + chunk * (half // CHUNKS) + step * count
    base = 1 + pieces
    coarse_base = base + 2 * half * kinds
    degree = jnp.transpose(degree_ref[0].astype(F32))
    results = []
    for pos in range(count):
        row = (first + pos) * kinds
        chosen = jnp.concatenate([table[scal[base + row + k]] for k in range(kinds)], axis=0)
        tiles = jnp.concatenate([fine_ref[pos, k] for k in range(kinds)], axis=1)
        stacked = jnp.concatenate(
            [
                coarse_f32[pl.ds(pl.multiple_of(scal[coarse_base + row + k], 8), CN_DEV), :]
                for k in range(kinds)
            ],
            axis=0,
        ).astype(BF16)
        summed = dot(tiles, chosen) + dot(ctile_ref[pos], stacked)
        results.append((summed / degree[:, pos : pos + 1]).astype(BF16))

    @pl.when(slot == 0)
    def _():
        for pos in range(count):
            send_ref[pos * block : (pos + 1) * block, :] = results[pos]

    @pl.when(slot == 1)
    def _():
        for pos in range(count):
            keep_ref[pos * block : (pos + 1) * block, :] = results[pos]


def aggregate_call(scal, pieces, coarse, fine_tile, coarse_tile, degree, chunk):
    blocks, kinds, block, _ = fine_tile.shape
    half = blocks // 2
    steps = half // CHUNKS // BLOCK_STEP
    columns = coarse.shape[1]
    rows = half // CHUNKS * block

    def place(slot, step, scal):
        which = jnp.where(slot == 0, 1 - scal[0], scal[0])
        return which * (half // BLOCK_STEP) + chunk * steps + step

    table_blocks = sum(piece.shape[0] for piece in pieces)
    return pl.pallas_call(
        functools.partial(aggregate_kernel, len(pieces), chunk, half),
        grid_spec=pltpu.PrefetchScalarGridSpec(
            num_scalar_prefetch=1,
            grid=(2, steps),
            in_specs=[pl.BlockSpec(memory_space=pl.ANY) for _ in pieces]
            + [
                pl.BlockSpec(coarse.shape, lambda s, i, scal: (0, 0)),
                pl.BlockSpec((BLOCK_STEP, kinds, block, block), lambda s, i, scal: (place(s, i, scal), 0, 0, 0)),
                pl.BlockSpec((BLOCK_STEP, block, coarse_tile.shape[2]), lambda s, i, scal: (place(s, i, scal), 0, 0)),
                pl.BlockSpec((1, BLOCK_STEP, block), lambda s, i, scal: (place(s, i, scal), 0, 0)),
            ],
            out_specs=[
                pl.BlockSpec((BLOCK_STEP * block, columns), lambda s, i, scal: (jnp.where(s == 0, i, steps - 1), 0)),
                pl.BlockSpec((BLOCK_STEP * block, columns), lambda s, i, scal: (jnp.where(s == 1, i, 0), 0)),
            ],
            scratch_shapes=[
                pltpu.VMEM((table_blocks, block, columns), BF16),
                pltpu.VMEM(coarse.shape, F32),
                pltpu.SemaphoreType.DMA((len(pieces),)),
            ],
        ),
        out_shape=[jax.ShapeDtypeStruct((rows, columns), BF16)] * 2,
        compiler_params=params(),
        name="aggregate",
    )(scal, *pieces, coarse, fine_tile, coarse_tile, degree)


def node_kernel(last, scal, state_ref, keep_ref, recv_ref, in_own, in_other, out_own, out_other, *refs):
    feat = scal[0]
    width = state_ref.shape[1]
    columns = keep_ref.shape[1]
    state = state_ref[...].astype(F32)
    joined = normalize([state, keep_ref[...].astype(F32), recv_ref[...].astype(F32)])
    keep_at = pl.multiple_of(width + feat * columns, columns)
    recv_at = pl.multiple_of(width + (1 - feat) * columns, columns)
    update = None
    for in_ref, out_ref in ((in_own, out_own), (in_other, out_other)):
        hidden = (
            dot(joined[0], in_ref[0, :width, :])
            + dot(joined[1], in_ref[0, pl.ds(keep_at, columns), :])
            + dot(joined[2], in_ref[0, pl.ds(recv_at, columns), :])
        )
        part = dot(silu(hidden).astype(BF16), out_ref[0])
        update = part if update is None else update + part
    new_state = (state + update).astype(BF16)
    if last:
        (state_out,) = refs
        state_out[...] = new_state
        return
    msg_own, msg_other, state_out, own_out, other_out = refs
    state_out[...] = new_state
    (normed,) = normalize([new_state.astype(F32)])
    own_out[...] = silu(dot(normed, msg_own[0])).astype(BF16)
    other_out[...] = silu(dot(normed, msg_other[0])).astype(BF16)


def node_call(scal, state, per_half, chunk, keep, recv, weights_in, weights_out, weights_msg, layer):
    rows, columns = keep.shape
    width = state.shape[1]
    last = weights_msg is None
    steps = rows // ROW_TILE

    def place(i, scal):
        return (scal[0] * per_half + chunk) * steps + i, 0

    def whole(array, at):
        return pl.BlockSpec((1,) + array.shape[1:], lambda i, scal: (at, 0, 0))

    tile = pl.BlockSpec((ROW_TILE, columns), lambda i, scal: (i, 0))
    operands = [state, keep, recv, *weights_in, *weights_out]
    in_specs = [pl.BlockSpec((ROW_TILE, width), place), tile, tile]
    in_specs += [whole(array, layer) for array in (*weights_in, *weights_out)]
    out_specs = [pl.BlockSpec((ROW_TILE, width), lambda i, scal: (i, 0))]
    out_shape = [jax.ShapeDtypeStruct((rows, width), BF16)]
    if not last:
        operands += list(weights_msg)
        in_specs += [whole(array, layer) for array in weights_msg]
        out_specs += [tile, tile]
        out_shape += [jax.ShapeDtypeStruct((rows, columns), BF16)] * 2
    return pl.pallas_call(
        functools.partial(node_kernel, last),
        grid_spec=pltpu.PrefetchScalarGridSpec(
            num_scalar_prefetch=1, grid=(steps,), in_specs=in_specs, out_specs=out_specs
        ),
        out_shape=out_shape,
        compiler_params=params(),
        name="node",
    )(scal, *operands)


def assemble_kernel(pieces, scal, *refs):
    piece_refs = refs[:pieces]
    out_ref, sems = refs[pieces:]
    copies = [
        pltpu.make_async_copy(
            ref, out_ref.at[pl.ds(pl.multiple_of(scal[pos], 8), ref.shape[0])], sems.at[pos]
        )
        for pos, ref in enumerate(piece_refs)
    ]
    for copy in copies:
        copy.start()
    for copy in copies:
        copy.wait()


def assemble_call(offsets, pieces):
    rows = sum(piece.shape[0] for piece in pieces)
    return pl.pallas_call(
        functools.partial(assemble_kernel, len(pieces)),
        grid_spec=pltpu.PrefetchScalarGridSpec(
            num_scalar_prefetch=1,
            in_specs=[pl.BlockSpec(memory_space=pl.ANY) for _ in pieces],
            out_specs=pl.BlockSpec(memory_space=pl.ANY),
            scratch_shapes=[pltpu.SemaphoreType.DMA((len(pieces),))],
        ),
        out_shape=jax.ShapeDtypeStruct((rows, pieces[0].shape[1]), pieces[0].dtype),
        compiler_params=params(),
        name="assemble",
    )(offsets, *pieces)


def swap_feat(array):
    return lax.ppermute(array, "feat", [(0, 1), (1, 0)])


def gather_patches(rows):
    count = lax.axis_size("patch")
    held = rows
    have = 1
    while have < count:
        more = min(have, count - have)
        pairs = [(pos, (pos - have) % count) for pos in range(count)]
        got = lax.ppermute(held[: more * rows.shape[0]], "patch", pairs)
        held = jnp.concatenate([held, got], axis=0)
        have += more
    return held


def shards(
    node_state, fine_tile, coarse_tile, fine_index, coarse_index, node_degree, w_msg, w_in, w_out
):
    patches = lax.axis_size("patch")
    patch_pos = lax.axis_index("patch")
    feat = lax.axis_index("feat")
    blocks, kinds, block, _ = fine_tile.shape
    half = blocks // 2
    half_rows = half * block
    halo_rows = HALO_BLK * block
    assert half == HALO_BLK and half % (CHUNKS * BLOCK_STEP) == 0
    columns = w_msg.shape[2]
    degree = node_degree.reshape(blocks // BLOCK_STEP, BLOCK_STEP, block)

    links = (fine_index - (patch_pos * blocks - HALO_BLK)).reshape(-1)
    coarse_links = ((coarse_index - patch_pos) % patches * CN_DEV).reshape(-1)

    def scalars(*places):
        head = jnp.stack([jnp.asarray(value, jnp.int32) for value in (feat, *places)])
        return jnp.concatenate([head, links, coarse_links])

    forward = [(pos, pos + 1) for pos in range(patches - 1)]
    backward = [(target, source) for source, target in forward]
    coarse_state = gather_patches(node_state[:CN_DEV])

    low = message_call(node_state, w_msg[0], 0, half_rows, 512)
    high_halo = lax.ppermute(low, "patch", backward)
    high = message_call(node_state, w_msg[0], half_rows, half_rows, 512)
    low_halo = lax.ppermute(high, "patch", forward)
    w_in, w_out, w_msg_late, _ = lax.optimization_barrier((w_in, w_out, w_msg[1:], high))
    weights_in = (w_in, swap_feat(w_in))
    weights_out = (w_out, swap_feat(w_out))
    weights_msg = (w_msg_late, swap_feat(w_msg_late))
    coarse = message_call(coarse_state, w_msg[0], 0, coarse_state.shape[0], coarse_state.shape[0])

    own_patch = [(2 * src + side, 2 * dst + side) for side, pairs in ((0, backward), (1, forward)) for src, dst in pairs]
    other_patch = [(2 * src + side, 2 * dst + 1 - side) for side, pairs in ((0, backward), (1, forward)) for src, dst in pairs]

    pieces = [low_halo, low, high, high_halo]
    scal = scalars(0, HALO_BLK, HALO_BLK + half, HALO_BLK + blocks)
    chunk_blocks = half // CHUNKS
    late_places = []
    for chunk in range(CHUNKS):
        at = chunk * chunk_blocks
        own = HALO_BLK + feat * half + at
        other = HALO_BLK + (1 - feat) * half + at
        near = jnp.where(feat == 0, HALO_BLK + blocks, 0) + at
        far = jnp.where(feat == 0, 0, HALO_BLK + blocks) + at
        late_places += [own, other, near, far]
    late_scal = scalars(*late_places)

    states = [node_state] * CHUNKS
    for layer in range(LAYERS):
        last = layer == LAYERS - 1
        shaped = [piece.reshape(-1, block, columns) for piece in pieces]
        sums = [
            aggregate_call(scal, shaped, coarse, fine_tile, coarse_tile, degree, chunk)
            for chunk in range(CHUNKS)
        ]
        received = [swap_feat(send) for send, _ in sums]
        new_states = []
        pieces = []
        for chunk in range(CHUNKS):
            results = node_call(
                scal, states[chunk], CHUNKS if layer == 0 else 0, chunk if layer == 0 else 0,
                sums[chunk][1], received[chunk], weights_in, weights_out,
                None if last else weights_msg, layer,
            )
            new_states.append(results[0])
            if not last:
                own, other = results[1:]
                near = lax.ppermute(own, ("patch", "feat"), own_patch)
                far = lax.ppermute(other, ("patch", "feat"), other_patch)
                sibling = swap_feat(other)
                pieces += [own, sibling, near, far]
                if chunk == 0:
                    mine = jnp.where(feat == 0, own[:CN_DEV], sibling[:CN_DEV])
                    coarse = gather_patches(mine)
        states = new_states
        scal = late_scal

    parts = []
    offsets = []
    chunk_rows = half_rows // CHUNKS
    for chunk in range(CHUNKS):
        parts += [states[chunk], swap_feat(states[chunk])]
        offsets += [feat * half_rows + chunk * chunk_rows, (1 - feat) * half_rows + chunk * chunk_rows]
    return assemble_call(jnp.stack(offsets).astype(jnp.int32), parts)


def solution(mesh):
    return jax.shard_map(
        shards,
        mesh=mesh,
        in_specs=(
            P(("member", "patch"), None),
            P("patch", None, None, None),
            P("patch", None, None),
            P("patch", None),
            P("patch", None),
            P("patch"),
            P(None, None, "feat"),
            P(None, None, "feat"),
            P(None, "feat", None),
        ),
        out_specs=P(("member", "patch"), None),
        check_vma=False,
    )
```

```python
import functools

import jax
import jax.numpy as jnp
from jax import lax
from jax.experimental import pallas as pl
from jax.experimental.pallas import tpu as pltpu
from jax.sharding import PartitionSpec as P

CN_DEV = 40
LAYERS = 2
HALO_BLK = 20
CHUNKS = 2
ROW_TILE = 640
BLOCK_STEP = 10
MESSAGE_TILE = 1280
VMEM_BYTES = 28 << 20
F32 = jnp.float32
BF16 = jnp.bfloat16


def silu(v):
    return 0.5 * v * (1.0 + jnp.tanh(0.5 * v))


def dot(a, b):
    return jnp.dot(a, b, preferred_element_type=F32)


def normalize(parts):
    width = sum(part.shape[-1] for part in parts)
    mean = sum(jnp.sum(part, axis=-1, keepdims=True) for part in parts) / width
    center = [part - mean for part in parts]
    spread = sum(jnp.sum(part * part, axis=-1, keepdims=True) for part in center) / width
    scale = lax.rsqrt(spread + 1e-05)
    return [(part * scale).astype(BF16) for part in center]


def params():
    return pltpu.CompilerParams(vmem_limit_bytes=VMEM_BYTES)


def message_kernel(state_ref, weight_ref, out_ref):
    (normed,) = normalize([state_ref[...].astype(F32)])
    out_ref[...] = silu(dot(normed, weight_ref[...])).astype(BF16)


def message_call(state, weight, start, rows, tile):
    first = start // tile
    return pl.pallas_call(
        message_kernel,
        grid=(rows // tile,),
        in_specs=[
            pl.BlockSpec((tile, state.shape[1]), lambda i: (first + i, 0)),
            pl.BlockSpec(weight.shape, lambda i: (0, 0)),
        ],
        out_specs=pl.BlockSpec((tile, weight.shape[1]), lambda i: (i, 0)),
        out_shape=jax.ShapeDtypeStruct((rows, weight.shape[1]), BF16),
        compiler_params=params(),
        name="message",
    )(state, weight)


def aggregate_kernel(pieces, chunk, half, scal, *refs):
    piece_refs = refs[:pieces]
    coarse_ref, fine_ref, ctile_ref, degree_ref, send_ref, keep_ref, table, coarse_f32, sems = refs[pieces:]
    slot = pl.program_id(0)
    step = pl.program_id(1)
    copies = [
        pltpu.make_async_copy(ref, table.at[pl.ds(scal[1 + pos], ref.shape[0])], sems.at[pos])
        for pos, ref in enumerate(piece_refs)
    ]

    @pl.when((slot == 0) & (step == 0))
    def _():
        for copy in copies:
            copy.start()
        coarse_f32[...] = coarse_ref[...].astype(F32)
        for copy in copies:
            copy.wait()

    feat = scal[0]
    which = jnp.where(slot == 0, 1 - feat, feat)
    count, block, _ = ctile_ref.shape
    kinds = fine_ref.shape[1]
    first = which * half + chunk * (half // CHUNKS) + step * count
    base = 1 + pieces
    coarse_base = base + 2 * half * kinds
    degree = jnp.transpose(degree_ref[0].astype(F32))
    results = []
    for pos in range(count):
        row = (first + pos) * kinds
        chosen = jnp.concatenate([table[scal[base + row + k]] for k in range(kinds)], axis=0)
        tiles = jnp.concatenate([fine_ref[pos, k] for k in range(kinds)], axis=1)
        stacked = jnp.concatenate(
            [
                coarse_f32[pl.ds(pl.multiple_of(scal[coarse_base + row + k], 8), CN_DEV), :]
                for k in range(kinds)
            ],
            axis=0,
        ).astype(BF16)
        summed = dot(tiles, chosen) + dot(ctile_ref[pos], stacked)
        results.append((summed / degree[:, pos : pos + 1]).astype(BF16))

    @pl.when(slot == 0)
    def _():
        for pos in range(count):
            send_ref[pos * block : (pos + 1) * block, :] = results[pos]

    @pl.when(slot == 1)
    def _():
        for pos in range(count):
            keep_ref[pos * block : (pos + 1) * block, :] = results[pos]


def aggregate_call(scal, pieces, coarse, fine_tile, coarse_tile, degree, chunk):
    blocks, kinds, block, _ = fine_tile.shape
    half = blocks // 2
    steps = half // CHUNKS // BLOCK_STEP
    columns = coarse.shape[1]
    rows = half // CHUNKS * block

    def place(slot, step, scal):
        which = jnp.where(slot == 0, 1 - scal[0], scal[0])
        return which * (half // BLOCK_STEP) + chunk * steps + step

    table_blocks = sum(piece.shape[0] for piece in pieces)
    return pl.pallas_call(
        functools.partial(aggregate_kernel, len(pieces), chunk, half),
        grid_spec=pltpu.PrefetchScalarGridSpec(
            num_scalar_prefetch=1,
            grid=(2, steps),
            in_specs=[pl.BlockSpec(memory_space=pl.ANY) for _ in pieces]
            + [
                pl.BlockSpec(coarse.shape, lambda s, i, scal: (0, 0)),
                pl.BlockSpec((BLOCK_STEP, kinds, block, block), lambda s, i, scal: (place(s, i, scal), 0, 0, 0)),
                pl.BlockSpec((BLOCK_STEP, block, coarse_tile.shape[2]), lambda s, i, scal: (place(s, i, scal), 0, 0)),
                pl.BlockSpec((1, BLOCK_STEP, block), lambda s, i, scal: (place(s, i, scal), 0, 0)),
            ],
            out_specs=[
                pl.BlockSpec((BLOCK_STEP * block, columns), lambda s, i, scal: (jnp.where(s == 0, i, steps - 1), 0)),
                pl.BlockSpec((BLOCK_STEP * block, columns), lambda s, i, scal: (jnp.where(s == 1, i, 0), 0)),
            ],
            scratch_shapes=[
                pltpu.VMEM((table_blocks, block, columns), BF16),
                pltpu.VMEM(coarse.shape, F32),
                pltpu.SemaphoreType.DMA((len(pieces),)),
            ],
        ),
        out_shape=[jax.ShapeDtypeStruct((rows, columns), BF16)] * 2,
        compiler_params=params(),
        name="aggregate",
    )(scal, *pieces, coarse, fine_tile, coarse_tile, degree)


def node_kernel(mode, scal, state_ref, keep_ref, recv_ref, in_own, in_other, out_own, out_other, *refs):
    feat = scal[0]
    width = state_ref.shape[1]
    columns = keep_ref.shape[1]
    state = state_ref[...].astype(F32)
    joined = normalize([state, keep_ref[...].astype(F32), recv_ref[...].astype(F32)])
    keep_at = pl.multiple_of(width + feat * columns, columns)
    recv_at = pl.multiple_of(width + (1 - feat) * columns, columns)
    update = None
    for in_ref, out_ref in ((in_own, out_own), (in_other, out_other)):
        hidden = (
            dot(joined[0], in_ref[0, :width, :])
            + dot(joined[1], in_ref[0, pl.ds(keep_at, columns), :])
            + dot(joined[2], in_ref[0, pl.ds(recv_at, columns), :])
        )
        part = dot(silu(hidden).astype(BF16), out_ref[0])
        update = part if update is None else update + part
    new_state = (state + update).astype(BF16)
    if mode == "last":
        refs[-2][...] = new_state
        refs[-1][...] = new_state
        return
    (normed,) = normalize([new_state.astype(F32)])
    if mode == "coarse":
        msg_own, own_out = refs
        own_out[...] = silu(dot(normed, msg_own[0])).astype(BF16)
        return
    msg_own, msg_other, state_out, own_out, other_out = refs
    state_out[...] = new_state
    own_out[...] = silu(dot(normed, msg_own[0])).astype(BF16)
    other_out[...] = silu(dot(normed, msg_other[0])).astype(BF16)


def node_call(mode, scal, state, per_half, chunk, keep, recv, weights_in, weights_out, weights_msg, layer, out=None, total=0):
    rows, columns = keep.shape
    width = state.shape[1]
    row_tile = min(rows, ROW_TILE)
    steps = rows // row_tile

    def place(i, scal):
        return ((scal[0] * per_half + chunk) * steps if per_half else 0) + i, 0

    def place_out(i, scal):
        return (scal[0] * CHUNKS + chunk) * steps + i, 0

    def whole(array, at):
        return pl.BlockSpec((1,) + array.shape[1:], lambda i, scal: (at, 0, 0))

    tile = pl.BlockSpec((row_tile, columns), lambda i, scal: (i, 0))
    state_tile = pl.BlockSpec((row_tile, width), lambda i, scal: (i, 0))
    message_shape = jax.ShapeDtypeStruct((rows, columns), BF16)
    state_shape = jax.ShapeDtypeStruct((rows, width), BF16)
    operands = [state, keep, recv, *weights_in, *weights_out]
    in_specs = [pl.BlockSpec((row_tile, width), place), tile, tile]
    in_specs += [whole(array, layer) for array in (*weights_in, *weights_out)]
    aliases = {}
    if mode == "last":
        out_specs = [state_tile, pl.BlockSpec((row_tile, width), place_out)]
        out_shape = [state_shape, jax.ShapeDtypeStruct((total, width), BF16)]
        if out is not None:
            operands.append(out)
            in_specs.append(pl.BlockSpec(memory_space=pl.ANY))
            aliases = {len(operands): 1}
    else:
        own_only = mode == "coarse"
        kept = weights_msg[:1] if own_only else weights_msg
        operands += list(kept)
        in_specs += [whole(array, layer) for array in kept]
        out_specs = [tile] if own_only else [state_tile, tile, tile]
        out_shape = [message_shape] if own_only else [state_shape, message_shape, message_shape]
    return pl.pallas_call(
        functools.partial(node_kernel, mode),
        grid_spec=pltpu.PrefetchScalarGridSpec(
            num_scalar_prefetch=1, grid=(steps,), in_specs=in_specs, out_specs=out_specs
        ),
        out_shape=out_shape,
        input_output_aliases=aliases,
        compiler_params=params(),
        name="node_" + mode,
    )(scal, *operands)


def assemble_kernel(scal, *refs):
    pieces = refs[:CHUNKS]
    out_ref = refs[-1]
    for pos, ref in enumerate(pieces):

        @pl.when(pl.program_id(0) == pos)
        def _():
            out_ref[...] = ref[...]


def assemble_call(scal, pieces, out):
    rows, width = pieces[0].shape
    return pl.pallas_call(
        assemble_kernel,
        grid_spec=pltpu.PrefetchScalarGridSpec(
            num_scalar_prefetch=1,
            grid=(CHUNKS,),
            in_specs=[pl.BlockSpec((rows, width), lambda i, scal: (0, 0)) for _ in pieces]
            + [pl.BlockSpec(memory_space=pl.ANY)],
            out_specs=pl.BlockSpec((rows, width), lambda i, scal: ((1 - scal[0]) * CHUNKS + i, 0)),
        ),
        out_shape=jax.ShapeDtypeStruct(out.shape, out.dtype),
        input_output_aliases={len(pieces) + 1: 0},
        compiler_params=params(),
        name="assemble",
    )(scal, *pieces, out)


def swap_feat(array):
    return lax.ppermute(array, "feat", [(0, 1), (1, 0)])


def strides(count):
    assert count & (count - 1) == 0
    stride = count // 2
    while stride:
        yield stride
        stride //= 2


def fetch_patches(held, stride):
    count = lax.axis_size("patch")
    pairs = [(pos, (pos - stride) % count) for pos in range(count)]
    return jnp.concatenate([held, lax.ppermute(held, "patch", pairs)], axis=0)


def held_places(count):
    offsets = [0]
    for stride in strides(count):
        offsets += [offset + stride for offset in offsets]
    return [offsets.index(pos) for pos in range(count)]


def shards(
    node_state, fine_tile, coarse_tile, fine_index, coarse_index, node_degree, w_msg, w_in, w_out
):
    barrier = lax.optimization_barrier
    patches = lax.axis_size("patch")
    patch_pos = lax.axis_index("patch")
    feat = lax.axis_index("feat")
    blocks, kinds, block, _ = fine_tile.shape
    half = blocks // 2
    half_rows = half * block
    assert half == HALO_BLK and half % (CHUNKS * BLOCK_STEP) == 0
    columns = w_msg.shape[2]
    degree = node_degree.reshape(blocks // BLOCK_STEP, BLOCK_STEP, block)

    forward = [(pos, pos + 1) for pos in range(patches - 1)]
    backward = [(target, source) for source, target in forward]
    sides = ((0, backward), (1, forward))
    own_patch = [(2 * src + side, 2 * dst + side) for side, pairs in sides for src, dst in pairs]
    other_patch = [(2 * src + side, 2 * dst + 1 - side) for side, pairs in sides for src, dst in pairs]
    first_stride, *more_strides = strides(patches)

    held = fetch_patches(node_state[:CN_DEV], first_stride)
    low = message_call(node_state, w_msg[0], 0, half_rows, MESSAGE_TILE)
    low, held = barrier((low, held))
    high_halo = lax.ppermute(low, "patch", backward)
    high = message_call(node_state, w_msg[0], half_rows, half_rows, MESSAGE_TILE)
    low_halo = lax.ppermute(high, "patch", forward)
    for stride in more_strides:
        held = fetch_patches(held, stride)
    coarse_state = held

    links = (fine_index - (patch_pos * blocks - HALO_BLK)).reshape(-1)
    away = ((coarse_index - patch_pos) % patches).reshape(-1)
    coarse_links = sum(
        jnp.where(away == pos, place * CN_DEV, 0) for pos, place in enumerate(held_places(patches))
    )

    def scalars(*places):
        head = jnp.stack([jnp.asarray(value, jnp.int32) for value in (feat, *places)])
        return jnp.concatenate([head, links, coarse_links])

    w_in, w_out, w_msg_late, _ = barrier((w_in, w_out, w_msg[1:], high))
    weights_in = (w_in, swap_feat(w_in))
    weights_out = (w_out, swap_feat(w_out))
    weights_msg = (w_msg_late, swap_feat(w_msg_late))
    coarse = message_call(coarse_state, w_msg[0], 0, coarse_state.shape[0], coarse_state.shape[0])

    pieces = [low_halo, low, high, high_halo]
    scal = scalars(0, HALO_BLK, HALO_BLK + half, HALO_BLK + blocks)
    chunk_blocks = half // CHUNKS
    late_places = []
    for chunk in range(CHUNKS):
        at = chunk * chunk_blocks
        own = HALO_BLK + feat * half + at
        other = HALO_BLK + (1 - feat) * half + at
        near = jnp.where(feat == 0, HALO_BLK + blocks, 0) + at
        far = jnp.where(feat == 0, 0, HALO_BLK + blocks) + at
        late_places += [own, other, near, far]
    late_scal = scalars(*late_places)

    def aggregate(scal, pieces, coarse, chunk):
        shaped = [piece.reshape(-1, block, columns) for piece in pieces]
        return aggregate_call(scal, shaped, coarse, fine_tile, coarse_tile, degree, chunk)

    send, keep = aggregate(scal, pieces, coarse, 0)
    held = fetch_patches(jnp.where(feat == 0, keep[:CN_DEV], send[:CN_DEV]), first_stride)
    recv = swap_feat(send)
    send_1, keep_1 = aggregate(scal, pieces, coarse, 1)
    recv, keep, held, send_1 = barrier((recv, keep, held, send_1))
    recv_1 = swap_feat(send_1)
    inputs = [(keep, recv), (keep_1, recv_1)]
    states = []
    pieces = []
    for chunk in range(CHUNKS):
        new_state, own, other = node_call(
            "mid", scal, node_state, CHUNKS, chunk, *inputs[chunk], weights_in, weights_out, weights_msg, 0
        )
        if chunk == 0:
            held = fetch_patches(held, more_strides[0])
            own, other, held = barrier((own, other, held))
        near = lax.ppermute(own, ("patch", "feat"), own_patch)
        far = lax.ppermute(other, ("patch", "feat"), other_patch)
        pieces += [own, swap_feat(other), near, far]
        states.append(new_state)
    for stride in more_strides[1:]:
        held = fetch_patches(held, stride)
    (coarse,) = node_call(
        "coarse", scal, coarse_state, 0, 0, held, swap_feat(held), weights_in, weights_out, weights_msg, 0
    )

    send, keep = aggregate(late_scal, pieces, coarse, 0)
    recv = swap_feat(send)
    send_1, keep_1 = aggregate(late_scal, pieces, coarse, 1)
    recv, keep, send_1 = barrier((recv, keep, send_1))
    recv_1 = swap_feat(send_1)
    inputs = [(keep, recv), (keep_1, recv_1)]
    out = None
    swapped = []
    for chunk in range(CHUNKS):
        new_state, out = node_call(
            "last", late_scal, states[chunk], 0, chunk, *inputs[chunk], weights_in, weights_out, None, 1,
            out, node_state.shape[0],
        )
        swapped.append(swap_feat(new_state))
    return assemble_call(late_scal, swapped, out)


def solution(mesh):
    return jax.shard_map(
        shards,
        mesh=mesh,
        in_specs=(
            P(("member", "patch"), None),
            P("patch", None, None, None),
            P("patch", None, None),
            P("patch", None),
            P("patch", None),
            P("patch"),
            P(None, None, "feat"),
            P(None, None, "feat"),
            P(None, "feat", None),
        ),
        out_specs=P(("member", "patch"), None),
        check_vma=False,
    )
```

```python
import functools

import jax
import jax.numpy as jnp
from jax import lax
from jax.experimental import pallas as pl
from jax.experimental.pallas import tpu as pltpu
from jax.sharding import PartitionSpec as P

CN_DEV = 40
LAYERS = 2
HALO_BLK = 20
CHUNKS = 2
MESSAGE_TILE = 1280
F32 = jnp.float32
BF16 = jnp.bfloat16
IN_VMEM = pl.BlockSpec(memory_space=pltpu.VMEM)
IN_HBM = pl.BlockSpec(memory_space=pltpu.HBM)


def silu(v):
    return 0.5 * v * (1.0 + jnp.tanh(0.5 * v))


def dot(a, b):
    return jnp.dot(a, b, preferred_element_type=F32)


def normalize(parts):
    width = sum(part.shape[-1] for part in parts)
    mean = sum(jnp.sum(part, axis=-1, keepdims=True) for part in parts) / width
    center = [part - mean for part in parts]
    spread = sum(jnp.sum(part * part, axis=-1, keepdims=True) for part in center) / width
    scale = lax.rsqrt(spread + 1e-05)
    return [(part * scale).astype(BF16) for part in center]


def params(mib):
    return pltpu.CompilerParams(vmem_limit_bytes=mib << 20)


def shaped(array):
    return jax.ShapeDtypeStruct(array.shape, array.dtype)


def run_copies(pairs, sems):
    copies = [pltpu.make_async_copy(src, dst, sems.at[pos]) for pos, (src, dst) in enumerate(pairs)]
    for copy in copies:
        copy.start()
    return copies


def wait_all(copies):
    for copy in copies:
        copy.wait()


def message_kernel(state_ref, weight_ref, out_ref):
    (normed,) = normalize([state_ref[...].astype(F32)])
    message = silu(dot(normed, weight_ref[0])).astype(BF16)
    out_ref[...] = message.astype(out_ref.dtype)


def message_call(state, weight, start, rows, tile):
    first = start // tile
    return pl.pallas_call(
        message_kernel,
        grid=(rows // tile,),
        in_specs=[
            pl.BlockSpec((tile, state.shape[1]), lambda i: (first + i, 0)),
            pl.BlockSpec((1,) + weight.shape[1:], lambda i: (0, 0, 0)),
        ],
        out_specs=pl.BlockSpec((tile, weight.shape[2]), lambda i: (i, 0)),
        out_shape=jax.ShapeDtypeStruct((rows, weight.shape[2]), BF16),
        compiler_params=params(56),
        name="message",
    )(state, weight)


def coarse_message_call(state, weight):
    return pl.pallas_call(
        message_kernel,
        in_specs=[IN_VMEM, IN_VMEM],
        out_specs=IN_VMEM,
        out_shape=pltpu.VMEM((state.shape[0], weight.shape[2]), F32),
        compiler_params=params(12),
        name="coarse_message",
    )(state, weight)


def stage_kernel(count, feat_ref, *refs):
    fine, coarse, state, low, high = refs[:5]
    weights = refs[5 : 5 + count]
    fine_out, coarse_out, state_out, table = refs[5 + count : 9 + count]
    weights_out = refs[9 + count : 9 + 2 * count]
    coarse_buf, sems = refs[9 + 2 * count :]
    block = fine.shape[-1]
    half_rows = low.shape[0]
    pairs = [(coarse, coarse_buf)]
    pairs += [
        (fine.at[:, kind], fine_out.at[:, :, pl.ds(kind * block, block)]) for kind in range(fine.shape[1])
    ]
    start = pl.multiple_of(feat_ref[0] * half_rows, 16)
    pairs.append((state.at[pl.ds(start, half_rows)], state_out))
    pairs.append((low, table.at[pl.ds(HALO_BLK * block, half_rows)]))
    pairs.append((high, table.at[pl.ds(HALO_BLK * block + half_rows, half_rows)]))
    pairs += list(zip(weights, weights_out))
    copies = run_copies(pairs, sems)
    copies[0].wait()

    def turn(pos, carry):
        coarse_out[pos] = jnp.transpose(coarse_buf[pos])
        return carry

    lax.fori_loop(0, coarse.shape[0], turn, 0)
    wait_all(copies[1:])


def stage_call(feat, fine, coarse, state, low, high, weights):
    blocks, kinds, block, _ = fine.shape
    rows, columns = low.shape
    out_shape = [
        pltpu.VMEM((blocks, block, kinds * block), BF16),
        pltpu.VMEM((blocks, block, coarse.shape[1]), BF16),
        pltpu.VMEM((rows, state.shape[1]), BF16),
        pltpu.VMEM((2 * rows + 2 * HALO_BLK * block, columns), BF16),
    ] + [pltpu.VMEM(weight.shape, BF16) for weight in weights]
    copies = 1 + kinds + 3 + len(weights)
    return pl.pallas_call(
        functools.partial(stage_kernel, len(weights)),
        grid_spec=pltpu.PrefetchScalarGridSpec(
            num_scalar_prefetch=1,
            in_specs=[IN_HBM] * (5 + len(weights)),
            out_specs=[IN_VMEM] * len(out_shape),
            scratch_shapes=[pltpu.VMEM(coarse.shape, BF16), pltpu.SemaphoreType.DMA((copies,))],
        ),
        out_shape=out_shape,
        compiler_params=params(12),
        name="stage",
    )(feat, fine, coarse, state, low, high, *weights)


def local_kernel(places, feat_ref, *refs):
    pieces = refs[: len(places)]
    table, sems = refs[-2:]
    pairs = []
    for place, piece in zip(places, pieces):
        start = pl.multiple_of(place(feat_ref[0]), 16)
        pairs.append((piece, table.at[pl.ds(start, piece.shape[0])]))
    wait_all(run_copies(pairs, sems))


def local_call(feat, places, pieces, table):
    return pl.pallas_call(
        functools.partial(local_kernel, places),
        grid_spec=pltpu.PrefetchScalarGridSpec(
            num_scalar_prefetch=1,
            in_specs=[pl.BlockSpec(memory_space=pl.ANY)] * len(pieces) + [IN_VMEM],
            out_specs=IN_VMEM,
            scratch_shapes=[pltpu.SemaphoreType.DMA((len(pieces),))],
        ),
        out_shape=pltpu.VMEM(table.shape, BF16),
        input_output_aliases={len(pieces) + 1: 0},
        compiler_params=params(4),
        name="local_messages",
    )(feat, *pieces, table)


def aggregate_kernel(places, chunk, feat_ref, links, *refs):
    fine, coarse_tile, coarse, degree = refs[:4]
    pieces = refs[4 : 4 + len(places)]
    if places:
        send, keep, first_rows, table, sems = refs[5 + len(places) :]
        pairs = []
        for place, piece in zip(places, pieces):
            start = pl.multiple_of(place(feat_ref[0]), 16)
            pairs.append((piece, table.at[pl.ds(start, piece.shape[0])]))
        copies = run_copies(pairs, sems)
    else:
        table, send, keep = refs[4:]
        copies = []
    blocks, block, fine_width = fine.shape
    kinds = fine_width // block
    count = send.shape[0] // block
    feat = feat_ref[0]
    wait_all(copies)
    for out_ref, which in ((send, 1 - feat), (keep, feat)):
        scale = 1.0 / jnp.transpose(degree[which * CHUNKS + chunk].astype(F32))
        first = which * (blocks // 2) + chunk * count
        for pos in range(count):
            row = (first + pos) * kinds
            chosen = jnp.concatenate(
                [table[pl.ds(pl.multiple_of(links[row + kind], block), block), :] for kind in range(kinds)], axis=0
            )
            base = blocks * kinds + row
            stacked = jnp.concatenate(
                [
                    coarse[pl.ds(pl.multiple_of(links[base + kind], 8), CN_DEV), :]
                    for kind in range(kinds)
                ],
                axis=0,
            ).astype(BF16)
            summed = dot(fine[first + pos], chosen) + dot(coarse_tile[first + pos], stacked)
            result = (summed * scale[:, pos : pos + 1]).astype(BF16)
            out_ref[pos * block : (pos + 1) * block, :] = result
    if places:

        @pl.when(feat == 0)
        def _():
            first_rows[...] = keep[:CN_DEV, :]

        @pl.when(feat != 0)
        def _():
            first_rows[...] = send[:CN_DEV, :]


def aggregate_call(feat, links, staged, coarse, degree, table, chunk, places=(), pieces=()):
    fine, coarse_tile = staged
    blocks, block, _ = fine.shape
    columns = table.shape[1]
    rows = blocks // (2 * CHUNKS) * block
    out_shape = [pltpu.VMEM((rows, columns), BF16)] * 2
    aliases = {}
    scratch = []
    if pieces:
        out_shape += [pltpu.VMEM((CN_DEV, columns), BF16), pltpu.VMEM(table.shape, BF16)]
        aliases = {6 + len(pieces): 3}
        scratch = [pltpu.SemaphoreType.DMA((len(pieces),))]
    return pl.pallas_call(
        functools.partial(aggregate_kernel, places, chunk),
        grid_spec=pltpu.PrefetchScalarGridSpec(
            num_scalar_prefetch=2,
            in_specs=[IN_VMEM] * 4 + [IN_HBM] * len(pieces) + [IN_VMEM],
            out_specs=[IN_VMEM] * len(out_shape),
            scratch_shapes=scratch,
        ),
        out_shape=out_shape,
        input_output_aliases=aliases,
        compiler_params=params(12),
        name="aggregate",
    )(feat, links, fine, coarse_tile, coarse, degree, *pieces, table)


def node_kernel(mode, layer, start, chunk, feat_ref, *refs):
    state_ref, keep, recv, in_own, in_other, out_own, out_other = refs[:7]
    refs = refs[7:]
    feat = feat_ref[0]
    rows, columns = keep.shape
    width = state_ref.shape[1]
    state = state_ref[start : start + rows, :].astype(F32)
    joined = normalize([state, keep[...].astype(F32), recv[...].astype(F32)])
    keep_at = pl.multiple_of(width + feat * columns, columns)
    recv_at = pl.multiple_of(width + (1 - feat) * columns, columns)
    update = None
    for in_ref, out_ref in ((in_own, out_own), (in_other, out_other)):
        hidden = (
            dot(joined[0], in_ref[layer, :width, :])
            + dot(joined[1], in_ref[layer, pl.ds(keep_at, columns), :])
            + dot(joined[2], in_ref[layer, pl.ds(recv_at, columns), :])
        )
        part = dot(silu(hidden).astype(BF16), out_ref[layer])
        update = part if update is None else update + part
    new_state = (state + update).astype(BF16)
    if mode == "last":
        state_out, out, sem = refs[-3:]
        state_out[...] = new_state
        half_rows = rows * CHUNKS
        at = pl.multiple_of(feat * half_rows + chunk * rows, 16)
        copy = pltpu.make_async_copy(state_out, out.at[pl.ds(at, rows)], sem)
        copy.start()
        copy.wait()
        return
    (normed,) = normalize([new_state.astype(F32)])
    if mode == "coarse":
        msg_own, own_out = refs
        own_out[...] = silu(dot(normed, msg_own[layer + 1])).astype(BF16).astype(F32)
        return
    msg_own, msg_other, state_out, own_out, other_out = refs
    own_out[...] = silu(dot(normed, msg_own[layer + 1])).astype(BF16)
    other_out[...] = silu(dot(normed, msg_other[layer + 1])).astype(BF16)
    state_out[...] = new_state


def node_call(mode, layer, feat, state, start, chunk, keep, recv, weights, out=None, total=0):
    rows, columns = keep.shape
    width = state.shape[1]
    operands = [state, keep, recv, *weights[:4]]
    aliases = {}
    scratch = []
    if mode == "last":
        out_shape = [pltpu.VMEM((rows, width), BF16), jax.ShapeDtypeStruct((total, width), BF16)]
        out_specs = [IN_VMEM, pl.BlockSpec(memory_space=pl.ANY)]
        in_specs = [IN_VMEM] * len(operands)
        scratch = [pltpu.SemaphoreType.DMA(())]
        if out is not None:
            aliases = {len(operands) + 1: 1}
            operands.append(out)
            in_specs.append(pl.BlockSpec(memory_space=pl.ANY))
    else:
        if mode == "coarse":
            operands.append(weights[4])
            out_shape = [pltpu.VMEM((rows, columns), F32)]
        else:
            operands += weights[4:]
            out_shape = [pltpu.VMEM((rows, shape), BF16) for shape in (width, columns, columns)]
        in_specs = [IN_VMEM] * len(operands)
        out_specs = [IN_VMEM] * len(out_shape)
    return pl.pallas_call(
        functools.partial(node_kernel, mode, layer, start, chunk),
        grid_spec=pltpu.PrefetchScalarGridSpec(
            num_scalar_prefetch=1, in_specs=in_specs, out_specs=out_specs, scratch_shapes=scratch
        ),
        out_shape=out_shape,
        input_output_aliases=aliases,
        compiler_params=params(28),
        name="node_" + mode,
    )(feat, *operands)


def assemble_kernel(feat_ref, *refs):
    pieces = refs[:CHUNKS]
    out, sems = refs[-2:]
    pairs = []
    for chunk, piece in enumerate(pieces):
        rows = piece.shape[0]
        at = pl.multiple_of((1 - feat_ref[0]) * rows * CHUNKS + chunk * rows, 16)
        pairs.append((piece, out.at[pl.ds(at, rows)]))
    wait_all(run_copies(pairs, sems))


def assemble_call(feat, pieces, out):
    return pl.pallas_call(
        assemble_kernel,
        grid_spec=pltpu.PrefetchScalarGridSpec(
            num_scalar_prefetch=1,
            in_specs=[IN_VMEM] * len(pieces) + [pl.BlockSpec(memory_space=pl.ANY)],
            out_specs=pl.BlockSpec(memory_space=pl.ANY),
            scratch_shapes=[pltpu.SemaphoreType.DMA((len(pieces),))],
        ),
        out_shape=shaped(out),
        input_output_aliases={len(pieces) + 1: 0},
        compiler_params=params(4),
        name="assemble",
    )(feat, *pieces, out)


def swap_feat(array):
    return lax.ppermute(array, "feat", [(0, 1), (1, 0)])


def fetch(held, stride):
    count = lax.axis_size("patch")
    return lax.ppermute(held, "patch", [(pos, (pos - stride) % count) for pos in range(count)])


def even_offsets(count):
    assert count & (count - 1) == 0
    offsets = [0]
    stride = count // 2
    while stride > 1:
        offsets += [offset + stride for offset in offsets]
        stride //= 2
    return offsets


def shards(
    node_state, fine_tile, coarse_tile, fine_index, coarse_index, node_degree, w_msg, w_in, w_out
):
    barrier = lax.optimization_barrier
    patches = lax.axis_size("patch")
    patch_pos = lax.axis_index("patch")
    feat_pos = lax.axis_index("feat")
    feat = feat_pos.astype(jnp.int32).reshape(1)
    blocks, kinds, block, _ = fine_tile.shape
    half = blocks // 2
    half_rows = half * block
    halo_rows = HALO_BLK * block
    assert half == HALO_BLK and half % CHUNKS == 0
    chunk_rows = half_rows // CHUNKS

    forward = [(pos, pos + 1) for pos in range(patches - 1)]
    backward = [(target, source) for source, target in forward]
    sides = ((0, backward), (1, forward))
    own_patch = [(2 * src + side, 2 * dst + side) for side, pairs in sides for src, dst in pairs]
    other_patch = [(2 * src + side, 2 * dst + 1 - side) for side, pairs in sides for src, dst in pairs]
    evens = even_offsets(patches)

    held = node_state[:CN_DEV]
    strides = [patches >> step for step in range(1, patches.bit_length())]
    held = jnp.concatenate([held, fetch(held, strides[0])], axis=0)
    low = message_call(node_state, w_msg, 0, half_rows, MESSAGE_TILE)
    low, held = barrier((low, held))
    high_halo = lax.ppermute(low, "patch", backward)
    high = message_call(node_state, w_msg, half_rows, half_rows, MESSAGE_TILE)
    low_halo = lax.ppermute(high, "patch", forward)
    for stride in strides[1:]:
        held = jnp.concatenate([held, fetch(held, stride)], axis=0)
    coarse_state = held

    offsets = evens + [offset + 1 for offset in evens]
    links = (fine_index - (patch_pos * blocks - HALO_BLK)).reshape(-1) * block
    away = ((coarse_index - patch_pos) % patches).reshape(-1)
    coarse_links = sum(jnp.where(away == offset, pos * CN_DEV, 0) for pos, offset in enumerate(offsets))
    links = jnp.concatenate([links, coarse_links])
    degree = node_degree.reshape(2 * CHUNKS, half // CHUNKS, block)

    w_in, w_out, w_late, _ = barrier((w_in, w_out, w_msg, high))
    weights = [w_in, swap_feat(w_in), w_out, swap_feat(w_out), w_late, swap_feat(w_late)]
    fine, ctile, state, table, *weights = stage_call(
        feat, fine_tile, jnp.swapaxes(coarse_tile, 1, 2), node_state, low, high, weights
    )
    staged = (fine, ctile)
    coarse = coarse_message_call(coarse_state, w_late)

    places = (lambda feat: 0, lambda feat: halo_rows + 2 * half_rows)
    send, keep, first_rows, table = aggregate_call(
        feat, links, staged, coarse, degree, table, 0, places, (low_halo, high_halo)
    )
    recv = swap_feat(send)
    others = [fetch(first_rows, offset) for offset in evens[1:]]
    send_1, keep_1 = aggregate_call(feat, links, staged, coarse, degree, table, 1)
    recv, keep, send_1, others = barrier((recv, keep, send_1, others))
    held = jnp.concatenate([first_rows, *others], axis=0)
    held = jnp.concatenate([held, fetch(held, 1)], axis=0)
    inputs = [(keep, recv), (keep_1, swap_feat(send_1))]
    states = []
    local = []
    halo = []
    for chunk in range(CHUNKS):
        new_state, own, other = node_call(
            "mid", 0, feat, state, chunk * chunk_rows, chunk, *inputs[chunk], weights
        )
        if chunk == 0:
            own, other, held = barrier((own, other, held))
        halo += [lax.ppermute(own, ("patch", "feat"), own_patch), lax.ppermute(other, ("patch", "feat"), other_patch)]
        local += [own, swap_feat(other)]
        states.append(new_state)
    (coarse,) = node_call("coarse", 0, feat, coarse_state, 0, 0, held, swap_feat(held), weights)

    local_places = []
    halo_places = []
    for chunk in range(CHUNKS):
        at = chunk * chunk_rows
        local_places += [
            lambda feat, at=at: halo_rows + feat * half_rows + at,
            lambda feat, at=at: halo_rows + (1 - feat) * half_rows + at,
        ]
        halo_places += [
            lambda feat, at=at: (1 - feat) * (halo_rows + 2 * half_rows) + at,
            lambda feat, at=at: feat * (halo_rows + 2 * half_rows) + at,
        ]
    table = local_call(feat, local_places, local, table)
    send, keep, _, table = aggregate_call(
        feat, links, staged, coarse, degree, table, 0, halo_places, halo
    )
    recv = swap_feat(send)
    send_1, keep_1 = aggregate_call(feat, links, staged, coarse, degree, table, 1)
    recv, keep, send_1 = barrier((recv, keep, send_1))
    inputs = [(keep, recv), (keep_1, swap_feat(send_1))]
    out = None
    swapped = []
    for chunk in range(CHUNKS):
        new_state, out = node_call(
            "last", 1, feat, states[chunk], 0, chunk, *inputs[chunk], weights, out, node_state.shape[0]
        )
        swapped.append(swap_feat(new_state))
    return assemble_call(feat, swapped, out)


def solution(mesh):
    return jax.shard_map(
        shards,
        mesh=mesh,
        in_specs=(
            P(("member", "patch"), None),
            P("patch", None, None, None),
            P("patch", None, None),
            P("patch", None),
            P("patch", None),
            P("patch"),
            P(None, None, "feat"),
            P(None, None, "feat"),
            P(None, "feat", None),
        ),
        out_specs=P(("member", "patch"), None),
        check_vma=False,
    )
```

```python
import functools

import jax
import jax.numpy as jnp
from jax import lax
from jax.experimental import pallas as pl
from jax.experimental.pallas import tpu as pltpu
from jax.sharding import PartitionSpec as P

CN_DEV = 40
LAYERS = 2
HALO_BLK = 20
CHUNKS = 2
MESSAGE_TILE = 1280
F32 = jnp.float32
BF16 = jnp.bfloat16
SMALL = pl.CostEstimate(flops=1 << 20, transcendentals=0, bytes_accessed=1 << 10)
IN_VMEM = pl.BlockSpec(memory_space=pltpu.VMEM)
IN_HBM = pl.BlockSpec(memory_space=pltpu.HBM)


def silu(v):
    return 0.5 * v * (1.0 + jnp.tanh(0.5 * v))


def dot(a, b):
    return jnp.dot(a, b, preferred_element_type=F32)


def normalize(parts):
    width = sum(part.shape[-1] for part in parts)
    mean = sum(jnp.sum(part, axis=-1, keepdims=True) for part in parts) / width
    center = [part - mean for part in parts]
    spread = sum(jnp.sum(part * part, axis=-1, keepdims=True) for part in center) / width
    scale = lax.rsqrt(spread + 1e-05)
    return [(part * scale).astype(BF16) for part in center]


def params(mib):
    return pltpu.CompilerParams(vmem_limit_bytes=mib << 20)


def shaped(array):
    return jax.ShapeDtypeStruct(array.shape, array.dtype)


def run_copies(pairs, sems):
    copies = [pltpu.make_async_copy(src, dst, sems.at[pos]) for pos, (src, dst) in enumerate(pairs)]
    for copy in copies:
        copy.start()
    return copies


def wait_all(copies):
    for copy in copies:
        copy.wait()


def message_kernel(state_ref, weight_ref, out_ref):
    (normed,) = normalize([state_ref[...].astype(F32)])
    message = silu(dot(normed, weight_ref[0])).astype(BF16)
    out_ref[...] = message.astype(out_ref.dtype)


def message_call(state, weight, start, rows, tile):
    first = start // tile
    return pl.pallas_call(
        message_kernel,
        grid=(rows // tile,),
        in_specs=[
            pl.BlockSpec((tile, state.shape[1]), lambda i: (first + i, 0)),
            pl.BlockSpec((1,) + weight.shape[1:], lambda i: (0, 0, 0)),
        ],
        out_specs=pl.BlockSpec((tile, weight.shape[2]), lambda i: (i, 0)),
        out_shape=jax.ShapeDtypeStruct((rows, weight.shape[2]), BF16),
        compiler_params=params(56),
        cost_estimate=SMALL,
        name="message",
    )(state, weight)


def coarse_message_call(state, weight):
    return pl.pallas_call(
        message_kernel,
        in_specs=[IN_VMEM, IN_VMEM],
        out_specs=IN_VMEM,
        out_shape=pltpu.VMEM((state.shape[0], weight.shape[2]), F32),
        compiler_params=params(12),
        cost_estimate=SMALL,
        name="coarse_message",
    )(state, weight)


def stage_kernel(count, feat_ref, *refs):
    fine, coarse, state, low, high = refs[:5]
    weights = refs[5 : 5 + count]
    fine_out, coarse_out, state_out, table = refs[5 + count : 9 + count]
    weights_out = refs[9 + count : 9 + 2 * count]
    coarse_buf, sems = refs[9 + 2 * count :]
    block = fine.shape[-1]
    half_rows = low.shape[0]
    pairs = [(coarse, coarse_buf)]
    pairs += [
        (fine.at[:, kind], fine_out.at[:, :, pl.ds(kind * block, block)]) for kind in range(fine.shape[1])
    ]
    start = pl.multiple_of(feat_ref[0] * half_rows, 16)
    pairs.append((state.at[pl.ds(start, half_rows)], state_out))
    pairs.append((low, table.at[pl.ds(HALO_BLK * block, half_rows)]))
    pairs.append((high, table.at[pl.ds(HALO_BLK * block + half_rows, half_rows)]))
    pairs += list(zip(weights, weights_out))
    copies = run_copies(pairs, sems)
    copies[0].wait()

    def turn(pos, carry):
        coarse_out[pos] = jnp.transpose(coarse_buf[pos])
        return carry

    lax.fori_loop(0, coarse.shape[0], turn, 0)
    wait_all(copies[1:])


def stage_call(feat, fine, coarse, state, low, high, weights):
    blocks, kinds, block, _ = fine.shape
    rows, columns = low.shape
    out_shape = [
        pltpu.VMEM((blocks, block, kinds * block), BF16),
        pltpu.VMEM((blocks, block, coarse.shape[1]), BF16),
        pltpu.VMEM((rows, state.shape[1]), BF16),
        pltpu.VMEM((2 * rows + 2 * HALO_BLK * block, columns), BF16),
    ] + [pltpu.VMEM(weight.shape, BF16) for weight in weights]
    copies = 1 + kinds + 3 + len(weights)
    return pl.pallas_call(
        functools.partial(stage_kernel, len(weights)),
        grid_spec=pltpu.PrefetchScalarGridSpec(
            num_scalar_prefetch=1,
            in_specs=[IN_HBM] * (5 + len(weights)),
            out_specs=[IN_VMEM] * len(out_shape),
            scratch_shapes=[pltpu.VMEM(coarse.shape, BF16), pltpu.SemaphoreType.DMA((copies,))],
        ),
        out_shape=out_shape,
        compiler_params=params(36),
        cost_estimate=SMALL,
        name="stage",
    )(feat, fine, coarse, state, low, high, *weights)


def weights_kernel(*refs):
    sems = refs[-1]
    count = len(refs) // 2
    wait_all(run_copies(list(zip(refs[:count], refs[count:-1])), sems))


def weights_call(weights):
    return pl.pallas_call(
        weights_kernel,
        in_specs=[IN_HBM] * len(weights),
        out_specs=[IN_VMEM] * len(weights),
        scratch_shapes=[pltpu.SemaphoreType.DMA((len(weights),))],
        out_shape=[pltpu.VMEM(weight.shape, BF16) for weight in weights],
        compiler_params=params(4),
        cost_estimate=SMALL,
        name="weights",
    )(*weights)


def local_kernel(places, feat_ref, *refs):
    pieces = refs[: len(places)]
    table, sems = refs[-2:]
    pairs = []
    for place, piece in zip(places, pieces):
        start = pl.multiple_of(place(feat_ref[0]), 16)
        pairs.append((piece, table.at[pl.ds(start, piece.shape[0])]))
    wait_all(run_copies(pairs, sems))


def local_call(feat, places, pieces, table):
    return pl.pallas_call(
        functools.partial(local_kernel, places),
        grid_spec=pltpu.PrefetchScalarGridSpec(
            num_scalar_prefetch=1,
            in_specs=[pl.BlockSpec(memory_space=pl.ANY)] * len(pieces) + [IN_VMEM],
            out_specs=IN_VMEM,
            scratch_shapes=[pltpu.SemaphoreType.DMA((len(pieces),))],
        ),
        out_shape=pltpu.VMEM(table.shape, BF16),
        input_output_aliases={len(pieces) + 1: 0},
        compiler_params=params(4),
        cost_estimate=SMALL,
        name="local_messages",
    )(feat, *pieces, table)


def aggregate_kernel(places, chunk, feat_ref, links, *refs):
    fine, coarse_tile, coarse, degree = refs[:4]
    pieces = refs[4 : 4 + len(places)]
    if places:
        send, keep, first_rows, table, sems = refs[5 + len(places) :]
        pairs = []
        for place, piece in zip(places, pieces):
            start = pl.multiple_of(place(feat_ref[0]), 16)
            pairs.append((piece, table.at[pl.ds(start, piece.shape[0])]))
        copies = run_copies(pairs, sems)
    else:
        table, send, keep = refs[4:]
        copies = []
    blocks, block, fine_width = fine.shape
    kinds = fine_width // block
    count = send.shape[0] // block
    feat = feat_ref[0]
    wait_all(copies)
    for out_ref, which in ((send, 1 - feat), (keep, feat)):
        scale = 1.0 / jnp.transpose(degree[which * CHUNKS + chunk].astype(F32))
        first = which * (blocks // 2) + chunk * count
        for pos in range(count):
            row = (first + pos) * kinds
            chosen = jnp.concatenate(
                [table[pl.ds(pl.multiple_of(links[row + kind], block), block), :] for kind in range(kinds)], axis=0
            )
            base = blocks * kinds + row
            stacked = jnp.concatenate(
                [
                    coarse[pl.ds(pl.multiple_of(links[base + kind], 8), CN_DEV), :]
                    for kind in range(kinds)
                ],
                axis=0,
            ).astype(BF16)
            summed = dot(fine[first + pos], chosen) + dot(coarse_tile[first + pos], stacked)
            result = (summed * scale[:, pos : pos + 1]).astype(BF16)
            out_ref[pos * block : (pos + 1) * block, :] = result
    if places:

        @pl.when(feat == 0)
        def _():
            first_rows[...] = keep[:CN_DEV, :]

        @pl.when(feat != 0)
        def _():
            first_rows[...] = send[:CN_DEV, :]


def aggregate_call(feat, links, staged, coarse, degree, table, chunk, places=(), pieces=()):
    fine, coarse_tile = staged
    blocks, block, _ = fine.shape
    columns = table.shape[1]
    rows = blocks // (2 * CHUNKS) * block
    out_shape = [pltpu.VMEM((rows, columns), BF16)] * 2
    aliases = {}
    scratch = []
    if pieces:
        out_shape += [pltpu.VMEM((CN_DEV, columns), BF16), pltpu.VMEM(table.shape, BF16)]
        aliases = {6 + len(pieces): 3}
        scratch = [pltpu.SemaphoreType.DMA((len(pieces),))]
    return pl.pallas_call(
        functools.partial(aggregate_kernel, places, chunk),
        grid_spec=pltpu.PrefetchScalarGridSpec(
            num_scalar_prefetch=2,
            in_specs=[IN_VMEM] * 4 + [IN_HBM] * len(pieces) + [IN_VMEM],
            out_specs=[IN_VMEM] * len(out_shape),
            scratch_shapes=scratch,
        ),
        out_shape=out_shape,
        input_output_aliases=aliases,
        compiler_params=params(12),
        cost_estimate=SMALL,
        name="aggregate",
    )(feat, links, fine, coarse_tile, coarse, degree, *pieces, table)


def node_kernel(mode, layer, start, chunk, feat_ref, *refs):
    state_ref, keep, recv, in_own, in_other, out_own, out_other = refs[:7]
    refs = refs[7:]
    feat = feat_ref[0]
    rows, columns = keep.shape
    width = state_ref.shape[1]
    state = state_ref[start : start + rows, :].astype(F32)
    joined = normalize([state, keep[...].astype(F32), recv[...].astype(F32)])
    keep_at = pl.multiple_of(width + feat * columns, columns)
    recv_at = pl.multiple_of(width + (1 - feat) * columns, columns)
    update = None
    for in_ref, out_ref in ((in_own, out_own), (in_other, out_other)):
        hidden = (
            dot(joined[0], in_ref[layer, :width, :])
            + dot(joined[1], in_ref[layer, pl.ds(keep_at, columns), :])
            + dot(joined[2], in_ref[layer, pl.ds(recv_at, columns), :])
        )
        part = dot(silu(hidden).astype(BF16), out_ref[layer])
        update = part if update is None else update + part
    new_state = (state + update).astype(BF16)
    if mode == "last":
        state_out, out, sem = refs[-3:]
        state_out[...] = new_state
        half_rows = rows * CHUNKS
        at = pl.multiple_of(feat * half_rows + chunk * rows, 16)
        copy = pltpu.make_async_copy(state_out, out.at[pl.ds(at, rows)], sem)
        copy.start()
        copy.wait()
        return
    (normed,) = normalize([new_state.astype(F32)])
    if mode == "coarse":
        msg_own, own_out = refs
        own_out[...] = silu(dot(normed, msg_own[layer + 1])).astype(BF16).astype(F32)
        return
    msg_own, msg_other, state_out, own_out, other_out = refs
    own_out[...] = silu(dot(normed, msg_own[layer + 1])).astype(BF16)
    other_out[...] = silu(dot(normed, msg_other[layer + 1])).astype(BF16)
    state_out[...] = new_state


def node_call(mode, layer, feat, state, start, chunk, keep, recv, weights, out=None, total=0):
    rows, columns = keep.shape
    width = state.shape[1]
    operands = [state, keep, recv, *weights[:4]]
    aliases = {}
    scratch = []
    if mode == "last":
        out_shape = [pltpu.VMEM((rows, width), BF16), jax.ShapeDtypeStruct((total, width), BF16)]
        out_specs = [IN_VMEM, pl.BlockSpec(memory_space=pl.ANY)]
        in_specs = [IN_VMEM] * len(operands)
        scratch = [pltpu.SemaphoreType.DMA(())]
        if out is not None:
            aliases = {len(operands) + 1: 1}
            operands.append(out)
            in_specs.append(pl.BlockSpec(memory_space=pl.ANY))
    else:
        if mode == "coarse":
            operands.append(weights[4])
            out_shape = [pltpu.VMEM((rows, columns), F32)]
        else:
            operands += weights[4:]
            out_shape = [pltpu.VMEM((rows, shape), BF16) for shape in (width, columns, columns)]
        in_specs = [IN_VMEM] * len(operands)
        out_specs = [IN_VMEM] * len(out_shape)
    return pl.pallas_call(
        functools.partial(node_kernel, mode, layer, start, chunk),
        grid_spec=pltpu.PrefetchScalarGridSpec(
            num_scalar_prefetch=1, in_specs=in_specs, out_specs=out_specs, scratch_shapes=scratch
        ),
        out_shape=out_shape,
        input_output_aliases=aliases,
        compiler_params=params(28),
        cost_estimate=SMALL,
        name="node_" + mode,
    )(feat, *operands)


def assemble_kernel(feat_ref, *refs):
    pieces = refs[:CHUNKS]
    out, sems = refs[-2:]
    pairs = []
    for chunk, piece in enumerate(pieces):
        rows = piece.shape[0]
        at = pl.multiple_of((1 - feat_ref[0]) * rows * CHUNKS + chunk * rows, 16)
        pairs.append((piece, out.at[pl.ds(at, rows)]))
    wait_all(run_copies(pairs, sems))


def assemble_call(feat, pieces, out):
    return pl.pallas_call(
        assemble_kernel,
        grid_spec=pltpu.PrefetchScalarGridSpec(
            num_scalar_prefetch=1,
            in_specs=[IN_VMEM] * len(pieces) + [pl.BlockSpec(memory_space=pl.ANY)],
            out_specs=pl.BlockSpec(memory_space=pl.ANY),
            scratch_shapes=[pltpu.SemaphoreType.DMA((len(pieces),))],
        ),
        out_shape=shaped(out),
        input_output_aliases={len(pieces) + 1: 0},
        compiler_params=params(4),
        cost_estimate=SMALL,
        name="assemble",
    )(feat, *pieces, out)


def swap_feat(array):
    return lax.ppermute(array, "feat", [(0, 1), (1, 0)])


def fetch(held, stride):
    count = lax.axis_size("patch")
    return lax.ppermute(held, "patch", [(pos, (pos - stride) % count) for pos in range(count)])


def even_offsets(count):
    assert count & (count - 1) == 0
    offsets = [0]
    stride = count // 2
    while stride > 1:
        offsets += [offset + stride for offset in offsets]
        stride //= 2
    return offsets


def shards(
    node_state, fine_tile, coarse_tile, fine_index, coarse_index, node_degree, w_msg, w_in, w_out
):
    barrier = lax.optimization_barrier
    patches = lax.axis_size("patch")
    patch_pos = lax.axis_index("patch")
    feat_pos = lax.axis_index("feat")
    feat = feat_pos.astype(jnp.int32).reshape(1)
    blocks, kinds, block, _ = fine_tile.shape
    half = blocks // 2
    half_rows = half * block
    halo_rows = HALO_BLK * block
    assert half == HALO_BLK and half % CHUNKS == 0
    chunk_rows = half_rows // CHUNKS

    forward = [(pos, pos + 1) for pos in range(patches - 1)]
    backward = [(target, source) for source, target in forward]
    sides = ((0, backward), (1, forward))
    own_patch = [(2 * src + side, 2 * dst + side) for side, pairs in sides for src, dst in pairs]
    other_patch = [(2 * src + side, 2 * dst + 1 - side) for side, pairs in sides for src, dst in pairs]
    evens = even_offsets(patches)

    held = node_state[:CN_DEV]
    held = jnp.concatenate([held, fetch(held, 1)], axis=0)
    low = message_call(node_state, w_msg, 0, half_rows, MESSAGE_TILE)
    low, held = barrier((low, held))
    high_halo = lax.ppermute(low, "patch", backward)
    high = message_call(node_state, w_msg, half_rows, half_rows, MESSAGE_TILE)
    low_halo = lax.ppermute(high, "patch", forward)

    offsets = [even + odd for even in evens for odd in (0, 1)]
    fine_index, coarse_index, node_degree, w_in, w_out, w_late, _ = barrier(
        (fine_index, coarse_index, node_degree, w_in, w_out, w_msg, high)
    )
    links = (fine_index - (patch_pos * blocks - HALO_BLK)).reshape(-1) * block
    away = ((coarse_index - patch_pos) % patches).reshape(-1)
    coarse_links = sum(jnp.where(away == offset, pos * CN_DEV, 0) for pos, offset in enumerate(offsets))
    links = jnp.concatenate([links, coarse_links])
    degree = node_degree.reshape(2 * CHUNKS, half // CHUNKS, block)
    fine, ctile, state, table, in_own, out_own, msg_own = stage_call(
        feat, fine_tile, jnp.swapaxes(coarse_tile, 1, 2), node_state, low, high, (w_in, w_out, w_late)
    )
    staged = (fine, ctile)
    others = weights_call([swap_feat(w_in), swap_feat(w_out), swap_feat(w_late)])
    strides = [patches >> step for step in range(1, patches.bit_length() - 1)]
    for step, stride in enumerate(strides):
        got = fetch(held, stride)
        if step == 0:
            got, links, degree, table = barrier((got, links, degree, table))
        if step == len(strides) - 1:
            got, others = barrier((got, others))
        held = jnp.concatenate([held, got], axis=0)
    coarse_state = held
    weights = [in_own, others[0], out_own, others[1], msg_own, others[2]]
    coarse = coarse_message_call(coarse_state, msg_own)

    places = (lambda feat: 0, lambda feat: halo_rows + 2 * half_rows)
    send, keep, first_rows, table = aggregate_call(
        feat, links, staged, coarse, degree, table, 0, places, (low_halo, high_halo)
    )
    recv = swap_feat(send)
    got = fetch(first_rows, 1)
    send_1, keep_1 = aggregate_call(feat, links, staged, coarse, degree, table, 1)
    recv, keep, send_1, got = barrier((recv, keep, send_1, got))
    held = jnp.concatenate([first_rows, got], axis=0)
    got = fetch(held, strides[0])
    inputs = [(keep, recv), (keep_1, swap_feat(send_1))]
    states = []
    local = []
    halo = []
    for chunk in range(CHUNKS):
        new_state, own, other = node_call(
            "mid", 0, feat, state, chunk * chunk_rows, chunk, *inputs[chunk], weights
        )
        if chunk == 0:
            own, other, got = barrier((own, other, got))
            held = jnp.concatenate([held, got], axis=0)
        sibling = swap_feat(other)
        if chunk + 1 < CHUNKS:
            sibling, state = barrier((sibling, state))
        halo += [lax.ppermute(own, ("patch", "feat"), own_patch), lax.ppermute(other, ("patch", "feat"), other_patch)]
        local += [own, sibling]
        states.append(new_state)

    local_places = []
    halo_places = []
    for chunk in range(CHUNKS):
        at = chunk * chunk_rows
        local_places += [
            lambda feat, at=at: halo_rows + feat * half_rows + at,
            lambda feat, at=at: halo_rows + (1 - feat) * half_rows + at,
        ]
        halo_places += [
            lambda feat, at=at: (1 - feat) * (halo_rows + 2 * half_rows) + at,
            lambda feat, at=at: feat * (halo_rows + 2 * half_rows) + at,
        ]
    early = 2 * (CHUNKS - 1)
    table = local_call(feat, local_places + halo_places[:early], local + halo[:early], table)
    held, table = barrier((held, table))
    for stride in strides[1:]:
        held = jnp.concatenate([held, fetch(held, stride)], axis=0)
    (coarse,) = node_call("coarse", 0, feat, coarse_state, 0, 0, held, swap_feat(held), weights)
    send, keep, _, table = aggregate_call(
        feat, links, staged, coarse, degree, table, 0, halo_places[early:], halo[early:]
    )
    recv = swap_feat(send)
    send_1, keep_1 = aggregate_call(feat, links, staged, coarse, degree, table, 1)
    recv, keep, send_1 = barrier((recv, keep, send_1))
    inputs = [(keep, recv), (keep_1, swap_feat(send_1))]
    out = None
    swapped = []
    for chunk in range(CHUNKS):
        new_state, out = node_call(
            "last", 1, feat, states[chunk], 0, chunk, *inputs[chunk], weights, out, node_state.shape[0]
        )
        swapped.append(swap_feat(new_state))
    return assemble_call(feat, swapped, out)


def solution(mesh):
    return jax.shard_map(
        shards,
        mesh=mesh,
        in_specs=(
            P(("member", "patch"), None),
            P("patch", None, None, None),
            P("patch", None, None),
            P("patch", None),
            P("patch", None),
            P("patch"),
            P(None, None, "feat"),
            P(None, None, "feat"),
            P(None, "feat", None),
        ),
        out_specs=P(("member", "patch"), None),
        check_vma=False,
    )
```

```python
import functools

import jax
import jax.numpy as jnp
from jax import lax
from jax.experimental import pallas as pl
from jax.experimental.pallas import tpu as pltpu
from jax.sharding import PartitionSpec as P

CN_DEV = 40
LAYERS = 2
HALO_BLK = 20
MID_BLOCKS = (10, 10)
LAST_BLOCKS = (10, 10)
LAST_ROWS = ((0, 0, 10), (1, 0, 5), (1, 5, 5))
MESSAGE_ROWS = ((0, 20), (20, 20))
MESSAGE_TILE = 640
NODE_SPLIT = 2
F32 = jnp.float32
BF16 = jnp.bfloat16
SMALL = pl.CostEstimate(flops=1 << 20, transcendentals=0, bytes_accessed=1 << 10)
IN_VMEM = pl.BlockSpec(memory_space=pltpu.VMEM)
IN_HBM = pl.BlockSpec(memory_space=pltpu.HBM)


def silu(v):
    return 0.5 * v * (1.0 + jnp.tanh(0.5 * v))


def dot(a, b):
    return jnp.dot(a, b, preferred_element_type=F32)


def normalize(parts):
    width = sum(part.shape[-1] for part in parts)
    mean = sum(jnp.sum(part, axis=-1, keepdims=True) for part in parts) / width
    center = [part - mean for part in parts]
    spread = sum(jnp.sum(part * part, axis=-1, keepdims=True) for part in center) / width
    scale = lax.rsqrt(spread + 1e-05)
    return [(part * scale).astype(BF16) for part in center]


def params(mib):
    return pltpu.CompilerParams(vmem_limit_bytes=mib << 20)


def shaped(array):
    return jax.ShapeDtypeStruct(array.shape, array.dtype)


def run_copies(pairs, sems):
    copies = [pltpu.make_async_copy(src, dst, sems.at[pos]) for pos, (src, dst) in enumerate(pairs)]
    for copy in copies:
        copy.start()
    return copies


def wait_all(copies):
    for copy in copies:
        copy.wait()


def coarse_message_kernel(state_ref, weight_ref, out_ref):
    (normed,) = normalize([state_ref[...].astype(F32)])
    out_ref[...] = silu(dot(normed, weight_ref[0])).astype(BF16).astype(F32)


def message_kernel(start, tile, state, weight, out_ref, state_buf, weight_buf, sems):
    rows = out_ref.shape[0]
    tiles = [(at, tile) for at in range(0, rows, tile)]
    pairs = [(state.at[pl.ds(start + at, size)], state_buf.at[pl.ds(at, size)]) for at, size in tiles]
    copies = run_copies(pairs[:1] + [(weight.at[0], weight_buf)] + pairs[1:], sems)
    weight_copy = copies.pop(1)
    normed = []
    for pos in range(len(tiles) + 1):
        if pos < len(tiles):
            at, size = tiles[pos]
            copies[pos].wait()
            normed += normalize([state_buf[at : at + size, :].astype(F32)])
        if pos == 0:
            weight_copy.wait()
            continue
        at, size = tiles[pos - 1]
        out_ref[at : at + size, :] = silu(dot(normed[pos - 1], weight_buf[...])).astype(BF16)


def message_call(state, weight, start, rows, tile):
    width, columns = weight.shape[1:]
    return pl.pallas_call(
        functools.partial(message_kernel, start, tile),
        in_specs=[IN_HBM, IN_HBM],
        out_specs=IN_VMEM,
        out_shape=pltpu.VMEM((rows, columns), BF16),
        scratch_shapes=[
            pltpu.VMEM((rows, width), BF16),
            pltpu.VMEM((width, columns), BF16),
            pltpu.SemaphoreType.DMA((1 + rows // tile,)),
        ],
        compiler_params=params(58),
        cost_estimate=SMALL,
        name="message",
    )(state, weight)


def coarse_message_call(state, weight):
    return pl.pallas_call(
        coarse_message_kernel,
        in_specs=[IN_VMEM, IN_VMEM],
        out_specs=IN_VMEM,
        out_shape=pltpu.VMEM((state.shape[0], weight.shape[2]), F32),
        compiler_params=params(12),
        cost_estimate=SMALL,
        name="coarse_message",
    )(state, weight)


def stage_kernel(locals_, count, feat_ref, *refs):
    fine, coarse, state = refs[:3]
    pieces = refs[3 : 3 + locals_]
    refs = refs[3 + locals_ :]
    weights = refs[:count]
    fine_out, coarse_out, state_out, table = refs[count : 4 + count]
    weights_out = refs[4 + count : 4 + 2 * count]
    coarse_buf, sems = refs[4 + 2 * count :]
    block = fine.shape[-1]
    half_rows = state_out.shape[0]
    pairs = [(coarse, coarse_buf)]
    pairs += [
        (fine.at[:, kind], fine_out.at[:, :, pl.ds(kind * block, block)]) for kind in range(fine.shape[1])
    ]
    start = pl.multiple_of(feat_ref[0] * half_rows, 16)
    pairs.append((state.at[pl.ds(start, half_rows)], state_out))
    at = HALO_BLK * block
    for piece in pieces:
        pairs.append((piece, table.at[pl.ds(at, piece.shape[0])]))
        at += piece.shape[0]
    pairs += list(zip(weights, weights_out))
    copies = run_copies(pairs, sems)
    copies[0].wait()

    def turn(pos, carry):
        coarse_out[pos] = jnp.transpose(coarse_buf[pos])
        return carry

    lax.fori_loop(0, coarse.shape[0], turn, 0)
    wait_all(copies[1:])


def stage_call(feat, fine, coarse, state, pieces, weights):
    blocks, kinds, block, _ = fine.shape
    rows, columns = blocks // 2 * block, pieces[0].shape[1]
    out_shape = [
        pltpu.VMEM((blocks, block, kinds * block), BF16),
        pltpu.VMEM((blocks, block, coarse.shape[1]), BF16),
        pltpu.VMEM((rows, state.shape[1]), BF16),
        pltpu.VMEM((2 * rows + 2 * HALO_BLK * block, columns), BF16),
    ] + [pltpu.VMEM(weight.shape, BF16) for weight in weights]
    copies = 2 + kinds + len(pieces) + len(weights)
    return pl.pallas_call(
        functools.partial(stage_kernel, len(pieces), len(weights)),
        grid_spec=pltpu.PrefetchScalarGridSpec(
            num_scalar_prefetch=1,
            in_specs=[IN_HBM] * (3 + len(pieces) + len(weights)),
            out_specs=[IN_VMEM] * len(out_shape),
            scratch_shapes=[pltpu.VMEM(coarse.shape, BF16), pltpu.SemaphoreType.DMA((copies,))],
        ),
        out_shape=out_shape,
        compiler_params=params(36),
        cost_estimate=SMALL,
        name="stage",
    )(feat, fine, coarse, state, *pieces, *weights)


def weights_kernel(*refs):
    sems = refs[-1]
    count = len(refs) // 2
    wait_all(run_copies(list(zip(refs[:count], refs[count:-1])), sems))


def weights_call(weights):
    return pl.pallas_call(
        weights_kernel,
        in_specs=[IN_HBM] * len(weights),
        out_specs=[IN_VMEM] * len(weights),
        scratch_shapes=[pltpu.SemaphoreType.DMA((len(weights),))],
        out_shape=[pltpu.VMEM(weight.shape, BF16) for weight in weights],
        compiler_params=params(4),
        cost_estimate=SMALL,
        name="weights",
    )(*weights)


def local_kernel(places, feat_ref, *refs):
    pieces = refs[: len(places)]
    table, sems = refs[-2:]
    pairs = []
    for place, piece in zip(places, pieces):
        start = pl.multiple_of(place(feat_ref[0]), 16)
        pairs.append((piece, table.at[pl.ds(start, piece.shape[0])]))
    wait_all(run_copies(pairs, sems))


def local_call(feat, places, pieces, table):
    return pl.pallas_call(
        functools.partial(local_kernel, places),
        grid_spec=pltpu.PrefetchScalarGridSpec(
            num_scalar_prefetch=1,
            in_specs=[pl.BlockSpec(memory_space=pl.ANY)] * len(pieces) + [IN_VMEM],
            out_specs=IN_VMEM,
            scratch_shapes=[pltpu.SemaphoreType.DMA((len(pieces),))],
        ),
        out_shape=pltpu.VMEM(table.shape, BF16),
        input_output_aliases={len(pieces) + 1: 0},
        compiler_params=params(4),
        cost_estimate=SMALL,
        name="local_messages",
    )(feat, *pieces, table)


def aggregate_kernel(places, start, feat_ref, links, *refs):
    fine, coarse_tile, coarse, degree = refs[:4]
    pieces = refs[4 : 4 + len(places)]
    if places:
        send, keep, first_rows, table, sems = refs[5 + len(places) :]
        pairs = []
        for place, piece in zip(places, pieces):
            at = pl.multiple_of(place(feat_ref[0]), 16)
            pairs.append((piece, table.at[pl.ds(at, piece.shape[0])]))
        copies = run_copies(pairs, sems)
    else:
        table, send, keep = refs[4:]
        copies = []
    blocks, block, fine_width = fine.shape
    kinds = fine_width // block
    count = send.shape[0] // block
    feat = feat_ref[0]
    wait_all(copies)
    for out_ref, which in ((send, 1 - feat), (keep, feat)):
        scale = 1.0 / jnp.transpose(degree[which].astype(F32))
        first = which * (blocks // 2) + start
        for pos in range(count):
            row = (first + pos) * kinds
            chosen = jnp.concatenate(
                [table[pl.ds(pl.multiple_of(links[row + kind], block), block), :] for kind in range(kinds)], axis=0
            )
            base = blocks * kinds + row
            stacked = jnp.concatenate(
                [
                    coarse[pl.ds(pl.multiple_of(links[base + kind], 8), CN_DEV), :]
                    for kind in range(kinds)
                ],
                axis=0,
            ).astype(BF16)
            summed = dot(fine[first + pos], chosen) + dot(coarse_tile[first + pos], stacked)
            result = (summed * scale[:, start + pos : start + pos + 1]).astype(BF16)
            out_ref[pos * block : (pos + 1) * block, :] = result
    if places:

        @pl.when(feat == 0)
        def _():
            first_rows[...] = keep[:CN_DEV, :]

        @pl.when(feat != 0)
        def _():
            first_rows[...] = send[:CN_DEV, :]


def aggregate_call(feat, links, staged, coarse, degree, table, span, places=(), pieces=()):
    fine, coarse_tile = staged
    blocks, block, _ = fine.shape
    columns = table.shape[1]
    start, count = span
    out_shape = [pltpu.VMEM((count * block, columns), BF16)] * 2
    aliases = {}
    scratch = []
    if pieces:
        out_shape += [pltpu.VMEM((CN_DEV, columns), BF16), pltpu.VMEM(table.shape, BF16)]
        aliases = {6 + len(pieces): 3}
        scratch = [pltpu.SemaphoreType.DMA((len(pieces),))]
    return pl.pallas_call(
        functools.partial(aggregate_kernel, places, start),
        grid_spec=pltpu.PrefetchScalarGridSpec(
            num_scalar_prefetch=2,
            in_specs=[IN_VMEM] * 4 + [IN_HBM] * len(pieces) + [IN_VMEM],
            out_specs=[IN_VMEM] * len(out_shape),
            scratch_shapes=scratch,
        ),
        out_shape=out_shape,
        input_output_aliases=aliases,
        compiler_params=params(12),
        cost_estimate=SMALL,
        name="aggregate",
    )(feat, links, fine, coarse_tile, coarse, degree, *pieces, table)


def node_kernel(mode, layer, start, offset, rows, placed, feat_ref, *refs):
    state_ref, keep, recv, in_own, in_other, out_own, out_other = refs[:7]
    refs = refs[7:]
    feat = feat_ref[0]
    columns = keep.shape[1]
    width = state_ref.shape[1]
    if mode == "last":
        state_out, out, sems = refs[-3:]
        half_rows = out.shape[0] // 2
        pairs = []
        for place, piece in zip(placed, refs):
            at = pl.multiple_of((1 - feat) * half_rows + place, 16)
            pairs.append((piece, out.at[pl.ds(at, piece.shape[0])]))
        copies = run_copies(pairs, sems)
    keep_at = pl.multiple_of(width + feat * columns, columns)
    recv_at = pl.multiple_of(width + (1 - feat) * columns, columns)
    split = NODE_SPLIT if rows % (NODE_SPLIT * 640) == 0 else 1
    size = rows // split
    joined, hidden, state = {}, {}, {}

    def join(at):
        joined[at] = normalize(
            [state_ref[start + at : start + at + size, :].astype(F32)]
            + [ref[offset + at : offset + at + size, :].astype(F32) for ref in (keep, recv)]
        )

    def hide(at):
        parts = joined[at]
        hidden[at] = [
            silu(
                dot(parts[0], in_ref[layer, :width, :])
                + dot(parts[1], in_ref[layer, pl.ds(keep_at, columns), :])
                + dot(parts[2], in_ref[layer, pl.ds(recv_at, columns), :])
            ).astype(BF16)
            for in_ref in (in_own, in_other)
        ]

    def update(at):
        change = dot(hidden[at][0], out_own[layer]) + dot(hidden[at][1], out_other[layer])
        state[at] = (state_ref[start + at : start + at + size, :].astype(F32) + change).astype(BF16)
        if mode == "last":
            state_out[at : at + size, :] = state[at]
        elif mode == "mid":
            refs[2][start + at : start + at + size, :] = state[at]

    def norm(at):
        (joined[at],) = normalize([state[at].astype(F32)])

    def tell(at):
        if mode == "coarse":
            refs[1][...] = silu(dot(joined[at], refs[0][layer + 1])).astype(BF16).astype(F32)
            return
        for weight, message in ((refs[0], refs[3]), (refs[1], refs[4])):
            message[at : at + size, :] = silu(dot(joined[at], weight[layer + 1])).astype(BF16)

    stages = [join, hide, update] + ([] if mode == "last" else [norm, tell])
    for step in range(len(stages) + split - 1):
        for pos in range(split):
            if 0 <= step - pos < len(stages):
                stages[step - pos](pos * size)
    if mode == "last":
        at = pl.multiple_of(feat * half_rows + start, 16)
        copy = pltpu.make_async_copy(state_out, out.at[pl.ds(at, rows)], sems.at[len(placed)])
        copy.start()
        wait_all(copies)
        copy.wait()


def node_call(mode, layer, feat, state, start, offset, rows, keep, recv, weights, out=None, total=0, placed=(), pieces=()):
    columns = keep.shape[1]
    width = state.shape[1]
    operands = [state, keep, recv, *weights[:4]]
    aliases = {}
    scratch = []
    in_specs = [IN_VMEM] * len(operands)
    if mode == "last":
        out_shape = [pltpu.VMEM((rows, width), BF16), jax.ShapeDtypeStruct((total, width), BF16)]
        out_specs = [IN_VMEM, pl.BlockSpec(memory_space=pl.ANY)]
        scratch = [pltpu.SemaphoreType.DMA((1 + len(pieces),))]
        operands += pieces
        in_specs += [IN_VMEM] * len(pieces)
        if out is not None:
            aliases = {len(operands) + 1: 1}
            operands.append(out)
            in_specs.append(pl.BlockSpec(memory_space=pl.ANY))
    else:
        if mode == "coarse":
            operands.append(weights[4])
            out_shape = [pltpu.VMEM((rows, columns), F32)]
        else:
            operands += weights[4:]
            out_shape = [pltpu.VMEM(state.shape, BF16)] + [pltpu.VMEM((rows, columns), BF16)] * 2
            aliases = {1: 0}
        in_specs = [IN_VMEM] * len(operands)
        out_specs = [IN_VMEM] * len(out_shape)
    return pl.pallas_call(
        functools.partial(node_kernel, mode, layer, start, offset, rows, placed),
        grid_spec=pltpu.PrefetchScalarGridSpec(
            num_scalar_prefetch=1, in_specs=in_specs, out_specs=out_specs, scratch_shapes=scratch
        ),
        out_shape=out_shape,
        input_output_aliases=aliases,
        compiler_params=params(28),
        cost_estimate=SMALL,
        name="node_" + mode,
    )(feat, *operands)


def assemble_kernel(placed, feat_ref, *refs):
    pieces = refs[: len(placed)]
    out, sems = refs[-2:]
    half_rows = out.shape[0] // 2
    pairs = []
    for place, piece in zip(placed, pieces):
        at = pl.multiple_of((1 - feat_ref[0]) * half_rows + place, 16)
        pairs.append((piece, out.at[pl.ds(at, piece.shape[0])]))
    wait_all(run_copies(pairs, sems))


def assemble_call(feat, placed, pieces, out):
    return pl.pallas_call(
        functools.partial(assemble_kernel, placed),
        grid_spec=pltpu.PrefetchScalarGridSpec(
            num_scalar_prefetch=1,
            in_specs=[IN_VMEM] * len(pieces) + [pl.BlockSpec(memory_space=pl.ANY)],
            out_specs=pl.BlockSpec(memory_space=pl.ANY),
            scratch_shapes=[pltpu.SemaphoreType.DMA((len(pieces),))],
        ),
        out_shape=shaped(out),
        input_output_aliases={len(pieces) + 1: 0},
        compiler_params=params(4),
        cost_estimate=SMALL,
        name="assemble",
    )(feat, *pieces, out)


def swap_feat(array):
    return lax.ppermute(array, "feat", [(0, 1), (1, 0)])


def fetch(held, stride):
    count = lax.axis_size("patch")
    return lax.ppermute(held, "patch", [(pos, (pos - stride) % count) for pos in range(count)])


def even_offsets(count):
    assert count & (count - 1) == 0
    offsets = [0]
    stride = count // 2
    while stride > 1:
        offsets += [offset + stride for offset in offsets]
        stride //= 2
    return offsets


def shards(
    node_state, fine_tile, coarse_tile, fine_index, coarse_index, node_degree, w_msg, w_in, w_out
):
    barrier = lax.optimization_barrier
    patches = lax.axis_size("patch")
    patch_pos = lax.axis_index("patch")
    feat_pos = lax.axis_index("feat")
    feat = feat_pos.astype(jnp.int32).reshape(1)
    blocks, kinds, block, _ = fine_tile.shape
    half = blocks // 2
    half_rows = half * block
    halo_rows = HALO_BLK * block
    assert half == HALO_BLK == sum(MID_BLOCKS) == sum(LAST_BLOCKS)

    forward = [(pos, pos + 1) for pos in range(patches - 1)]
    backward = [(target, source) for source, target in forward]
    sides = ((0, backward), (1, forward))
    own_patch = [(2 * src + side, 2 * dst + side) for side, pairs in sides for src, dst in pairs]
    other_patch = [(2 * src + side, 2 * dst + 1 - side) for side, pairs in sides for src, dst in pairs]
    evens = even_offsets(patches)

    held = node_state[:CN_DEV]
    held = jnp.concatenate([held, fetch(held, 1)], axis=0)
    sends = []
    halo = []
    for first, count in MESSAGE_ROWS:
        message = message_call(node_state, w_msg, first * block, count * block, MESSAGE_TILE)
        if not sends:
            message, held = barrier((message, held))
        sends.append(message)
        halo.append(lax.ppermute(message, "patch", backward if first < half else forward))
    high = sends[-1]

    offsets = [even + odd for even in evens for odd in (0, 1)]
    fine_index, coarse_index, node_degree, w_in, w_out, w_late, _ = barrier(
        (fine_index, coarse_index, node_degree, w_in, w_out, w_msg, high)
    )
    links = (fine_index - (patch_pos * blocks - HALO_BLK)).reshape(-1) * block
    away = ((coarse_index - patch_pos) % patches).reshape(-1)
    coarse_links = sum(jnp.where(away == offset, pos * CN_DEV, 0) for pos, offset in enumerate(offsets))
    links = jnp.concatenate([links, coarse_links])
    degree = node_degree.reshape(2, half, block)
    fine, ctile, state, table, in_own, out_own, msg_own = stage_call(
        feat, fine_tile, jnp.swapaxes(coarse_tile, 1, 2), node_state, sends, (w_in, w_out, w_late)
    )
    staged = (fine, ctile)
    others = weights_call([swap_feat(w_in), swap_feat(w_out), swap_feat(w_late)])
    strides = [patches >> step for step in range(1, patches.bit_length() - 1)]
    for step, stride in enumerate(strides):
        got = fetch(held, stride)
        if step == 0:
            got, links, degree, table = barrier((got, links, degree, table))
        if step == len(strides) - 1:
            got, others = barrier((got, others))
        held = jnp.concatenate([held, got], axis=0)
    coarse_state = held
    weights = [in_own, others[0], out_own, others[1], msg_own, others[2]]
    coarse = coarse_message_call(coarse_state, msg_own)

    halo_places = [
        lambda feat, at=first * block: halo_rows + 2 * half_rows + at if at < half_rows else at - half_rows
        for first, _ in MESSAGE_ROWS
    ]
    first_span, last_span = (0, MID_BLOCKS[0]), MID_BLOCKS
    send, keep, first_rows, table = aggregate_call(
        feat, links, staged, coarse, degree, table, first_span, halo_places, halo
    )
    recv = swap_feat(send)
    got = fetch(first_rows, 1)
    send_1, keep_1 = aggregate_call(feat, links, staged, coarse, degree, table, last_span)
    recv, keep, send_1, got = barrier((recv, keep, send_1, got))
    held = jnp.concatenate([first_rows, got], axis=0)
    got = fetch(held, strides[0])
    inputs = [(keep, recv), (keep_1, swap_feat(send_1))]
    local = []
    local_places = []
    halo = []
    halo_places = []
    at = 0
    for chunk, count in enumerate(MID_BLOCKS):
        rows = count * block
        state, own, other = node_call("mid", 0, feat, state, at, 0, rows, *inputs[chunk], weights)
        if chunk == 0:
            own, other, got = barrier((own, other, got))
            held = jnp.concatenate([held, got], axis=0)
        sibling = swap_feat(other)
        if chunk == 0:
            sibling, state = barrier((sibling, state))
        halo += [lax.ppermute(own, ("patch", "feat"), own_patch), lax.ppermute(other, ("patch", "feat"), other_patch)]
        local += [own, sibling]
        local_places += [
            lambda feat, at=at: halo_rows + feat * half_rows + at,
            lambda feat, at=at: halo_rows + (1 - feat) * half_rows + at,
        ]
        halo_places += [
            lambda feat, at=at: (1 - feat) * (halo_rows + 2 * half_rows) + at,
            lambda feat, at=at: feat * (halo_rows + 2 * half_rows) + at,
        ]
        at += rows

    early = len(halo) - 2
    table = local_call(feat, local_places + halo_places[:early], local + halo[:early], table)
    held, table = barrier((held, table))
    for stride in strides[1:]:
        held = jnp.concatenate([held, fetch(held, stride)], axis=0)
    (coarse,) = node_call(
        "coarse", 0, feat, coarse_state, 0, 0, held.shape[0], held, swap_feat(held), weights
    )
    send, keep, _, table = aggregate_call(
        feat, links, staged, coarse, degree, table, (0, LAST_BLOCKS[0]), halo_places[early:], halo[early:]
    )
    recv = swap_feat(send)
    send_1, keep_1 = aggregate_call(feat, links, staged, coarse, degree, table, LAST_BLOCKS)
    recv, keep, send_1 = barrier((recv, keep, send_1))
    inputs = [(keep, recv), (keep_1, swap_feat(send_1))]
    out = None
    swapped = []
    placed = []
    for chunk, offset, count in LAST_ROWS:
        at = (chunk * LAST_BLOCKS[0] + offset) * block
        done = 1 if len(swapped) == len(LAST_ROWS) - 1 else 0
        new_state, out = node_call(
            "last", 1, feat, state, at, offset * block, count * block, *inputs[chunk], weights,
            out, node_state.shape[0], placed[:done], swapped[:done],
        )
        swapped.append(swap_feat(new_state))
        placed.append(at)
    return assemble_call(feat, placed[1:], swapped[1:], out)


def solution(mesh):
    return jax.shard_map(
        shards,
        mesh=mesh,
        in_specs=(
            P(("member", "patch"), None),
            P("patch", None, None, None),
            P("patch", None, None),
            P("patch", None),
            P("patch", None),
            P("patch"),
            P(None, None, "feat"),
            P(None, None, "feat"),
            P(None, "feat", None),
        ),
        out_specs=P(("member", "patch"), None),
        check_vma=False,
    )
```

```python
import functools

import jax
import jax.numpy as jnp
from jax import lax
from jax.experimental import pallas as pl
from jax.experimental.pallas import tpu as pltpu
from jax.sharding import PartitionSpec as P

CN_DEV = 40
LAYERS = 2
HALO_BLK = 20
MID_BLOCKS = (10, 10)
LAST_BLOCKS = (10, 10)
LAST_ROWS = ((0, 0, 10), (1, 0, 5), (1, 5, 5))
MESSAGE_ROWS = ((0, 20), (20, 20))
MESSAGE_TILE = 640
NODE_SPLIT = 2
F32 = jnp.float32
BF16 = jnp.bfloat16
LONG = pl.CostEstimate(flops=1 << 33, transcendentals=0, bytes_accessed=1 << 10)
SMALL = pl.CostEstimate(flops=1 << 20, transcendentals=0, bytes_accessed=1 << 10)
IN_VMEM = pl.BlockSpec(memory_space=pltpu.VMEM)
IN_HBM = pl.BlockSpec(memory_space=pltpu.HBM)


def silu(v):
    return 0.5 * v * (1.0 + jnp.tanh(0.5 * v))


def dot(a, b):
    return jnp.dot(a, b, preferred_element_type=F32)


def normalize(parts):
    width = sum(part.shape[-1] for part in parts)
    mean = sum(jnp.sum(part, axis=-1, keepdims=True) for part in parts) / width
    center = [part - mean for part in parts]
    spread = sum(jnp.sum(part * part, axis=-1, keepdims=True) for part in center) / width
    scale = lax.rsqrt(spread + 1e-05)
    return [(part * scale).astype(BF16) for part in center]


def params(mib):
    return pltpu.CompilerParams(vmem_limit_bytes=mib << 20)


def shaped(array):
    return jax.ShapeDtypeStruct(array.shape, array.dtype)


def run_copies(pairs, sems):
    copies = [pltpu.make_async_copy(src, dst, sems.at[pos]) for pos, (src, dst) in enumerate(pairs)]
    for copy in copies:
        copy.start()
    return copies


def wait_all(copies):
    for copy in copies:
        copy.wait()


def coarse_message_kernel(state_ref, weight_ref, out_ref):
    (normed,) = normalize([state_ref[...].astype(F32)])
    out_ref[...] = silu(dot(normed, weight_ref[0])).astype(BF16).astype(F32)


def message_kernel(start, tile, state, weight, out, state_buf, weight_buf, out_ref, sems):
    rows = out_ref.shape[0]
    tiles = [(at, tile) for at in range(0, rows, tile)]
    pairs = [(state.at[pl.ds(start + at, size)], state_buf.at[pl.ds(at, size)]) for at, size in tiles]
    copies = run_copies(pairs[:1] + [(weight.at[0], weight_buf)] + pairs[1:], sems)
    weight_copy = copies.pop(1)
    normed = []
    for pos in range(len(tiles) + 1):
        if pos < len(tiles):
            at, size = tiles[pos]
            copies[pos].wait()
            normed += normalize([state_buf[at : at + size, :].astype(F32)])
        if pos == 0:
            weight_copy.wait()
            continue
        at, size = tiles[pos - 1]
        out_ref[at : at + size, :] = silu(dot(normed[pos - 1], weight_buf[...])).astype(BF16)
        span = pl.ds(at, size)
        copy = pltpu.make_async_copy(out_ref.at[span], out.at[span], sems.at[len(tiles) + pos])
        copy.start()
        copies.append(copy)
    wait_all(copies[len(tiles) :])


def message_call(state, weight, start, rows, tile):
    width, columns = weight.shape[1:]
    return pl.pallas_call(
        functools.partial(message_kernel, start, tile),
        in_specs=[IN_HBM, IN_HBM],
        out_specs=IN_HBM,
        out_shape=jax.ShapeDtypeStruct((rows, columns), BF16),
        scratch_shapes=[
            pltpu.VMEM((rows, width), BF16),
            pltpu.VMEM((width, columns), BF16),
            pltpu.VMEM((rows, columns), BF16),
            pltpu.SemaphoreType.DMA((1 + 2 * (rows // tile),)),
        ],
        compiler_params=params(56),
        cost_estimate=SMALL,
        name="message",
    )(state, weight)


def coarse_message_call(state, weight):
    return pl.pallas_call(
        coarse_message_kernel,
        in_specs=[IN_VMEM, IN_VMEM],
        out_specs=IN_VMEM,
        out_shape=pltpu.VMEM((state.shape[0], weight.shape[2]), F32),
        compiler_params=params(12),
        cost_estimate=SMALL,
        name="coarse_message",
    )(state, weight)


def stage_kernel(locals_, count, feat_ref, *refs):
    fine, coarse, state = refs[:3]
    pieces = refs[3 : 3 + locals_]
    refs = refs[3 + locals_ :]
    weights = refs[:count]
    fine_out, coarse_out, state_out, table = refs[count : 4 + count]
    weights_out = refs[4 + count : 4 + 2 * count]
    coarse_buf, sems = refs[4 + 2 * count :]
    block = fine.shape[-1]
    half_rows = state_out.shape[0]
    pairs = [(coarse, coarse_buf)]
    pairs += [
        (fine.at[:, kind], fine_out.at[:, :, pl.ds(kind * block, block)]) for kind in range(fine.shape[1])
    ]
    start = pl.multiple_of(feat_ref[0] * half_rows, 16)
    pairs.append((state.at[pl.ds(start, half_rows)], state_out))
    at = HALO_BLK * block
    for piece in pieces:
        pairs.append((piece, table.at[pl.ds(at, piece.shape[0])]))
        at += piece.shape[0]
    pairs += list(zip(weights, weights_out))
    copies = run_copies(pairs, sems)
    copies[0].wait()

    def turn(pos, carry):
        coarse_out[pos] = jnp.transpose(coarse_buf[pos])
        return carry

    lax.fori_loop(0, coarse.shape[0], turn, 0)
    wait_all(copies[1:])


def stage_call(feat, fine, coarse, state, pieces, weights):
    blocks, kinds, block, _ = fine.shape
    rows, columns = blocks // 2 * block, pieces[0].shape[1]
    out_shape = [
        pltpu.VMEM((blocks, block, kinds * block), BF16),
        pltpu.VMEM((blocks, block, coarse.shape[1]), BF16),
        pltpu.VMEM((rows, state.shape[1]), BF16),
        pltpu.VMEM((2 * rows + 2 * HALO_BLK * block, columns), BF16),
    ] + [pltpu.VMEM(weight.shape, BF16) for weight in weights]
    copies = 2 + kinds + len(pieces) + len(weights)
    return pl.pallas_call(
        functools.partial(stage_kernel, len(pieces), len(weights)),
        grid_spec=pltpu.PrefetchScalarGridSpec(
            num_scalar_prefetch=1,
            in_specs=[IN_HBM] * (3 + len(pieces) + len(weights)),
            out_specs=[IN_VMEM] * len(out_shape),
            scratch_shapes=[pltpu.VMEM(coarse.shape, BF16), pltpu.SemaphoreType.DMA((copies,))],
        ),
        out_shape=out_shape,
        compiler_params=params(36),
        cost_estimate=SMALL,
        name="stage",
    )(feat, fine, coarse, state, *pieces, *weights)


def weights_kernel(*refs):
    sems = refs[-1]
    count = len(refs) // 2
    wait_all(run_copies(list(zip(refs[:count], refs[count:-1])), sems))


def weights_call(weights):
    return pl.pallas_call(
        weights_kernel,
        in_specs=[IN_HBM] * len(weights),
        out_specs=[IN_VMEM] * len(weights),
        scratch_shapes=[pltpu.SemaphoreType.DMA((len(weights),))],
        out_shape=[pltpu.VMEM(weight.shape, BF16) for weight in weights],
        compiler_params=params(4),
        cost_estimate=SMALL,
        name="weights",
    )(*weights)


def local_kernel(places, feat_ref, *refs):
    pieces = refs[: len(places)]
    table, sems = refs[-2:]
    pairs = []
    for place, piece in zip(places, pieces):
        start = pl.multiple_of(place(feat_ref[0]), 16)
        pairs.append((piece, table.at[pl.ds(start, piece.shape[0])]))
    wait_all(run_copies(pairs, sems))


def local_call(feat, places, pieces, table):
    return pl.pallas_call(
        functools.partial(local_kernel, places),
        grid_spec=pltpu.PrefetchScalarGridSpec(
            num_scalar_prefetch=1,
            in_specs=[pl.BlockSpec(memory_space=pl.ANY)] * len(pieces) + [IN_VMEM],
            out_specs=IN_VMEM,
            scratch_shapes=[pltpu.SemaphoreType.DMA((len(pieces),))],
        ),
        out_shape=pltpu.VMEM(table.shape, BF16),
        input_output_aliases={len(pieces) + 1: 0},
        compiler_params=params(4),
        cost_estimate=SMALL,
        name="local_messages",
    )(feat, *pieces, table)


def aggregate_kernel(places, start, feat_ref, links, *refs):
    fine, coarse_tile, coarse, degree = refs[:4]
    pieces = refs[4 : 4 + len(places)]
    if places:
        send, keep, first_rows, table, sems = refs[5 + len(places) :]
        pairs = []
        for place, piece in zip(places, pieces):
            at = pl.multiple_of(place(feat_ref[0]), 16)
            pairs.append((piece, table.at[pl.ds(at, piece.shape[0])]))
        copies = run_copies(pairs, sems)
    else:
        table, send, keep = refs[4:]
        copies = []
    blocks, block, fine_width = fine.shape
    kinds = fine_width // block
    count = send.shape[0] // block
    feat = feat_ref[0]
    wait_all(copies)
    for out_ref, which in ((send, 1 - feat), (keep, feat)):
        scale = 1.0 / jnp.transpose(degree[which].astype(F32))
        first = which * (blocks // 2) + start
        for pos in range(count):
            row = (first + pos) * kinds
            chosen = jnp.concatenate(
                [table[pl.ds(pl.multiple_of(links[row + kind], block), block), :] for kind in range(kinds)], axis=0
            )
            base = blocks * kinds + row
            stacked = jnp.concatenate(
                [
                    coarse[pl.ds(pl.multiple_of(links[base + kind], 8), CN_DEV), :]
                    for kind in range(kinds)
                ],
                axis=0,
            ).astype(BF16)
            summed = dot(fine[first + pos], chosen) + dot(coarse_tile[first + pos], stacked)
            result = (summed * scale[:, start + pos : start + pos + 1]).astype(BF16)
            out_ref[pos * block : (pos + 1) * block, :] = result
    if places:

        @pl.when(feat == 0)
        def _():
            first_rows[...] = keep[:CN_DEV, :]

        @pl.when(feat != 0)
        def _():
            first_rows[...] = send[:CN_DEV, :]


def aggregate_call(feat, links, staged, coarse, degree, table, span, places=(), pieces=()):
    fine, coarse_tile = staged
    blocks, block, _ = fine.shape
    columns = table.shape[1]
    start, count = span
    out_shape = [pltpu.VMEM((count * block, columns), BF16)] * 2
    aliases = {}
    scratch = []
    if pieces:
        out_shape += [pltpu.VMEM((CN_DEV, columns), BF16), pltpu.VMEM(table.shape, BF16)]
        aliases = {6 + len(pieces): 3}
        scratch = [pltpu.SemaphoreType.DMA((len(pieces),))]
    return pl.pallas_call(
        functools.partial(aggregate_kernel, places, start),
        grid_spec=pltpu.PrefetchScalarGridSpec(
            num_scalar_prefetch=2,
            in_specs=[IN_VMEM] * 4 + [IN_HBM] * len(pieces) + [IN_VMEM],
            out_specs=[IN_VMEM] * len(out_shape),
            scratch_shapes=scratch,
        ),
        out_shape=out_shape,
        input_output_aliases=aliases,
        compiler_params=params(12),
        cost_estimate=SMALL,
        name="aggregate",
    )(feat, links, fine, coarse_tile, coarse, degree, *pieces, table)


def node_kernel(mode, layer, start, offset, rows, placed, feat_ref, *refs):
    state_ref, keep, recv, in_own, in_other, out_own, out_other = refs[:7]
    refs = refs[7:]
    feat = feat_ref[0]
    columns = keep.shape[1]
    width = state_ref.shape[1]
    if mode == "last":
        state_out, out, sems = refs[-3:]
        half_rows = out.shape[0] // 2
        pairs = []
        for place, piece in zip(placed, refs):
            at = pl.multiple_of((1 - feat) * half_rows + place, 16)
            pairs.append((piece, out.at[pl.ds(at, piece.shape[0])]))
        copies = run_copies(pairs, sems)
    keep_at = pl.multiple_of(width + feat * columns, columns)
    recv_at = pl.multiple_of(width + (1 - feat) * columns, columns)
    split = NODE_SPLIT if rows % (NODE_SPLIT * 640) == 0 else 1
    size = rows // split
    joined, hidden, state = {}, {}, {}

    def join(at):
        joined[at] = normalize(
            [state_ref[start + at : start + at + size, :].astype(F32)]
            + [ref[offset + at : offset + at + size, :].astype(F32) for ref in (keep, recv)]
        )

    def hide(at):
        parts = joined[at]
        hidden[at] = [
            silu(
                dot(parts[0], in_ref[layer, :width, :])
                + dot(parts[1], in_ref[layer, pl.ds(keep_at, columns), :])
                + dot(parts[2], in_ref[layer, pl.ds(recv_at, columns), :])
            ).astype(BF16)
            for in_ref in (in_own, in_other)
        ]

    def update(at):
        change = dot(hidden[at][0], out_own[layer]) + dot(hidden[at][1], out_other[layer])
        state[at] = (state_ref[start + at : start + at + size, :].astype(F32) + change).astype(BF16)
        if mode == "last":
            state_out[at : at + size, :] = state[at]
        elif mode == "mid":
            refs[2][start + at : start + at + size, :] = state[at]

    def norm(at):
        (joined[at],) = normalize([state[at].astype(F32)])

    def tell(at):
        if mode == "coarse":
            refs[1][...] = silu(dot(joined[at], refs[0][layer + 1])).astype(BF16).astype(F32)
            return
        for weight, message in ((refs[0], refs[3]), (refs[1], refs[4])):
            message[at : at + size, :] = silu(dot(joined[at], weight[layer + 1])).astype(BF16)

    stages = [join, hide, update] + ([] if mode == "last" else [norm, tell])
    for step in range(len(stages) + split - 1):
        for pos in range(split):
            if 0 <= step - pos < len(stages):
                stages[step - pos](pos * size)
    if mode == "last":
        at = pl.multiple_of(feat * half_rows + start, 16)
        copy = pltpu.make_async_copy(state_out, out.at[pl.ds(at, rows)], sems.at[len(placed)])
        copy.start()
        wait_all(copies)
        copy.wait()


def node_call(mode, layer, feat, state, start, offset, rows, keep, recv, weights, out=None, total=0, placed=(), pieces=()):
    columns = keep.shape[1]
    width = state.shape[1]
    operands = [state, keep, recv, *weights[:4]]
    aliases = {}
    scratch = []
    in_specs = [IN_VMEM] * len(operands)
    if mode == "last":
        out_shape = [pltpu.VMEM((rows, width), BF16), jax.ShapeDtypeStruct((total, width), BF16)]
        out_specs = [IN_VMEM, pl.BlockSpec(memory_space=pl.ANY)]
        scratch = [pltpu.SemaphoreType.DMA((1 + len(pieces),))]
        operands += pieces
        in_specs += [IN_VMEM] * len(pieces)
        if out is not None:
            aliases = {len(operands) + 1: 1}
            operands.append(out)
            in_specs.append(pl.BlockSpec(memory_space=pl.ANY))
    else:
        if mode == "coarse":
            operands.append(weights[4])
            out_shape = [pltpu.VMEM((rows, columns), F32)]
        else:
            operands += weights[4:]
            out_shape = [pltpu.VMEM(state.shape, BF16)] + [pltpu.VMEM((rows, columns), BF16)] * 2
            aliases = {1: 0}
        in_specs = [IN_VMEM] * len(operands)
        out_specs = [IN_VMEM] * len(out_shape)
    return pl.pallas_call(
        functools.partial(node_kernel, mode, layer, start, offset, rows, placed),
        grid_spec=pltpu.PrefetchScalarGridSpec(
            num_scalar_prefetch=1, in_specs=in_specs, out_specs=out_specs, scratch_shapes=scratch
        ),
        out_shape=out_shape,
        input_output_aliases=aliases,
        compiler_params=params(28),
        cost_estimate=LONG if mode == "last" else SMALL,
        name="node_" + mode,
    )(feat, *operands)


def assemble_kernel(placed, feat_ref, *refs):
    pieces = refs[: len(placed)]
    out, sems = refs[-2:]
    half_rows = out.shape[0] // 2
    pairs = []
    for place, piece in zip(placed, pieces):
        at = pl.multiple_of((1 - feat_ref[0]) * half_rows + place, 16)
        pairs.append((piece, out.at[pl.ds(at, piece.shape[0])]))
    wait_all(run_copies(pairs, sems))


def assemble_call(feat, placed, pieces, out):
    return pl.pallas_call(
        functools.partial(assemble_kernel, placed),
        grid_spec=pltpu.PrefetchScalarGridSpec(
            num_scalar_prefetch=1,
            in_specs=[IN_VMEM] * len(pieces) + [pl.BlockSpec(memory_space=pl.ANY)],
            out_specs=pl.BlockSpec(memory_space=pl.ANY),
            scratch_shapes=[pltpu.SemaphoreType.DMA((len(pieces),))],
        ),
        out_shape=shaped(out),
        input_output_aliases={len(pieces) + 1: 0},
        compiler_params=params(4),
        cost_estimate=SMALL,
        name="assemble",
    )(feat, *pieces, out)


def swap_feat(array):
    return lax.ppermute(array, "feat", [(0, 1), (1, 0)])


def fetch(held, stride):
    count = lax.axis_size("patch")
    return lax.ppermute(held, "patch", [(pos, (pos - stride) % count) for pos in range(count)])


def even_offsets(count):
    assert count & (count - 1) == 0
    offsets = [0]
    stride = count // 2
    while stride > 1:
        offsets += [offset + stride for offset in offsets]
        stride //= 2
    return offsets


def shards(
    node_state, fine_tile, coarse_tile, fine_index, coarse_index, node_degree, w_msg, w_in, w_out
):
    barrier = lax.optimization_barrier
    patches = lax.axis_size("patch")
    patch_pos = lax.axis_index("patch")
    feat_pos = lax.axis_index("feat")
    feat = feat_pos.astype(jnp.int32).reshape(1)
    blocks, kinds, block, _ = fine_tile.shape
    half = blocks // 2
    half_rows = half * block
    halo_rows = HALO_BLK * block
    assert half == HALO_BLK == sum(MID_BLOCKS) == sum(LAST_BLOCKS)

    forward = [(pos, pos + 1) for pos in range(patches - 1)]
    backward = [(target, source) for source, target in forward]
    sides = ((0, backward), (1, forward))
    own_patch = [(2 * src + side, 2 * dst + side) for side, pairs in sides for src, dst in pairs]
    other_patch = [(2 * src + side, 2 * dst + 1 - side) for side, pairs in sides for src, dst in pairs]
    evens = even_offsets(patches)

    held = node_state[:CN_DEV]
    held = jnp.concatenate([held, fetch(held, 1)], axis=0)
    sends = []
    halo = []
    for first, count in MESSAGE_ROWS:
        message = message_call(node_state, w_msg, first * block, count * block, MESSAGE_TILE)
        if not sends:
            message, held = barrier((message, held))
        sends.append(message)
        halo.append(lax.ppermute(message, "patch", backward if first < half else forward))
    high = sends[-1]

    offsets = [even + odd for even in evens for odd in (0, 1)]
    fine_index, coarse_index, node_degree, w_in, w_out, w_late, _ = barrier(
        (fine_index, coarse_index, node_degree, w_in, w_out, w_msg, high)
    )
    links = (fine_index - (patch_pos * blocks - HALO_BLK)).reshape(-1) * block
    away = ((coarse_index - patch_pos) % patches).reshape(-1)
    coarse_links = sum(jnp.where(away == offset, pos * CN_DEV, 0) for pos, offset in enumerate(offsets))
    links = jnp.concatenate([links, coarse_links])
    degree = node_degree.reshape(2, half, block)
    fine, ctile, state, table, in_own, out_own, msg_own = stage_call(
        feat, fine_tile, jnp.swapaxes(coarse_tile, 1, 2), node_state, sends, (w_in, w_out, w_late)
    )
    staged = (fine, ctile)
    others = weights_call([swap_feat(w_in), swap_feat(w_out), swap_feat(w_late)])
    strides = [patches >> step for step in range(1, patches.bit_length() - 1)]
    for step, stride in enumerate(strides):
        got = fetch(held, stride)
        if step == 0:
            got, links, degree, table = barrier((got, links, degree, table))
        if step == len(strides) - 1:
            got, others = barrier((got, others))
        held = jnp.concatenate([held, got], axis=0)
    coarse_state = held
    weights = [in_own, others[0], out_own, others[1], msg_own, others[2]]
    coarse = coarse_message_call(coarse_state, msg_own)

    halo_places = [
        lambda feat, at=first * block: halo_rows + 2 * half_rows + at if at < half_rows else at - half_rows
        for first, _ in MESSAGE_ROWS
    ]
    first_span, last_span = (0, MID_BLOCKS[0]), MID_BLOCKS
    send, keep, first_rows, table = aggregate_call(
        feat, links, staged, coarse, degree, table, first_span, halo_places, halo
    )
    recv = swap_feat(send)
    got = fetch(first_rows, 1)
    send_1, keep_1 = aggregate_call(feat, links, staged, coarse, degree, table, last_span)
    recv, keep, send_1, got = barrier((recv, keep, send_1, got))
    held = jnp.concatenate([first_rows, got], axis=0)
    got = fetch(held, strides[0])
    inputs = [(keep, recv), (keep_1, swap_feat(send_1))]
    local = []
    local_places = []
    halo = []
    halo_places = []
    at = 0
    for chunk, count in enumerate(MID_BLOCKS):
        rows = count * block
        state, own, other = node_call("mid", 0, feat, state, at, 0, rows, *inputs[chunk], weights)
        if chunk == 0:
            own, other, got = barrier((own, other, got))
            held = jnp.concatenate([held, got], axis=0)
        sibling = swap_feat(other)
        if chunk == 0:
            sibling, state = barrier((sibling, state))
        halo += [lax.ppermute(own, ("patch", "feat"), own_patch), lax.ppermute(other, ("patch", "feat"), other_patch)]
        local += [own, sibling]
        local_places += [
            lambda feat, at=at: halo_rows + feat * half_rows + at,
            lambda feat, at=at: halo_rows + (1 - feat) * half_rows + at,
        ]
        halo_places += [
            lambda feat, at=at: (1 - feat) * (halo_rows + 2 * half_rows) + at,
            lambda feat, at=at: feat * (halo_rows + 2 * half_rows) + at,
        ]
        at += rows

    early = len(halo) - 2
    table = local_call(feat, local_places + halo_places[:early], local + halo[:early], table)
    held, table = barrier((held, table))
    for stride in strides[1:]:
        held = jnp.concatenate([held, fetch(held, stride)], axis=0)
    (coarse,) = node_call(
        "coarse", 0, feat, coarse_state, 0, 0, held.shape[0], held, swap_feat(held), weights
    )
    send, keep, _, table = aggregate_call(
        feat, links, staged, coarse, degree, table, (0, LAST_BLOCKS[0]), halo_places[early:], halo[early:]
    )
    recv = swap_feat(send)
    send_1, keep_1 = aggregate_call(feat, links, staged, coarse, degree, table, LAST_BLOCKS)
    recv, keep, send_1 = barrier((recv, keep, send_1))
    inputs = [(keep, recv), (keep_1, swap_feat(send_1))]
    out = None
    swapped = []
    placed = []
    for chunk, offset, count in LAST_ROWS:
        at = (chunk * LAST_BLOCKS[0] + offset) * block
        done = 1 if len(swapped) == len(LAST_ROWS) - 1 else 0
        new_state, out = node_call(
            "last", 1, feat, state, at, offset * block, count * block, *inputs[chunk], weights,
            out, node_state.shape[0], placed[:done], swapped[:done],
        )
        swapped.append(swap_feat(new_state))
        placed.append(at)
    return assemble_call(feat, placed[1:], swapped[1:], out)


def solution(mesh):
    return jax.shard_map(
        shards,
        mesh=mesh,
        in_specs=(
            P(("member", "patch"), None),
            P("patch", None, None, None),
            P("patch", None, None),
            P("patch", None),
            P("patch", None),
            P("patch"),
            P(None, None, "feat"),
            P(None, None, "feat"),
            P(None, "feat", None),
        ),
        out_specs=P(("member", "patch"), None),
        check_vma=False,
    )
```

```python
import functools

import jax
import jax.numpy as jnp
from jax import lax
from jax.experimental import pallas as pl
from jax.experimental.pallas import tpu as pltpu
from jax.sharding import PartitionSpec as P

CN_DEV = 40
LAYERS = 2
HALO_BLK = 20
MID_BLOCKS = (10, 10)
LAST_BLOCKS = (10, 10)
LAST_ROWS = ((0, 0, 10), (1, 0, 5), (1, 5, 5))
MESSAGE_ROWS = ((0, 20), (20, 20))
MESSAGE_TILE = 640
NODE_SPLIT = 2
F32 = jnp.float32
BF16 = jnp.bfloat16
LONG = pl.CostEstimate(flops=1 << 33, transcendentals=0, bytes_accessed=1 << 10)
SMALL = pl.CostEstimate(flops=1 << 20, transcendentals=0, bytes_accessed=1 << 10)
IN_VMEM = pl.BlockSpec(memory_space=pltpu.VMEM)
IN_HBM = pl.BlockSpec(memory_space=pltpu.HBM)


def silu(v):
    return 0.5 * v * (1.0 + jnp.tanh(0.5 * v))


def dot(a, b):
    return jnp.dot(a, b, preferred_element_type=F32)


def normalize(parts):
    width = sum(part.shape[-1] for part in parts)
    mean = sum(jnp.sum(part, axis=-1, keepdims=True) for part in parts) / width
    center = [part - mean for part in parts]
    spread = sum(jnp.sum(part * part, axis=-1, keepdims=True) for part in center) / width
    scale = lax.rsqrt(spread + 1e-05)
    return [(part * scale).astype(BF16) for part in center]


def params(mib):
    return pltpu.CompilerParams(vmem_limit_bytes=mib << 20)


def shaped(array):
    return jax.ShapeDtypeStruct(array.shape, array.dtype)


def run_copies(pairs, sems):
    copies = [pltpu.make_async_copy(src, dst, sems.at[pos]) for pos, (src, dst) in enumerate(pairs)]
    for copy in copies:
        copy.start()
    return copies


def wait_all(copies):
    for copy in copies:
        copy.wait()


def coarse_message_kernel(state_ref, weight_ref, out_ref):
    (normed,) = normalize([state_ref[...].astype(F32)])
    out_ref[...] = silu(dot(normed, weight_ref[0])).astype(BF16).astype(F32)


def message_kernel(start, tile, state, weight, out, state_buf, weight_buf, out_ref, sems):
    rows = out_ref.shape[0]
    tiles = [(at, tile) for at in range(0, rows, tile)]
    pairs = [(state.at[pl.ds(start + at, size)], state_buf.at[pl.ds(at, size)]) for at, size in tiles]
    copies = run_copies(pairs[:1] + [(weight.at[0], weight_buf)] + pairs[1:], sems)
    weight_copy = copies.pop(1)
    normed = []
    for pos in range(len(tiles) + 1):
        if pos < len(tiles):
            at, size = tiles[pos]
            copies[pos].wait()
            normed += normalize([state_buf[at : at + size, :].astype(F32)])
        if pos == 0:
            weight_copy.wait()
            continue
        at, size = tiles[pos - 1]
        out_ref[at : at + size, :] = silu(dot(normed[pos - 1], weight_buf[...])).astype(BF16)
        span = pl.ds(at, size)
        copy = pltpu.make_async_copy(out_ref.at[span], out.at[span], sems.at[len(tiles) + pos])
        copy.start()
        copies.append(copy)
    wait_all(copies[len(tiles) :])


def message_call(state, weight, start, rows, tile):
    width, columns = weight.shape[1:]
    return pl.pallas_call(
        functools.partial(message_kernel, start, tile),
        in_specs=[IN_HBM, IN_HBM],
        out_specs=IN_HBM,
        out_shape=jax.ShapeDtypeStruct((rows, columns), BF16),
        scratch_shapes=[
            pltpu.VMEM((rows, width), BF16),
            pltpu.VMEM((width, columns), BF16),
            pltpu.VMEM((rows, columns), BF16),
            pltpu.SemaphoreType.DMA((1 + 2 * (rows // tile),)),
        ],
        compiler_params=params(56),
        cost_estimate=SMALL,
        name="message",
    )(state, weight)


def coarse_message_call(state, weight):
    return pl.pallas_call(
        coarse_message_kernel,
        in_specs=[IN_VMEM, IN_VMEM],
        out_specs=IN_VMEM,
        out_shape=pltpu.VMEM((state.shape[0], weight.shape[2]), F32),
        compiler_params=params(12),
        cost_estimate=SMALL,
        name="coarse_message",
    )(state, weight)


def stage_kernel(locals_, count, feat_ref, *refs):
    fine, coarse, state = refs[:3]
    pieces = refs[3 : 3 + locals_]
    refs = refs[3 + locals_ :]
    weights = refs[:count]
    fine_out, coarse_out, state_out, table = refs[count : 4 + count]
    weights_out = refs[4 + count : 4 + 2 * count]
    coarse_buf, sems = refs[4 + 2 * count :]
    block = fine.shape[-1]
    half_rows = state_out.shape[0]
    pairs = [(coarse, coarse_buf)]
    pairs += [
        (fine.at[:, kind], fine_out.at[:, :, pl.ds(kind * block, block)]) for kind in range(fine.shape[1])
    ]
    start = pl.multiple_of(feat_ref[0] * half_rows, 16)
    pairs.append((state.at[pl.ds(start, half_rows)], state_out))
    at = HALO_BLK * block
    for piece in pieces:
        pairs.append((piece, table.at[pl.ds(at, piece.shape[0])]))
        at += piece.shape[0]
    pairs += list(zip(weights, weights_out))
    copies = run_copies(pairs, sems)
    copies[0].wait()

    def turn(pos, carry):
        coarse_out[pos] = jnp.transpose(coarse_buf[pos])
        return carry

    lax.fori_loop(0, coarse.shape[0], turn, 0)
    wait_all(copies[1:])


def stage_call(feat, fine, coarse, state, pieces, weights):
    blocks, kinds, block, _ = fine.shape
    rows, columns = blocks // 2 * block, pieces[0].shape[1]
    out_shape = [
        pltpu.VMEM((blocks, block, kinds * block), BF16),
        pltpu.VMEM((blocks, block, coarse.shape[1]), BF16),
        pltpu.VMEM((rows, state.shape[1]), BF16),
        pltpu.VMEM((2 * rows + 2 * HALO_BLK * block, columns), BF16),
    ] + [pltpu.VMEM(weight.shape, BF16) for weight in weights]
    copies = 2 + kinds + len(pieces) + len(weights)
    return pl.pallas_call(
        functools.partial(stage_kernel, len(pieces), len(weights)),
        grid_spec=pltpu.PrefetchScalarGridSpec(
            num_scalar_prefetch=1,
            in_specs=[IN_HBM] * (3 + len(pieces) + len(weights)),
            out_specs=[IN_VMEM] * len(out_shape),
            scratch_shapes=[pltpu.VMEM(coarse.shape, BF16), pltpu.SemaphoreType.DMA((copies,))],
        ),
        out_shape=out_shape,
        compiler_params=params(36),
        cost_estimate=SMALL,
        name="stage",
    )(feat, fine, coarse, state, *pieces, *weights)


def weights_kernel(*refs):
    sems = refs[-1]
    count = len(refs) // 2
    wait_all(run_copies(list(zip(refs[:count], refs[count:-1])), sems))


def weights_call(weights):
    return pl.pallas_call(
        weights_kernel,
        in_specs=[IN_HBM] * len(weights),
        out_specs=[IN_VMEM] * len(weights),
        scratch_shapes=[pltpu.SemaphoreType.DMA((len(weights),))],
        out_shape=[pltpu.VMEM(weight.shape, BF16) for weight in weights],
        compiler_params=params(4),
        cost_estimate=SMALL,
        name="weights",
    )(*weights)


def local_kernel(places, feat_ref, *refs):
    pieces = refs[: len(places)]
    table, sems = refs[-2:]
    pairs = []
    for place, piece in zip(places, pieces):
        start = pl.multiple_of(place(feat_ref[0]), 16)
        pairs.append((piece, table.at[pl.ds(start, piece.shape[0])]))
    wait_all(run_copies(pairs, sems))


def local_call(feat, places, pieces, table):
    return pl.pallas_call(
        functools.partial(local_kernel, places),
        grid_spec=pltpu.PrefetchScalarGridSpec(
            num_scalar_prefetch=1,
            in_specs=[pl.BlockSpec(memory_space=pl.ANY)] * len(pieces) + [IN_VMEM],
            out_specs=IN_VMEM,
            scratch_shapes=[pltpu.SemaphoreType.DMA((len(pieces),))],
        ),
        out_shape=pltpu.VMEM(table.shape, BF16),
        input_output_aliases={len(pieces) + 1: 0},
        compiler_params=params(4),
        cost_estimate=SMALL,
        name="local_messages",
    )(feat, *pieces, table)


def aggregate_kernel(places, start, feat_ref, links, *refs):
    fine, coarse_tile, coarse, degree = refs[:4]
    pieces = refs[4 : 4 + len(places)]
    if places:
        send, keep, first_rows, table, sems = refs[5 + len(places) :]
        pairs = []
        for place, piece in zip(places, pieces):
            at = pl.multiple_of(place(feat_ref[0]), 16)
            pairs.append((piece, table.at[pl.ds(at, piece.shape[0])]))
        copies = run_copies(pairs, sems)
    else:
        table, send, keep = refs[4:]
        copies = []
    blocks, block, fine_width = fine.shape
    kinds = fine_width // block
    count = send.shape[0] // block
    feat = feat_ref[0]
    wait_all(copies)
    for out_ref, which in ((send, 1 - feat), (keep, feat)):
        scale = 1.0 / jnp.transpose(degree[which].astype(F32))
        first = which * (blocks // 2) + start
        for pos in range(count):
            row = (first + pos) * kinds
            chosen = jnp.concatenate(
                [table[pl.ds(pl.multiple_of(links[row + kind], block), block), :] for kind in range(kinds)], axis=0
            )
            base = blocks * kinds + row
            stacked = jnp.concatenate(
                [
                    coarse[pl.ds(pl.multiple_of(links[base + kind], 8), CN_DEV), :]
                    for kind in range(kinds)
                ],
                axis=0,
            ).astype(BF16)
            summed = dot(fine[first + pos], chosen) + dot(coarse_tile[first + pos], stacked)
            result = (summed * scale[:, start + pos : start + pos + 1]).astype(BF16)
            out_ref[pos * block : (pos + 1) * block, :] = result
    if places:

        @pl.when(feat == 0)
        def _():
            first_rows[...] = keep[:CN_DEV, :]

        @pl.when(feat != 0)
        def _():
            first_rows[...] = send[:CN_DEV, :]


def aggregate_call(feat, links, staged, coarse, degree, table, span, places=(), pieces=()):
    fine, coarse_tile = staged
    blocks, block, _ = fine.shape
    columns = table.shape[1]
    start, count = span
    out_shape = [pltpu.VMEM((count * block, columns), BF16)] * 2
    aliases = {}
    scratch = []
    if pieces:
        out_shape += [pltpu.VMEM((CN_DEV, columns), BF16), pltpu.VMEM(table.shape, BF16)]
        aliases = {6 + len(pieces): 3}
        scratch = [pltpu.SemaphoreType.DMA((len(pieces),))]
    return pl.pallas_call(
        functools.partial(aggregate_kernel, places, start),
        grid_spec=pltpu.PrefetchScalarGridSpec(
            num_scalar_prefetch=2,
            in_specs=[IN_VMEM] * 4 + [IN_HBM] * len(pieces) + [IN_VMEM],
            out_specs=[IN_VMEM] * len(out_shape),
            scratch_shapes=scratch,
        ),
        out_shape=out_shape,
        input_output_aliases=aliases,
        compiler_params=params(12),
        cost_estimate=SMALL,
        name="aggregate",
    )(feat, links, fine, coarse_tile, coarse, degree, *pieces, table)


def node_kernel(mode, layer, start, offset, rows, placed, feat_ref, *refs):
    state_ref, keep, recv, in_own, in_other, out_own, out_other = refs[:7]
    refs = refs[7:]
    feat = feat_ref[0]
    columns = keep.shape[1]
    width = state_ref.shape[1]
    if mode == "last":
        state_out, out, sems = refs[-3:]
        half_rows = out.shape[0] // 2
        pairs = []
        for place, piece in zip(placed, refs):
            at = pl.multiple_of((1 - feat) * half_rows + place, 16)
            pairs.append((piece, out.at[pl.ds(at, piece.shape[0])]))
        copies = run_copies(pairs, sems)
    keep_at = pl.multiple_of(width + feat * columns, columns)
    recv_at = pl.multiple_of(width + (1 - feat) * columns, columns)
    split = NODE_SPLIT if rows % (NODE_SPLIT * 640) == 0 else 1
    size = rows // split
    joined, hidden, state = {}, {}, {}

    def join(at):
        joined[at] = normalize(
            [state_ref[start + at : start + at + size, :].astype(F32)]
            + [ref[offset + at : offset + at + size, :].astype(F32) for ref in (keep, recv)]
        )

    def hide(at):
        parts = joined[at]
        hidden[at] = [
            silu(
                dot(parts[0], in_ref[layer, :width, :])
                + dot(parts[1], in_ref[layer, pl.ds(keep_at, columns), :])
                + dot(parts[2], in_ref[layer, pl.ds(recv_at, columns), :])
            ).astype(BF16)
            for in_ref in (in_own, in_other)
        ]

    def update(at):
        change = dot(hidden[at][0], out_own[layer]) + dot(hidden[at][1], out_other[layer])
        state[at] = (state_ref[start + at : start + at + size, :].astype(F32) + change).astype(BF16)
        if mode == "last":
            state_out[at : at + size, :] = state[at]
        elif mode == "mid":
            refs[2][start + at : start + at + size, :] = state[at]

    def norm(at):
        (joined[at],) = normalize([state[at].astype(F32)])

    def tell(at):
        if mode == "coarse":
            refs[1][...] = silu(dot(joined[at], refs[0][layer + 1])).astype(BF16).astype(F32)
            return
        for weight, message in ((refs[0], refs[3]), (refs[1], refs[4])):
            message[at : at + size, :] = silu(dot(joined[at], weight[layer + 1])).astype(BF16)

    stages = [join, hide, update] + ([] if mode == "last" else [norm, tell])
    for step in range(len(stages) + split - 1):
        for pos in range(split):
            if 0 <= step - pos < len(stages):
                stages[step - pos](pos * size)
    if mode == "last":
        at = pl.multiple_of(feat * half_rows + start, 16)
        copy = pltpu.make_async_copy(state_out, out.at[pl.ds(at, rows)], sems.at[len(placed)])
        copy.start()
        wait_all(copies)
        copy.wait()


def node_call(mode, layer, feat, state, start, offset, rows, keep, recv, weights, out=None, total=0, placed=(), pieces=()):
    columns = keep.shape[1]
    width = state.shape[1]
    operands = [state, keep, recv, *weights[:4]]
    aliases = {}
    scratch = []
    in_specs = [IN_VMEM] * len(operands)
    if mode == "last":
        out_shape = [pltpu.VMEM((rows, width), BF16), jax.ShapeDtypeStruct((total, width), BF16)]
        out_specs = [IN_VMEM, pl.BlockSpec(memory_space=pl.ANY)]
        scratch = [pltpu.SemaphoreType.DMA((1 + len(pieces),))]
        operands += pieces
        in_specs += [IN_VMEM] * len(pieces)
        if out is not None:
            aliases = {len(operands) + 1: 1}
            operands.append(out)
            in_specs.append(pl.BlockSpec(memory_space=pl.ANY))
    else:
        if mode == "coarse":
            operands.append(weights[4])
            out_shape = [pltpu.VMEM((rows, columns), F32)]
        else:
            operands += weights[4:]
            out_shape = [pltpu.VMEM(state.shape, BF16)] + [pltpu.VMEM((rows, columns), BF16)] * 2
            aliases = {1: 0}
        in_specs = [IN_VMEM] * len(operands)
        out_specs = [IN_VMEM] * len(out_shape)
    return pl.pallas_call(
        functools.partial(node_kernel, mode, layer, start, offset, rows, placed),
        grid_spec=pltpu.PrefetchScalarGridSpec(
            num_scalar_prefetch=1, in_specs=in_specs, out_specs=out_specs, scratch_shapes=scratch
        ),
        out_shape=out_shape,
        input_output_aliases=aliases,
        compiler_params=params(28),
        cost_estimate=LONG if mode == "last" else SMALL,
        name="node_" + mode,
    )(feat, *operands)


def assemble_kernel(placed, feat_ref, *refs):
    pieces = refs[: len(placed)]
    out, sems = refs[-2:]
    half_rows = out.shape[0] // 2
    pairs = []
    for place, piece in zip(placed, pieces):
        at = pl.multiple_of((1 - feat_ref[0]) * half_rows + place, 16)
        pairs.append((piece, out.at[pl.ds(at, piece.shape[0])]))
    wait_all(run_copies(pairs, sems))


def assemble_call(feat, placed, pieces, out):
    return pl.pallas_call(
        functools.partial(assemble_kernel, placed),
        grid_spec=pltpu.PrefetchScalarGridSpec(
            num_scalar_prefetch=1,
            in_specs=[IN_VMEM] * len(pieces) + [pl.BlockSpec(memory_space=pl.ANY)],
            out_specs=pl.BlockSpec(memory_space=pl.ANY),
            scratch_shapes=[pltpu.SemaphoreType.DMA((len(pieces),))],
        ),
        out_shape=shaped(out),
        input_output_aliases={len(pieces) + 1: 0},
        compiler_params=params(4),
        cost_estimate=SMALL,
        name="assemble",
    )(feat, *pieces, out)


def swap_feat(array):
    return lax.ppermute(array, "feat", [(0, 1), (1, 0)])


def fetch(held, stride):
    count = lax.axis_size("patch")
    return lax.ppermute(held, "patch", [(pos, (pos - stride) % count) for pos in range(count)])


def even_offsets(count):
    assert count & (count - 1) == 0
    offsets = [0]
    stride = count // 2
    while stride > 1:
        offsets += [offset + stride for offset in offsets]
        stride //= 2
    return offsets


def shards(
    node_state, fine_tile, coarse_tile, fine_index, coarse_index, node_degree, w_msg, w_in, w_out
):
    barrier = lax.optimization_barrier
    patches = lax.axis_size("patch")
    patch_pos = lax.axis_index("patch")
    feat_pos = lax.axis_index("feat")
    feat = feat_pos.astype(jnp.int32).reshape(1)
    blocks, kinds, block, _ = fine_tile.shape
    half = blocks // 2
    half_rows = half * block
    halo_rows = HALO_BLK * block
    assert half == HALO_BLK == sum(MID_BLOCKS) == sum(LAST_BLOCKS)

    forward = [(pos, pos + 1) for pos in range(patches - 1)]
    backward = [(target, source) for source, target in forward]
    sides = ((0, backward), (1, forward))
    own_patch = [(2 * src + side, 2 * dst + side) for side, pairs in sides for src, dst in pairs]
    other_patch = [(2 * src + side, 2 * dst + 1 - side) for side, pairs in sides for src, dst in pairs]
    evens = even_offsets(patches)

    held = node_state[:CN_DEV]
    held = jnp.concatenate([held, fetch(held, 1)], axis=0)
    sends = []
    halo = []
    for first, count in MESSAGE_ROWS:
        message = message_call(node_state, w_msg, first * block, count * block, MESSAGE_TILE)
        if not sends:
            message, held = barrier((message, held))
        sends.append(message)
        halo.append(lax.ppermute(message, "patch", backward if first < half else forward))
    high = sends[-1]

    offsets = [even + odd for even in evens for odd in (0, 1)]
    fine_index, coarse_index, node_degree, w_in, w_out, w_late, _ = barrier(
        (fine_index, coarse_index, node_degree, w_in, w_out, w_msg, high)
    )
    links = (fine_index - (patch_pos * blocks - HALO_BLK)).reshape(-1) * block
    away = ((coarse_index - patch_pos) % patches).reshape(-1)
    coarse_links = sum(jnp.where(away == offset, pos * CN_DEV, 0) for pos, offset in enumerate(offsets))
    links = jnp.concatenate([links, coarse_links])
    degree = node_degree.reshape(2, half, block)
    fine, ctile, state, table, in_own, out_own, msg_own = stage_call(
        feat, fine_tile, jnp.swapaxes(coarse_tile, 1, 2), node_state, sends, (w_in, w_out, w_late)
    )
    staged = (fine, ctile)
    others = weights_call([swap_feat(w_in), swap_feat(w_out), swap_feat(w_late)])
    strides = [patches >> step for step in range(1, patches.bit_length() - 1)]
    for step, stride in enumerate(strides):
        got = fetch(held, stride)
        if step == 0:
            got, links, degree, table = barrier((got, links, degree, table))
        if step == len(strides) - 1:
            got, others = barrier((got, others))
        held = jnp.concatenate([held, got], axis=0)
    coarse_state = held
    weights = [in_own, others[0], out_own, others[1], msg_own, others[2]]
    coarse = coarse_message_call(coarse_state, msg_own)

    halo_places = [
        lambda feat, at=first * block: halo_rows + 2 * half_rows + at if at < half_rows else at - half_rows
        for first, _ in MESSAGE_ROWS
    ]
    first_span, last_span = (0, MID_BLOCKS[0]), MID_BLOCKS
    send, keep, first_rows, table = aggregate_call(
        feat, links, staged, coarse, degree, table, first_span, halo_places, halo
    )
    recv = swap_feat(send)
    got = fetch(first_rows, 1)
    send_1, keep_1 = aggregate_call(feat, links, staged, coarse, degree, table, last_span)
    recv, keep, send_1 = barrier((recv, keep, send_1))
    inputs = [(keep, recv), (keep_1, swap_feat(send_1))]
    local = []
    local_places = []
    halo = []
    halo_places = []
    at = 0
    for chunk, count in enumerate(MID_BLOCKS):
        rows = count * block
        state, own, other = node_call("mid", 0, feat, state, at, 0, rows, *inputs[chunk], weights)
        if chunk == 0:
            own, other, got = barrier((own, other, got))
        sibling = swap_feat(other)
        if chunk == 0:
            sibling, state = barrier((sibling, state))
        halo += [lax.ppermute(own, ("patch", "feat"), own_patch), lax.ppermute(other, ("patch", "feat"), other_patch)]
        local += [own, sibling]
        local_places += [
            lambda feat, at=at: halo_rows + feat * half_rows + at,
            lambda feat, at=at: halo_rows + (1 - feat) * half_rows + at,
        ]
        halo_places += [
            lambda feat, at=at: (1 - feat) * (halo_rows + 2 * half_rows) + at,
            lambda feat, at=at: feat * (halo_rows + 2 * half_rows) + at,
        ]
        at += rows

    early = len(halo) - 2
    table = local_call(feat, local_places + halo_places[:early], local + halo[:early], table)
    held = jnp.concatenate([first_rows, got], axis=0)
    held, table = barrier((held, table))
    held = jnp.concatenate([held] + [fetch(held, offset) for offset in evens[1:]], axis=0)
    (coarse,) = node_call(
        "coarse", 0, feat, coarse_state, 0, 0, held.shape[0], held, swap_feat(held), weights
    )
    send, keep, _, table = aggregate_call(
        feat, links, staged, coarse, degree, table, (0, LAST_BLOCKS[0]), halo_places[early:], halo[early:]
    )
    recv = swap_feat(send)
    send_1, keep_1 = aggregate_call(feat, links, staged, coarse, degree, table, LAST_BLOCKS)
    recv, keep, send_1 = barrier((recv, keep, send_1))
    inputs = [(keep, recv), (keep_1, swap_feat(send_1))]
    out = None
    swapped = []
    placed = []
    for chunk, offset, count in LAST_ROWS:
        at = (chunk * LAST_BLOCKS[0] + offset) * block
        done = 1 if len(swapped) == len(LAST_ROWS) - 1 else 0
        new_state, out = node_call(
            "last", 1, feat, state, at, offset * block, count * block, *inputs[chunk], weights,
            out, node_state.shape[0], placed[:done], swapped[:done],
        )
        swapped.append(swap_feat(new_state))
        placed.append(at)
    return assemble_call(feat, placed[1:], swapped[1:], out)


def solution(mesh):
    return jax.shard_map(
        shards,
        mesh=mesh,
        in_specs=(
            P(("member", "patch"), None),
            P("patch", None, None, None),
            P("patch", None, None),
            P("patch", None),
            P("patch", None),
            P("patch"),
            P(None, None, "feat"),
            P(None, None, "feat"),
            P(None, "feat", None),
        ),
        out_specs=P(("member", "patch"), None),
        check_vma=False,
    )
```

```python
import functools

import jax
import jax.numpy as jnp
from jax import lax
from jax.experimental import pallas as pl
from jax.experimental.pallas import tpu as pltpu
from jax.sharding import PartitionSpec as P

CN_DEV = 40
LAYERS = 2
HALO_BLK = 20
MID_BLOCKS = (10, 10)
LAST_BLOCKS = (10, 10)
LAST_ROWS = ((0, 0, 10), (1, 0, 5), (1, 5, 5))
MESSAGE_ROWS = ((0, 20), (20, 20))
MESSAGE_TILE = 640
NODE_SPLIT = 2
F32 = jnp.float32
BF16 = jnp.bfloat16
LONG = pl.CostEstimate(flops=1 << 33, transcendentals=0, bytes_accessed=1 << 10)
SMALL = pl.CostEstimate(flops=1 << 20, transcendentals=0, bytes_accessed=1 << 10)
IN_VMEM = pl.BlockSpec(memory_space=pltpu.VMEM)
IN_HBM = pl.BlockSpec(memory_space=pltpu.HBM)


def silu(v):
    return 0.5 * v * (1.0 + jnp.tanh(0.5 * v))


def dot(a, b):
    return jnp.dot(a, b, preferred_element_type=F32)


def normalize(parts):
    width = sum(part.shape[-1] for part in parts)
    mean = sum(jnp.sum(part, axis=-1, keepdims=True) for part in parts) / width
    center = [part - mean for part in parts]
    spread = sum(jnp.sum(part * part, axis=-1, keepdims=True) for part in center) / width
    scale = lax.rsqrt(spread + 1e-05)
    return [(part * scale).astype(BF16) for part in center]


def params(mib):
    return pltpu.CompilerParams(vmem_limit_bytes=mib << 20)


def shaped(array):
    return jax.ShapeDtypeStruct(array.shape, array.dtype)


def run_copies(pairs, sems):
    copies = [pltpu.make_async_copy(src, dst, sems.at[pos]) for pos, (src, dst) in enumerate(pairs)]
    for copy in copies:
        copy.start()
    return copies


def wait_all(copies):
    for copy in copies:
        copy.wait()


def coarse_message_kernel(state_ref, weight_ref, out_ref):
    (normed,) = normalize([state_ref[...].astype(F32)])
    out_ref[...] = silu(dot(normed, weight_ref[0])).astype(BF16).astype(F32)


def message_kernel(start, tile, state, weight, out, state_buf, weight_buf, out_ref, sems):
    rows = out_ref.shape[0]
    tiles = [(at, tile) for at in range(0, rows, tile)]
    pairs = [(state.at[pl.ds(start + at, size)], state_buf.at[pl.ds(at, size)]) for at, size in tiles]
    copies = run_copies(pairs[:1] + [(weight.at[0], weight_buf)] + pairs[1:], sems)
    weight_copy = copies.pop(1)
    normed = []
    for pos in range(len(tiles) + 1):
        if pos < len(tiles):
            at, size = tiles[pos]
            copies[pos].wait()
            normed += normalize([state_buf[at : at + size, :].astype(F32)])
        if pos == 0:
            weight_copy.wait()
            continue
        at, size = tiles[pos - 1]
        out_ref[at : at + size, :] = silu(dot(normed[pos - 1], weight_buf[...])).astype(BF16)
        span = pl.ds(at, size)
        copy = pltpu.make_async_copy(out_ref.at[span], out.at[span], sems.at[len(tiles) + pos])
        copy.start()
        copies.append(copy)
    wait_all(copies[len(tiles) :])


def message_call(state, weight, start, rows, tile):
    width, columns = weight.shape[1:]
    return pl.pallas_call(
        functools.partial(message_kernel, start, tile),
        in_specs=[IN_HBM, IN_HBM],
        out_specs=IN_HBM,
        out_shape=jax.ShapeDtypeStruct((rows, columns), BF16),
        scratch_shapes=[
            pltpu.VMEM((rows, width), BF16),
            pltpu.VMEM((width, columns), BF16),
            pltpu.VMEM((rows, columns), BF16),
            pltpu.SemaphoreType.DMA((1 + 2 * (rows // tile),)),
        ],
        compiler_params=params(56),
        cost_estimate=SMALL,
        name="message",
    )(state, weight)


def coarse_message_call(state, weight):
    return pl.pallas_call(
        coarse_message_kernel,
        in_specs=[IN_VMEM, IN_VMEM],
        out_specs=IN_VMEM,
        out_shape=pltpu.VMEM((state.shape[0], weight.shape[2]), F32),
        compiler_params=params(12),
        cost_estimate=SMALL,
        name="coarse_message",
    )(state, weight)


def stage_kernel(locals_, count, feat_ref, *refs):
    fine, coarse, state = refs[:3]
    pieces = refs[3 : 3 + locals_]
    refs = refs[3 + locals_ :]
    weights = refs[:count]
    fine_out, coarse_out, state_out, table = refs[count : 4 + count]
    weights_out = refs[4 + count : 4 + 2 * count]
    coarse_buf, sems = refs[4 + 2 * count :]
    block = fine.shape[-1]
    half_rows = state_out.shape[0]
    pairs = [(coarse, coarse_buf)]
    pairs += [
        (fine.at[:, kind], fine_out.at[:, :, pl.ds(kind * block, block)]) for kind in range(fine.shape[1])
    ]
    start = pl.multiple_of(feat_ref[0] * half_rows, 16)
    pairs.append((state.at[pl.ds(start, half_rows)], state_out))
    at = HALO_BLK * block
    for piece in pieces:
        pairs.append((piece, table.at[pl.ds(at, piece.shape[0])]))
        at += piece.shape[0]
    pairs += list(zip(weights, weights_out))
    copies = run_copies(pairs, sems)
    copies[0].wait()

    def turn(pos, carry):
        coarse_out[pos] = jnp.transpose(coarse_buf[pos])
        return carry

    lax.fori_loop(0, coarse.shape[0], turn, 0)
    wait_all(copies[1:])


def stage_call(feat, fine, coarse, state, pieces, weights):
    blocks, kinds, block, _ = fine.shape
    rows, columns = blocks // 2 * block, pieces[0].shape[1]
    out_shape = [
        pltpu.VMEM((blocks, block, kinds * block), BF16),
        pltpu.VMEM((blocks, block, coarse.shape[1]), BF16),
        pltpu.VMEM((rows, state.shape[1]), BF16),
        pltpu.VMEM((2 * rows + 2 * HALO_BLK * block, columns), BF16),
    ] + [pltpu.VMEM(weight.shape, BF16) for weight in weights]
    copies = 2 + kinds + len(pieces) + len(weights)
    return pl.pallas_call(
        functools.partial(stage_kernel, len(pieces), len(weights)),
        grid_spec=pltpu.PrefetchScalarGridSpec(
            num_scalar_prefetch=1,
            in_specs=[IN_HBM] * (3 + len(pieces) + len(weights)),
            out_specs=[IN_VMEM] * len(out_shape),
            scratch_shapes=[pltpu.VMEM(coarse.shape, BF16), pltpu.SemaphoreType.DMA((copies,))],
        ),
        out_shape=out_shape,
        compiler_params=params(36),
        cost_estimate=SMALL,
        name="stage",
    )(feat, fine, coarse, state, *pieces, *weights)


def weights_kernel(*refs):
    sems = refs[-1]
    count = len(refs) // 2
    wait_all(run_copies(list(zip(refs[:count], refs[count:-1])), sems))


def weights_call(weights):
    return pl.pallas_call(
        weights_kernel,
        in_specs=[IN_HBM] * len(weights),
        out_specs=[IN_VMEM] * len(weights),
        scratch_shapes=[pltpu.SemaphoreType.DMA((len(weights),))],
        out_shape=[pltpu.VMEM(weight.shape, BF16) for weight in weights],
        compiler_params=params(4),
        cost_estimate=SMALL,
        name="weights",
    )(*weights)


def local_kernel(places, feat_ref, *refs):
    pieces = refs[: len(places)]
    table, sems = refs[-2:]
    pairs = []
    for place, piece in zip(places, pieces):
        start = pl.multiple_of(place(feat_ref[0]), 16)
        pairs.append((piece, table.at[pl.ds(start, piece.shape[0])]))
    wait_all(run_copies(pairs, sems))


def local_call(feat, places, pieces, table):
    return pl.pallas_call(
        functools.partial(local_kernel, places),
        grid_spec=pltpu.PrefetchScalarGridSpec(
            num_scalar_prefetch=1,
            in_specs=[pl.BlockSpec(memory_space=pl.ANY)] * len(pieces) + [IN_VMEM],
            out_specs=IN_VMEM,
            scratch_shapes=[pltpu.SemaphoreType.DMA((len(pieces),))],
        ),
        out_shape=pltpu.VMEM(table.shape, BF16),
        input_output_aliases={len(pieces) + 1: 0},
        compiler_params=params(4),
        cost_estimate=SMALL,
        name="local_messages",
    )(feat, *pieces, table)


def aggregate_kernel(places, start, feat_ref, links, *refs):
    fine, coarse_tile, coarse, degree = refs[:4]
    pieces = refs[4 : 4 + len(places)]
    if places:
        send, keep, first_rows, table, sems = refs[5 + len(places) :]
        pairs = []
        for place, piece in zip(places, pieces):
            at = pl.multiple_of(place(feat_ref[0]), 16)
            pairs.append((piece, table.at[pl.ds(at, piece.shape[0])]))
        copies = run_copies(pairs, sems)
    else:
        table, send, keep = refs[4:]
        copies = []
    blocks, block, fine_width = fine.shape
    kinds = fine_width // block
    count = send.shape[0] // block
    feat = feat_ref[0]
    wait_all(copies)
    for out_ref, which in ((send, 1 - feat), (keep, feat)):
        scale = 1.0 / jnp.transpose(degree[which].astype(F32))
        first = which * (blocks // 2) + start
        for pos in range(count):
            row = (first + pos) * kinds
            chosen = jnp.concatenate(
                [table[pl.ds(pl.multiple_of(links[row + kind], block), block), :] for kind in range(kinds)], axis=0
            )
            base = blocks * kinds + row
            stacked = jnp.concatenate(
                [
                    coarse[pl.ds(pl.multiple_of(links[base + kind], 8), CN_DEV), :]
                    for kind in range(kinds)
                ],
                axis=0,
            ).astype(BF16)
            summed = dot(fine[first + pos], chosen) + dot(coarse_tile[first + pos], stacked)
            result = (summed * scale[:, start + pos : start + pos + 1]).astype(BF16)
            out_ref[pos * block : (pos + 1) * block, :] = result
    if places:

        @pl.when(feat == 0)
        def _():
            first_rows[...] = keep[:CN_DEV, :]

        @pl.when(feat != 0)
        def _():
            first_rows[...] = send[:CN_DEV, :]


def aggregate_call(feat, links, staged, coarse, degree, table, span, places=(), pieces=()):
    fine, coarse_tile = staged
    blocks, block, _ = fine.shape
    columns = table.shape[1]
    start, count = span
    out_shape = [pltpu.VMEM((count * block, columns), BF16)] * 2
    aliases = {}
    scratch = []
    if pieces:
        out_shape += [pltpu.VMEM((CN_DEV, columns), BF16), pltpu.VMEM(table.shape, BF16)]
        aliases = {6 + len(pieces): 3}
        scratch = [pltpu.SemaphoreType.DMA((len(pieces),))]
    return pl.pallas_call(
        functools.partial(aggregate_kernel, places, start),
        grid_spec=pltpu.PrefetchScalarGridSpec(
            num_scalar_prefetch=2,
            in_specs=[IN_VMEM] * 4 + [IN_HBM] * len(pieces) + [IN_VMEM],
            out_specs=[IN_VMEM] * len(out_shape),
            scratch_shapes=scratch,
        ),
        out_shape=out_shape,
        input_output_aliases=aliases,
        compiler_params=params(12),
        cost_estimate=SMALL,
        name="aggregate",
    )(feat, links, fine, coarse_tile, coarse, degree, *pieces, table)


def node_kernel(mode, layer, start, offset, rows, placed, feat_ref, *refs):
    state_ref, keep, recv, in_own, in_other, out_own, out_other = refs[:7]
    refs = refs[7:]
    feat = feat_ref[0]
    columns = in_own.shape[2]
    width = state_ref.shape[1]
    sides = ((keep, 0), (recv, columns if mode == "coarse" else 0))
    if mode == "last":
        state_out, out, sems = refs[-3:]
        half_rows = out.shape[0] // 2
        pairs = []
        for place, piece in zip(placed, refs):
            at = pl.multiple_of((1 - feat) * half_rows + place, 16)
            pairs.append((piece, out.at[pl.ds(at, piece.shape[0])]))
        copies = run_copies(pairs, sems)
    keep_at = pl.multiple_of(width + feat * columns, columns)
    recv_at = pl.multiple_of(width + (1 - feat) * columns, columns)
    split = NODE_SPLIT if rows % (NODE_SPLIT * 640) == 0 else 1
    size = rows // split
    joined, hidden, state = {}, {}, {}

    def join(at):
        joined[at] = normalize(
            [state_ref[start + at : start + at + size, :].astype(F32)]
            + [ref[offset + at : offset + at + size, col : col + columns].astype(F32) for ref, col in sides]
        )

    def hide(at):
        parts = joined[at]
        hidden[at] = [
            silu(
                dot(parts[0], in_ref[layer, :width, :])
                + dot(parts[1], in_ref[layer, pl.ds(keep_at, columns), :])
                + dot(parts[2], in_ref[layer, pl.ds(recv_at, columns), :])
            ).astype(BF16)
            for in_ref in (in_own, in_other)
        ]

    def update(at):
        change = dot(hidden[at][0], out_own[layer]) + dot(hidden[at][1], out_other[layer])
        state[at] = (state_ref[start + at : start + at + size, :].astype(F32) + change).astype(BF16)
        if mode == "last":
            state_out[at : at + size, :] = state[at]
        elif mode == "mid":
            refs[2][start + at : start + at + size, :] = state[at]

    def norm(at):
        (joined[at],) = normalize([state[at].astype(F32)])

    def tell(at):
        if mode == "coarse":
            refs[1][...] = silu(dot(joined[at], refs[0][layer + 1])).astype(BF16).astype(F32)
            return
        for weight, message in ((refs[0], refs[3]), (refs[1], refs[4])):
            message[at : at + size, :] = silu(dot(joined[at], weight[layer + 1])).astype(BF16)

    stages = [join, hide, update] + ([] if mode == "last" else [norm, tell])
    for step in range(len(stages) + split - 1):
        for pos in range(split):
            if 0 <= step - pos < len(stages):
                stages[step - pos](pos * size)
    if mode == "last":
        at = pl.multiple_of(feat * half_rows + start, 16)
        copy = pltpu.make_async_copy(state_out, out.at[pl.ds(at, rows)], sems.at[len(placed)])
        copy.start()
        wait_all(copies)
        copy.wait()


def node_call(mode, layer, feat, state, start, offset, rows, keep, recv, weights, out=None, total=0, placed=(), pieces=()):
    columns = weights[0].shape[2]
    width = state.shape[1]
    operands = [state, keep, recv, *weights[:4]]
    aliases = {}
    scratch = []
    in_specs = [IN_VMEM] * len(operands)
    if mode == "last":
        out_shape = [pltpu.VMEM((rows, width), BF16), jax.ShapeDtypeStruct((total, width), BF16)]
        out_specs = [IN_VMEM, pl.BlockSpec(memory_space=pl.ANY)]
        scratch = [pltpu.SemaphoreType.DMA((1 + len(pieces),))]
        operands += pieces
        in_specs += [IN_VMEM] * len(pieces)
        if out is not None:
            aliases = {len(operands) + 1: 1}
            operands.append(out)
            in_specs.append(pl.BlockSpec(memory_space=pl.ANY))
    else:
        if mode == "coarse":
            operands.append(weights[4])
            out_shape = [pltpu.VMEM((rows, columns), F32)]
        else:
            operands += weights[4:]
            out_shape = [pltpu.VMEM(state.shape, BF16)] + [pltpu.VMEM((rows, columns), BF16)] * 2
            aliases = {1: 0}
        in_specs = [IN_VMEM] * len(operands)
        out_specs = [IN_VMEM] * len(out_shape)
    return pl.pallas_call(
        functools.partial(node_kernel, mode, layer, start, offset, rows, placed),
        grid_spec=pltpu.PrefetchScalarGridSpec(
            num_scalar_prefetch=1, in_specs=in_specs, out_specs=out_specs, scratch_shapes=scratch
        ),
        out_shape=out_shape,
        input_output_aliases=aliases,
        compiler_params=params(28),
        cost_estimate=LONG if mode == "last" else SMALL,
        name="node_" + mode,
    )(feat, *operands)


def assemble_kernel(placed, feat_ref, *refs):
    pieces = refs[: len(placed)]
    out, sems = refs[-2:]
    half_rows = out.shape[0] // 2
    pairs = []
    for place, piece in zip(placed, pieces):
        at = pl.multiple_of((1 - feat_ref[0]) * half_rows + place, 16)
        pairs.append((piece, out.at[pl.ds(at, piece.shape[0])]))
    wait_all(run_copies(pairs, sems))


def assemble_call(feat, placed, pieces, out):
    return pl.pallas_call(
        functools.partial(assemble_kernel, placed),
        grid_spec=pltpu.PrefetchScalarGridSpec(
            num_scalar_prefetch=1,
            in_specs=[IN_VMEM] * len(pieces) + [pl.BlockSpec(memory_space=pl.ANY)],
            out_specs=pl.BlockSpec(memory_space=pl.ANY),
            scratch_shapes=[pltpu.SemaphoreType.DMA((len(pieces),))],
        ),
        out_shape=shaped(out),
        input_output_aliases={len(pieces) + 1: 0},
        compiler_params=params(4),
        cost_estimate=SMALL,
        name="assemble",
    )(feat, *pieces, out)


def swap_feat(array):
    return lax.ppermute(array, "feat", [(0, 1), (1, 0)])


def fetch(held, stride):
    count = lax.axis_size("patch")
    return lax.ppermute(held, "patch", [(pos, (pos - stride) % count) for pos in range(count)])


def even_offsets(count):
    assert count & (count - 1) == 0
    offsets = [0]
    stride = count // 2
    while stride > 1:
        offsets += [offset + stride for offset in offsets]
        stride //= 2
    return offsets


def shards(
    node_state, fine_tile, coarse_tile, fine_index, coarse_index, node_degree, w_msg, w_in, w_out
):
    barrier = lax.optimization_barrier
    patches = lax.axis_size("patch")
    patch_pos = lax.axis_index("patch")
    feat_pos = lax.axis_index("feat")
    feat = feat_pos.astype(jnp.int32).reshape(1)
    blocks, kinds, block, _ = fine_tile.shape
    half = blocks // 2
    half_rows = half * block
    halo_rows = HALO_BLK * block
    assert half == HALO_BLK == sum(MID_BLOCKS) == sum(LAST_BLOCKS)

    forward = [(pos, pos + 1) for pos in range(patches - 1)]
    backward = [(target, source) for source, target in forward]
    sides = ((0, backward), (1, forward))
    own_patch = [(2 * src + side, 2 * dst + side) for side, pairs in sides for src, dst in pairs]
    other_patch = [(2 * src + side, 2 * dst + 1 - side) for side, pairs in sides for src, dst in pairs]
    evens = even_offsets(patches)

    held = node_state[:CN_DEV]
    held = jnp.concatenate([held, fetch(held, 1)], axis=0)
    sends = []
    halo = []
    for first, count in MESSAGE_ROWS:
        message = message_call(node_state, w_msg, first * block, count * block, MESSAGE_TILE)
        if not sends:
            message, held = barrier((message, held))
        sends.append(message)
        halo.append(lax.ppermute(message, "patch", backward if first < half else forward))
    high = sends[-1]

    offsets = [even + odd for even in evens for odd in (0, 1)]
    fine_index, coarse_index, node_degree, w_in, w_out, w_late, _ = barrier(
        (fine_index, coarse_index, node_degree, w_in, w_out, w_msg, high)
    )
    links = (fine_index - (patch_pos * blocks - HALO_BLK)).reshape(-1) * block
    away = ((coarse_index - patch_pos) % patches).reshape(-1)
    coarse_links = sum(jnp.where(away == offset, pos * CN_DEV, 0) for pos, offset in enumerate(offsets))
    links = jnp.concatenate([links, coarse_links])
    degree = node_degree.reshape(2, half, block)
    fine, ctile, state, table, in_own, out_own, msg_own = stage_call(
        feat, fine_tile, jnp.swapaxes(coarse_tile, 1, 2), node_state, sends, (w_in, w_out, w_late)
    )
    staged = (fine, ctile)
    others = weights_call([swap_feat(w_in), swap_feat(w_out), swap_feat(w_late)])
    strides = [patches >> step for step in range(1, patches.bit_length() - 1)]
    for step, stride in enumerate(strides):
        got = fetch(held, stride)
        if step == 0:
            got, links, degree, table = barrier((got, links, degree, table))
        if step == len(strides) - 1:
            got, others = barrier((got, others))
        held = jnp.concatenate([held, got], axis=0)
    coarse_state = held
    weights = [in_own, others[0], out_own, others[1], msg_own, others[2]]
    coarse = coarse_message_call(coarse_state, msg_own)

    halo_places = [
        lambda feat, at=first * block: halo_rows + 2 * half_rows + at if at < half_rows else at - half_rows
        for first, _ in MESSAGE_ROWS
    ]
    first_span, last_span = (0, MID_BLOCKS[0]), MID_BLOCKS
    send, keep, first_rows, table = aggregate_call(
        feat, links, staged, coarse, degree, table, first_span, halo_places, halo
    )
    recv = swap_feat(send)
    got = fetch(first_rows, 1)
    send_1, keep_1 = aggregate_call(feat, links, staged, coarse, degree, table, last_span)
    recv, keep, send_1 = barrier((recv, keep, send_1))
    inputs = [(keep, recv), (keep_1, swap_feat(send_1))]
    local = []
    local_places = []
    halo = []
    halo_places = []
    at = 0
    for chunk, count in enumerate(MID_BLOCKS):
        rows = count * block
        state, own, other = node_call("mid", 0, feat, state, at, 0, rows, *inputs[chunk], weights)
        if chunk == 0:
            own, other, got = barrier((own, other, got))
        sibling = swap_feat(other)
        if chunk == 0:
            sibling, state = barrier((sibling, state))
        halo += [lax.ppermute(own, ("patch", "feat"), own_patch), lax.ppermute(other, ("patch", "feat"), other_patch)]
        local += [own, sibling]
        local_places += [
            lambda feat, at=at: halo_rows + feat * half_rows + at,
            lambda feat, at=at: halo_rows + (1 - feat) * half_rows + at,
        ]
        halo_places += [
            lambda feat, at=at: (1 - feat) * (halo_rows + 2 * half_rows) + at,
            lambda feat, at=at: feat * (halo_rows + 2 * half_rows) + at,
        ]
        at += rows

    early = len(halo) - 2
    held = jnp.concatenate([first_rows, got], axis=0)
    held = jnp.concatenate([held, swap_feat(held)], axis=1)
    held, local[-1], *halo[:early] = barrier((held, local[-1], *halo[:early]))
    table = local_call(feat, local_places + halo_places[:early], local + halo[:early], table)
    held = jnp.concatenate([held] + [fetch(held, offset) for offset in evens[1:]], axis=0)
    (coarse,) = node_call(
        "coarse", 0, feat, coarse_state, 0, 0, held.shape[0], held, held, weights
    )
    send, keep, _, table = aggregate_call(
        feat, links, staged, coarse, degree, table, (0, LAST_BLOCKS[0]), halo_places[early:], halo[early:]
    )
    recv = swap_feat(send)
    send_1, keep_1 = aggregate_call(feat, links, staged, coarse, degree, table, LAST_BLOCKS)
    recv, keep, send_1 = barrier((recv, keep, send_1))
    inputs = [(keep, recv), (keep_1, swap_feat(send_1))]
    out = None
    swapped = []
    placed = []
    for chunk, offset, count in LAST_ROWS:
        at = (chunk * LAST_BLOCKS[0] + offset) * block
        done = 1 if len(swapped) == len(LAST_ROWS) - 1 else 0
        new_state, out = node_call(
            "last", 1, feat, state, at, offset * block, count * block, *inputs[chunk], weights,
            out, node_state.shape[0], placed[:done], swapped[:done],
        )
        swapped.append(swap_feat(new_state))
        placed.append(at)
    return assemble_call(feat, placed[1:], swapped[1:], out)


def solution(mesh):
    return jax.shard_map(
        shards,
        mesh=mesh,
        in_specs=(
            P(("member", "patch"), None),
            P("patch", None, None, None),
            P("patch", None, None),
            P("patch", None),
            P("patch", None),
            P("patch"),
            P(None, None, "feat"),
            P(None, None, "feat"),
            P(None, "feat", None),
        ),
        out_specs=P(("member", "patch"), None),
        check_vma=False,
    )
```

```python
import functools

import jax
import jax.numpy as jnp
from jax import lax
from jax.experimental import pallas as pl
from jax.experimental.pallas import tpu as pltpu
from jax.sharding import PartitionSpec as P

CN_DEV = 40
LAYERS = 2
HALO_BLK = 20
MID_BLOCKS = (10, 10)
LAST_BLOCKS = (10, 10)
LAST_ROWS = ((0, 0, 10), (1, 0, 5), (1, 5, 5))
MESSAGE_ROWS = ((0, 20), (20, 20))
MESSAGE_TILE = 640
NODE_SPLIT = 2
F32 = jnp.float32
BF16 = jnp.bfloat16
LONG = pl.CostEstimate(flops=1 << 33, transcendentals=0, bytes_accessed=1 << 10)
SMALL = pl.CostEstimate(flops=1 << 20, transcendentals=0, bytes_accessed=1 << 10)
IN_VMEM = pl.BlockSpec(memory_space=pltpu.VMEM)
IN_HBM = pl.BlockSpec(memory_space=pltpu.HBM)


def silu(v):
    return 0.5 * v * (1.0 + jnp.tanh(0.5 * v))


def dot(a, b):
    return jnp.dot(a, b, preferred_element_type=F32)


def normalize(parts):
    width = sum(part.shape[-1] for part in parts)
    mean = sum(jnp.sum(part, axis=-1, keepdims=True) for part in parts) / width
    center = [part - mean for part in parts]
    spread = sum(jnp.sum(part * part, axis=-1, keepdims=True) for part in center) / width
    scale = lax.rsqrt(spread + 1e-05)
    return [(part * scale).astype(BF16) for part in center]


def params(mib):
    return pltpu.CompilerParams(vmem_limit_bytes=mib << 20)


def shaped(array):
    return jax.ShapeDtypeStruct(array.shape, array.dtype)


def run_copies(pairs, sems):
    copies = [pltpu.make_async_copy(src, dst, sems.at[pos]) for pos, (src, dst) in enumerate(pairs)]
    for copy in copies:
        copy.start()
    return copies


def wait_all(copies):
    for copy in copies:
        copy.wait()


def coarse_message_kernel(state_ref, weight_ref, out_ref):
    (normed,) = normalize([state_ref[...].astype(F32)])
    out_ref[...] = silu(dot(normed, weight_ref[0])).astype(BF16).astype(F32)


def message_kernel(start, tile, state, weight, out, state_buf, weight_buf, out_ref, sems):
    rows = out_ref.shape[0]
    tiles = [(at, tile) for at in range(0, rows, tile)]
    pairs = [(state.at[pl.ds(start + at, size)], state_buf.at[pl.ds(at, size)]) for at, size in tiles]
    copies = run_copies(pairs[:1] + [(weight.at[0], weight_buf)] + pairs[1:], sems)
    weight_copy = copies.pop(1)
    normed = []
    for pos in range(len(tiles) + 1):
        if pos < len(tiles):
            at, size = tiles[pos]
            copies[pos].wait()
            normed += normalize([state_buf[at : at + size, :].astype(F32)])
        if pos == 0:
            weight_copy.wait()
            continue
        at, size = tiles[pos - 1]
        out_ref[at : at + size, :] = silu(dot(normed[pos - 1], weight_buf[...])).astype(BF16)
        span = pl.ds(at, size)
        copy = pltpu.make_async_copy(out_ref.at[span], out.at[span], sems.at[len(tiles) + pos])
        copy.start()
        copies.append(copy)
    wait_all(copies[len(tiles) :])


def message_call(state, weight, start, rows, tile):
    width, columns = weight.shape[1:]
    return pl.pallas_call(
        functools.partial(message_kernel, start, tile),
        in_specs=[IN_HBM, IN_HBM],
        out_specs=IN_HBM,
        out_shape=jax.ShapeDtypeStruct((rows, columns), BF16),
        scratch_shapes=[
            pltpu.VMEM((rows, width), BF16),
            pltpu.VMEM((width, columns), BF16),
            pltpu.VMEM((rows, columns), BF16),
            pltpu.SemaphoreType.DMA((1 + 2 * (rows // tile),)),
        ],
        compiler_params=params(56),
        cost_estimate=SMALL,
        name="message",
    )(state, weight)


def coarse_message_call(state, weight):
    return pl.pallas_call(
        coarse_message_kernel,
        in_specs=[IN_VMEM, IN_VMEM],
        out_specs=IN_VMEM,
        out_shape=pltpu.VMEM((state.shape[0], weight.shape[2]), F32),
        compiler_params=params(12),
        cost_estimate=SMALL,
        name="coarse_message",
    )(state, weight)


def stage_kernel(locals_, count, feat_ref, *refs):
    fine, coarse, state = refs[:3]
    pieces = refs[3 : 3 + locals_]
    refs = refs[3 + locals_ :]
    weights = refs[:count]
    fine_out, coarse_out, state_out, table = refs[count : 4 + count]
    weights_out = refs[4 + count : 4 + 2 * count]
    coarse_buf, sems = refs[4 + 2 * count :]
    block = fine.shape[-1]
    half_rows = state_out.shape[0]
    pairs = [(coarse, coarse_buf)]
    pairs += [
        (fine.at[:, kind], fine_out.at[:, :, pl.ds(kind * block, block)]) for kind in range(fine.shape[1])
    ]
    start = pl.multiple_of(feat_ref[0] * half_rows, 16)
    pairs.append((state.at[pl.ds(start, half_rows)], state_out))
    at = HALO_BLK * block
    for piece in pieces:
        pairs.append((piece, table.at[pl.ds(at, piece.shape[0])]))
        at += piece.shape[0]
    pairs += list(zip(weights, weights_out))
    copies = run_copies(pairs, sems)
    copies[0].wait()

    def turn(pos, carry):
        coarse_out[pos] = jnp.transpose(coarse_buf[pos])
        return carry

    lax.fori_loop(0, coarse.shape[0], turn, 0)
    wait_all(copies[1:])


def stage_call(feat, fine, coarse, state, pieces, weights):
    blocks, kinds, block, _ = fine.shape
    rows, columns = blocks // 2 * block, pieces[0].shape[1]
    out_shape = [
        pltpu.VMEM((blocks, block, kinds * block), BF16),
        pltpu.VMEM((blocks, block, coarse.shape[1]), BF16),
        pltpu.VMEM((rows, state.shape[1]), BF16),
        pltpu.VMEM((2 * rows + 2 * HALO_BLK * block, columns), BF16),
    ] + [pltpu.VMEM(weight.shape, BF16) for weight in weights]
    copies = 2 + kinds + len(pieces) + len(weights)
    return pl.pallas_call(
        functools.partial(stage_kernel, len(pieces), len(weights)),
        grid_spec=pltpu.PrefetchScalarGridSpec(
            num_scalar_prefetch=1,
            in_specs=[IN_HBM] * (3 + len(pieces) + len(weights)),
            out_specs=[IN_VMEM] * len(out_shape),
            scratch_shapes=[pltpu.VMEM(coarse.shape, BF16), pltpu.SemaphoreType.DMA((copies,))],
        ),
        out_shape=out_shape,
        compiler_params=params(36),
        cost_estimate=SMALL,
        name="stage",
    )(feat, fine, coarse, state, *pieces, *weights)


def weights_kernel(*refs):
    sems = refs[-1]
    count = len(refs) // 2
    wait_all(run_copies(list(zip(refs[:count], refs[count:-1])), sems))


def weights_call(weights):
    return pl.pallas_call(
        weights_kernel,
        in_specs=[IN_HBM] * len(weights),
        out_specs=[IN_VMEM] * len(weights),
        scratch_shapes=[pltpu.SemaphoreType.DMA((len(weights),))],
        out_shape=[pltpu.VMEM(weight.shape, BF16) for weight in weights],
        compiler_params=params(4),
        cost_estimate=SMALL,
        name="weights",
    )(*weights)


def local_kernel(places, feat_ref, *refs):
    pieces = refs[: len(places)]
    table, sems = refs[-2:]
    pairs = []
    for place, piece in zip(places, pieces):
        start = pl.multiple_of(place(feat_ref[0]), 16)
        pairs.append((piece, table.at[pl.ds(start, piece.shape[0])]))
    wait_all(run_copies(pairs, sems))


def local_call(feat, places, pieces, table):
    return pl.pallas_call(
        functools.partial(local_kernel, places),
        grid_spec=pltpu.PrefetchScalarGridSpec(
            num_scalar_prefetch=1,
            in_specs=[pl.BlockSpec(memory_space=pl.ANY)] * len(pieces) + [IN_VMEM],
            out_specs=IN_VMEM,
            scratch_shapes=[pltpu.SemaphoreType.DMA((len(pieces),))],
        ),
        out_shape=pltpu.VMEM(table.shape, BF16),
        input_output_aliases={len(pieces) + 1: 0},
        compiler_params=params(4),
        cost_estimate=SMALL,
        name="local_messages",
    )(feat, *pieces, table)


def aggregate_kernel(places, start, feat_ref, links, *refs):
    fine, coarse_tile, coarse, degree = refs[:4]
    pieces = refs[4 : 4 + len(places)]
    if places:
        send, keep, *first_rows, table, sems = refs[5 + len(places) :]
        pairs = []
        for place, piece in zip(places, pieces):
            at = pl.multiple_of(place(feat_ref[0]), 16)
            pairs.append((piece, table.at[pl.ds(at, piece.shape[0])]))
        copies = run_copies(pairs, sems)
    else:
        table, send, keep = refs[4:]
        copies = []
    blocks, block, fine_width = fine.shape
    kinds = fine_width // block
    count = send.shape[0] // block
    feat = feat_ref[0]
    wait_all(copies)
    for out_ref, which in ((send, 1 - feat), (keep, feat)):
        scale = 1.0 / jnp.transpose(degree[which].astype(F32))
        first = which * (blocks // 2) + start
        for pos in range(count):
            row = (first + pos) * kinds
            chosen = jnp.concatenate(
                [table[pl.ds(pl.multiple_of(links[row + kind], block), block), :] for kind in range(kinds)], axis=0
            )
            base = blocks * kinds + row
            stacked = jnp.concatenate(
                [
                    coarse[pl.ds(pl.multiple_of(links[base + kind], 8), CN_DEV), :]
                    for kind in range(kinds)
                ],
                axis=0,
            ).astype(BF16)
            summed = dot(fine[first + pos], chosen) + dot(coarse_tile[first + pos], stacked)
            result = (summed * scale[:, start + pos : start + pos + 1]).astype(BF16)
            out_ref[pos * block : (pos + 1) * block, :] = result
    if places and first_rows:

        @pl.when(feat == 0)
        def _():
            first_rows[0][...] = keep[:CN_DEV, :]

        @pl.when(feat != 0)
        def _():
            first_rows[0][...] = send[:CN_DEV, :]


def aggregate_call(feat, links, staged, coarse, degree, table, span, places=(), pieces=(), wants_first=False):
    fine, coarse_tile = staged
    blocks, block, _ = fine.shape
    columns = table.shape[1]
    start, count = span
    out_shape = [pltpu.VMEM((count * block, columns), BF16)] * 2
    aliases = {}
    scratch = []
    if pieces:
        out_shape += [pltpu.VMEM((CN_DEV, columns), BF16)] * wants_first + [pltpu.VMEM(table.shape, BF16)]
        aliases = {6 + len(pieces): len(out_shape) - 1}
        scratch = [pltpu.SemaphoreType.DMA((len(pieces),))]
    return pl.pallas_call(
        functools.partial(aggregate_kernel, places, start),
        grid_spec=pltpu.PrefetchScalarGridSpec(
            num_scalar_prefetch=2,
            in_specs=[IN_VMEM] * 4 + [IN_HBM] * len(pieces) + [IN_VMEM],
            out_specs=[IN_VMEM] * len(out_shape),
            scratch_shapes=scratch,
        ),
        out_shape=out_shape,
        input_output_aliases=aliases,
        compiler_params=params(12),
        cost_estimate=SMALL,
        name="aggregate",
    )(feat, links, fine, coarse_tile, coarse, degree, *pieces, table)


def node_kernel(mode, layer, start, offset, rows, placed, feat_ref, *refs):
    state_ref, keep, recv, in_own, in_other, out_own, out_other = refs[:7]
    refs = refs[7:]
    feat = feat_ref[0]
    columns = in_own.shape[2]
    width = state_ref.shape[1]
    sides = ((keep, 0), (recv, columns if mode == "coarse" else 0))
    if mode == "last":
        state_out, out, sems = refs[-3:]
        half_rows = out.shape[0] // 2
        pairs = []
        for place, piece in zip(placed, refs):
            at = pl.multiple_of((1 - feat) * half_rows + place, 16)
            pairs.append((piece, out.at[pl.ds(at, piece.shape[0])]))
        copies = run_copies(pairs, sems)
    keep_at = pl.multiple_of(width + feat * columns, columns)
    recv_at = pl.multiple_of(width + (1 - feat) * columns, columns)
    split = NODE_SPLIT if rows % (NODE_SPLIT * 640) == 0 else 1
    size = rows // split
    joined, hidden, state = {}, {}, {}

    def join(at):
        joined[at] = normalize(
            [state_ref[start + at : start + at + size, :].astype(F32)]
            + [ref[offset + at : offset + at + size, col : col + columns].astype(F32) for ref, col in sides]
        )

    def hide(at):
        parts = joined[at]
        hidden[at] = [
            silu(
                dot(parts[0], in_ref[layer, :width, :])
                + dot(parts[1], in_ref[layer, pl.ds(keep_at, columns), :])
                + dot(parts[2], in_ref[layer, pl.ds(recv_at, columns), :])
            ).astype(BF16)
            for in_ref in (in_own, in_other)
        ]

    def update(at):
        change = dot(hidden[at][0], out_own[layer]) + dot(hidden[at][1], out_other[layer])
        state[at] = (state_ref[start + at : start + at + size, :].astype(F32) + change).astype(BF16)
        if mode == "last":
            state_out[at : at + size, :] = state[at]
        elif mode == "mid":
            refs[2][start + at : start + at + size, :] = state[at]

    def norm(at):
        (joined[at],) = normalize([state[at].astype(F32)])

    def tell(at):
        if mode == "coarse":
            refs[1][...] = silu(dot(joined[at], refs[0][layer + 1])).astype(BF16).astype(F32)
            return
        for weight, message in ((refs[0], refs[3]), (refs[1], refs[4])):
            message[at : at + size, :] = silu(dot(joined[at], weight[layer + 1])).astype(BF16)

    stages = [join, hide, update] + ([] if mode == "last" else [norm, tell])
    for step in range(len(stages) + split - 1):
        for pos in range(split):
            if 0 <= step - pos < len(stages):
                stages[step - pos](pos * size)
    if mode == "last":
        at = pl.multiple_of(feat * half_rows + start, 16)
        copy = pltpu.make_async_copy(state_out, out.at[pl.ds(at, rows)], sems.at[len(placed)])
        copy.start()
        wait_all(copies)
        copy.wait()


def node_call(mode, layer, feat, state, start, offset, rows, keep, recv, weights, out=None, total=0, placed=(), pieces=()):
    columns = weights[0].shape[2]
    width = state.shape[1]
    operands = [state, keep, recv, *weights[:4]]
    aliases = {}
    scratch = []
    in_specs = [IN_VMEM] * len(operands)
    if mode == "last":
        out_shape = [pltpu.VMEM((rows, width), BF16), jax.ShapeDtypeStruct((total, width), BF16)]
        out_specs = [IN_VMEM, pl.BlockSpec(memory_space=pl.ANY)]
        scratch = [pltpu.SemaphoreType.DMA((1 + len(pieces),))]
        operands += pieces
        in_specs += [IN_VMEM] * len(pieces)
        if out is not None:
            aliases = {len(operands) + 1: 1}
            operands.append(out)
            in_specs.append(pl.BlockSpec(memory_space=pl.ANY))
    else:
        if mode == "coarse":
            operands.append(weights[4])
            out_shape = [pltpu.VMEM((rows, columns), F32)]
        else:
            operands += weights[4:]
            out_shape = [pltpu.VMEM(state.shape, BF16)] + [pltpu.VMEM((rows, columns), BF16)] * 2
            aliases = {1: 0}
        in_specs = [IN_VMEM] * len(operands)
        out_specs = [IN_VMEM] * len(out_shape)
    return pl.pallas_call(
        functools.partial(node_kernel, mode, layer, start, offset, rows, placed),
        grid_spec=pltpu.PrefetchScalarGridSpec(
            num_scalar_prefetch=1, in_specs=in_specs, out_specs=out_specs, scratch_shapes=scratch
        ),
        out_shape=out_shape,
        input_output_aliases=aliases,
        compiler_params=params(28),
        cost_estimate=LONG if mode == "last" else SMALL,
        name="node_" + mode,
    )(feat, *operands)


def assemble_kernel(placed, feat_ref, *refs):
    pieces = refs[: len(placed)]
    out, sems = refs[-2:]
    half_rows = out.shape[0] // 2
    pairs = []
    for place, piece in zip(placed, pieces):
        at = pl.multiple_of((1 - feat_ref[0]) * half_rows + place, 16)
        pairs.append((piece, out.at[pl.ds(at, piece.shape[0])]))
    wait_all(run_copies(pairs, sems))


def assemble_call(feat, placed, pieces, out):
    return pl.pallas_call(
        functools.partial(assemble_kernel, placed),
        grid_spec=pltpu.PrefetchScalarGridSpec(
            num_scalar_prefetch=1,
            in_specs=[IN_VMEM] * len(pieces) + [pl.BlockSpec(memory_space=pl.ANY)],
            out_specs=pl.BlockSpec(memory_space=pl.ANY),
            scratch_shapes=[pltpu.SemaphoreType.DMA((len(pieces),))],
        ),
        out_shape=shaped(out),
        input_output_aliases={len(pieces) + 1: 0},
        compiler_params=params(4),
        cost_estimate=SMALL,
        name="assemble",
    )(feat, *pieces, out)


def swap_feat(array):
    return lax.ppermute(array, "feat", [(0, 1), (1, 0)])


def fetch(held, stride):
    count = lax.axis_size("patch")
    return lax.ppermute(held, "patch", [(pos, pos ^ stride) for pos in range(count)])


def even_offsets(count):
    assert count & (count - 1) == 0
    offsets = [0]
    stride = count // 2
    while stride > 1:
        offsets += [offset + stride for offset in offsets]
        stride //= 2
    return offsets


def shards(
    node_state, fine_tile, coarse_tile, fine_index, coarse_index, node_degree, w_msg, w_in, w_out
):
    barrier = lax.optimization_barrier
    patches = lax.axis_size("patch")
    patch_pos = lax.axis_index("patch")
    feat_pos = lax.axis_index("feat")
    feat = feat_pos.astype(jnp.int32).reshape(1)
    blocks, kinds, block, _ = fine_tile.shape
    half = blocks // 2
    half_rows = half * block
    halo_rows = HALO_BLK * block
    assert half == HALO_BLK == sum(MID_BLOCKS) == sum(LAST_BLOCKS)

    forward = [(pos, pos + 1) for pos in range(patches - 1)]
    backward = [(target, source) for source, target in forward]
    sides = ((0, backward), (1, forward))
    own_patch = [(2 * src + side, 2 * dst + side) for side, pairs in sides for src, dst in pairs]
    other_patch = [(2 * src + side, 2 * dst + 1 - side) for side, pairs in sides for src, dst in pairs]
    evens = even_offsets(patches)

    held = node_state[:CN_DEV]
    held = jnp.concatenate([held, fetch(held, 1)], axis=0)
    sends = []
    halo = []
    for first, count in MESSAGE_ROWS:
        message = message_call(node_state, w_msg, first * block, count * block, MESSAGE_TILE)
        if not sends:
            message, held = barrier((message, held))
        sends.append(message)
        halo.append(lax.ppermute(message, "patch", backward if first < half else forward))
    high = sends[-1]

    offsets = [even + odd for even in evens for odd in (0, 1)]
    fine_index, coarse_index, node_degree, w_in, w_out, w_late, _ = barrier(
        (fine_index, coarse_index, node_degree, w_in, w_out, w_msg, high)
    )
    links = (fine_index - (patch_pos * blocks - HALO_BLK)).reshape(-1) * block
    away = (coarse_index ^ patch_pos).reshape(-1)
    coarse_links = sum(jnp.where(away == offset, pos * CN_DEV, 0) for pos, offset in enumerate(offsets))
    links = jnp.concatenate([links, coarse_links])
    degree = node_degree.reshape(2, half, block)
    fine, ctile, state, table, in_own, out_own, msg_own = stage_call(
        feat, fine_tile, jnp.swapaxes(coarse_tile, 1, 2), node_state, sends, (w_in, w_out, w_late)
    )
    staged = (fine, ctile)
    others = weights_call([swap_feat(w_in), swap_feat(w_out), swap_feat(w_late)])
    strides = [patches >> step for step in range(1, patches.bit_length() - 1)]
    for step, stride in enumerate(strides):
        got = fetch(held, stride)
        if step == 0:
            got, links, degree, table = barrier((got, links, degree, table))
        if step == len(strides) - 1:
            got, others = barrier((got, others))
        held = jnp.concatenate([held, got], axis=0)
    coarse_state = held
    weights = [in_own, others[0], out_own, others[1], msg_own, others[2]]
    coarse = coarse_message_call(coarse_state, msg_own)

    halo_places = [
        lambda feat, at=first * block: halo_rows + 2 * half_rows + at if at < half_rows else at - half_rows
        for first, _ in MESSAGE_ROWS
    ]
    first_span, last_span = (0, MID_BLOCKS[0]), MID_BLOCKS
    send, keep, first_rows, table = aggregate_call(
        feat, links, staged, coarse, degree, table, first_span, halo_places, halo, True
    )
    recv = swap_feat(send)
    got = fetch(first_rows, 1)
    send_1, keep_1 = aggregate_call(feat, links, staged, coarse, degree, table, last_span)
    recv, keep, send_1 = barrier((recv, keep, send_1))
    inputs = [(keep, recv), (keep_1, swap_feat(send_1))]
    local = []
    local_places = []
    halo = []
    halo_places = []
    at = 0
    for chunk, count in enumerate(MID_BLOCKS):
        rows = count * block
        state, own, other = node_call("mid", 0, feat, state, at, 0, rows, *inputs[chunk], weights)
        if chunk == 0:
            own, other, got = barrier((own, other, got))
        sibling = swap_feat(other)
        if chunk == 0:
            sibling, state = barrier((sibling, state))
        halo += [lax.ppermute(own, ("patch", "feat"), own_patch), lax.ppermute(other, ("patch", "feat"), other_patch)]
        local += [own, sibling]
        local_places += [
            lambda feat, at=at: halo_rows + feat * half_rows + at,
            lambda feat, at=at: halo_rows + (1 - feat) * half_rows + at,
        ]
        halo_places += [
            lambda feat, at=at: (1 - feat) * (halo_rows + 2 * half_rows) + at,
            lambda feat, at=at: feat * (halo_rows + 2 * half_rows) + at,
        ]
        at += rows

    early = len(halo) - 2
    held = jnp.concatenate([first_rows, got], axis=0)
    held = jnp.concatenate([held, swap_feat(held)], axis=1)
    held, local[-1], *halo[:early] = barrier((held, local[-1], *halo[:early]))
    table = local_call(feat, local_places + halo_places[:early], local + halo[:early], table)
    held = jnp.concatenate([held] + [fetch(held, offset) for offset in evens[1:]], axis=0)
    (coarse,) = node_call(
        "coarse", 0, feat, coarse_state, 0, 0, held.shape[0], held, held, weights
    )
    send, keep, table = aggregate_call(
        feat, links, staged, coarse, degree, table, (0, LAST_BLOCKS[0]), halo_places[early:], halo[early:]
    )
    recv = swap_feat(send)
    send_1, keep_1 = aggregate_call(feat, links, staged, coarse, degree, table, LAST_BLOCKS)
    recv, keep, send_1 = barrier((recv, keep, send_1))
    inputs = [(keep, recv), (keep_1, swap_feat(send_1))]
    out = None
    swapped = []
    placed = []
    for chunk, offset, count in LAST_ROWS:
        at = (chunk * LAST_BLOCKS[0] + offset) * block
        done = 1 if len(swapped) == len(LAST_ROWS) - 1 else 0
        new_state, out = node_call(
            "last", 1, feat, state, at, offset * block, count * block, *inputs[chunk], weights,
            out, node_state.shape[0], placed[:done], swapped[:done],
        )
        swapped.append(swap_feat(new_state))
        placed.append(at)
    return assemble_call(feat, placed[1:], swapped[1:], out)


def solution(mesh):
    return jax.shard_map(
        shards,
        mesh=mesh,
        in_specs=(
            P(("member", "patch"), None),
            P("patch", None, None, None),
            P("patch", None, None),
            P("patch", None),
            P("patch", None),
            P("patch"),
            P(None, None, "feat"),
            P(None, None, "feat"),
            P(None, "feat", None),
        ),
        out_specs=P(("member", "patch"), None),
        check_vma=False,
    )
```

```python
import functools

import jax
import jax.numpy as jnp
from jax import lax
from jax.experimental import pallas as pl
from jax.experimental.pallas import tpu as pltpu
from jax.sharding import PartitionSpec as P

CN_DEV = 40
LAYERS = 2
HALO_BLK = 20
MID_BLOCKS = (10, 10)
LAST_BLOCKS = (10, 10)
LAST_ROWS = ((0, 0, 10), (1, 0, 7), (1, 7, 3))
MESSAGE_ROWS = ((0, 20), (20, 20))
MESSAGE_TILES = (512, 640, 640, 512, 256)
NODE_SPLIT = 2
F32 = jnp.float32
BF16 = jnp.bfloat16
LONG = pl.CostEstimate(flops=1 << 33, transcendentals=0, bytes_accessed=1 << 10)
SMALL = pl.CostEstimate(flops=1 << 20, transcendentals=0, bytes_accessed=1 << 10)
IN_VMEM = pl.BlockSpec(memory_space=pltpu.VMEM)
IN_HBM = pl.BlockSpec(memory_space=pltpu.HBM)


def silu(v):
    return 0.5 * v * (1.0 + jnp.tanh(0.5 * v))


def dot(a, b):
    return jnp.dot(a, b, preferred_element_type=F32)


def normalize(parts):
    width = sum(part.shape[-1] for part in parts)
    mean = sum(jnp.sum(part, axis=-1, keepdims=True) for part in parts) / width
    center = [part - mean for part in parts]
    spread = sum(jnp.sum(part * part, axis=-1, keepdims=True) for part in center) / width
    scale = lax.rsqrt(spread + 1e-05)
    return [(part * scale).astype(BF16) for part in center]


def params(mib):
    return pltpu.CompilerParams(vmem_limit_bytes=mib << 20)


def shaped(array):
    return jax.ShapeDtypeStruct(array.shape, array.dtype)


def run_copies(pairs, sems):
    copies = [pltpu.make_async_copy(src, dst, sems.at[pos]) for pos, (src, dst) in enumerate(pairs)]
    for copy in copies:
        copy.start()
    return copies


def wait_all(copies):
    for copy in copies:
        copy.wait()


def coarse_message_kernel(state_ref, weight_ref, out_ref):
    (normed,) = normalize([state_ref[...].astype(F32)])
    out_ref[...] = silu(dot(normed, weight_ref[0])).astype(BF16).astype(F32)


def message_kernel(start, sizes, state, weight, out, state_buf, weight_buf, out_ref, sems):
    tiles = [(sum(sizes[:pos]), size) for pos, size in enumerate(sizes)]
    pairs = [(state.at[pl.ds(start + at, size)], state_buf.at[pl.ds(at, size)]) for at, size in tiles]
    copies = run_copies(pairs[:1] + [(weight.at[0], weight_buf)] + pairs[1:], sems)
    weight_copy = copies.pop(1)
    normed = []
    for pos in range(len(tiles) + 1):
        if pos < len(tiles):
            at, size = tiles[pos]
            copies[pos].wait()
            normed += normalize([state_buf[at : at + size, :].astype(F32)])
        if pos == 0:
            weight_copy.wait()
            continue
        at, size = tiles[pos - 1]
        out_ref[at : at + size, :] = silu(dot(normed[pos - 1], weight_buf[...])).astype(BF16)
        span = pl.ds(at, size)
        copy = pltpu.make_async_copy(out_ref.at[span], out.at[span], sems.at[len(tiles) + pos])
        copy.start()
        copies.append(copy)
    wait_all(copies[len(tiles) :])


def message_call(state, weight, start, rows, sizes):
    assert sum(sizes) == rows
    width, columns = weight.shape[1:]
    return pl.pallas_call(
        functools.partial(message_kernel, start, sizes),
        in_specs=[IN_HBM, IN_HBM],
        out_specs=IN_HBM,
        out_shape=jax.ShapeDtypeStruct((rows, columns), BF16),
        scratch_shapes=[
            pltpu.VMEM((rows, width), BF16),
            pltpu.VMEM((width, columns), BF16),
            pltpu.VMEM((rows, columns), BF16),
            pltpu.SemaphoreType.DMA((1 + 2 * len(sizes),)),
        ],
        compiler_params=params(56),
        cost_estimate=SMALL,
        name="message",
    )(state, weight)


def coarse_message_call(state, weight):
    return pl.pallas_call(
        coarse_message_kernel,
        in_specs=[IN_VMEM, IN_VMEM],
        out_specs=IN_VMEM,
        out_shape=pltpu.VMEM((state.shape[0], weight.shape[2]), F32),
        compiler_params=params(12),
        cost_estimate=SMALL,
        name="coarse_message",
    )(state, weight)


def stage_kernel(locals_, count, feat_ref, *refs):
    fine, coarse, state = refs[:3]
    pieces = refs[3 : 3 + locals_]
    refs = refs[3 + locals_ :]
    weights = refs[:count]
    fine_out, coarse_out, state_out, table = refs[count : 4 + count]
    weights_out = refs[4 + count : 4 + 2 * count]
    coarse_buf, sems = refs[4 + 2 * count :]
    block = fine.shape[-1]
    half_rows = state_out.shape[0]
    pairs = [(coarse, coarse_buf)]
    pairs += [
        (fine.at[:, kind], fine_out.at[:, :, pl.ds(kind * block, block)]) for kind in range(fine.shape[1])
    ]
    start = pl.multiple_of(feat_ref[0] * half_rows, 16)
    pairs.append((state.at[pl.ds(start, half_rows)], state_out))
    at = HALO_BLK * block
    for piece in pieces:
        pairs.append((piece, table.at[pl.ds(at, piece.shape[0])]))
        at += piece.shape[0]
    pairs += list(zip(weights, weights_out))
    copies = run_copies(pairs, sems)
    copies[0].wait()

    def turn(pos, carry):
        coarse_out[pos] = jnp.transpose(coarse_buf[pos])
        return carry

    lax.fori_loop(0, coarse.shape[0], turn, 0)
    wait_all(copies[1:])


def stage_call(feat, fine, coarse, state, pieces, weights):
    blocks, kinds, block, _ = fine.shape
    rows, columns = blocks // 2 * block, pieces[0].shape[1]
    out_shape = [
        pltpu.VMEM((blocks, block, kinds * block), BF16),
        pltpu.VMEM((blocks, block, coarse.shape[1]), BF16),
        pltpu.VMEM((rows, state.shape[1]), BF16),
        pltpu.VMEM((2 * rows + 2 * HALO_BLK * block, columns), BF16),
    ] + [pltpu.VMEM(weight.shape, BF16) for weight in weights]
    copies = 2 + kinds + len(pieces) + len(weights)
    return pl.pallas_call(
        functools.partial(stage_kernel, len(pieces), len(weights)),
        grid_spec=pltpu.PrefetchScalarGridSpec(
            num_scalar_prefetch=1,
            in_specs=[IN_HBM] * (3 + len(pieces) + len(weights)),
            out_specs=[IN_VMEM] * len(out_shape),
            scratch_shapes=[pltpu.VMEM(coarse.shape, BF16), pltpu.SemaphoreType.DMA((copies,))],
        ),
        out_shape=out_shape,
        compiler_params=params(36),
        cost_estimate=SMALL,
        name="stage",
    )(feat, fine, coarse, state, *pieces, *weights)


def weights_kernel(*refs):
    sems = refs[-1]
    count = len(refs) // 2
    wait_all(run_copies(list(zip(refs[:count], refs[count:-1])), sems))


def weights_call(weights):
    return pl.pallas_call(
        weights_kernel,
        in_specs=[IN_HBM] * len(weights),
        out_specs=[IN_VMEM] * len(weights),
        scratch_shapes=[pltpu.SemaphoreType.DMA((len(weights),))],
        out_shape=[pltpu.VMEM(weight.shape, BF16) for weight in weights],
        compiler_params=params(4),
        cost_estimate=SMALL,
        name="weights",
    )(*weights)


def local_kernel(places, feat_ref, *refs):
    pieces = refs[: len(places)]
    table, sems = refs[-2:]
    pairs = []
    for place, piece in zip(places, pieces):
        start = pl.multiple_of(place(feat_ref[0]), 16)
        pairs.append((piece, table.at[pl.ds(start, piece.shape[0])]))
    wait_all(run_copies(pairs, sems))


def local_call(feat, places, pieces, table):
    return pl.pallas_call(
        functools.partial(local_kernel, places),
        grid_spec=pltpu.PrefetchScalarGridSpec(
            num_scalar_prefetch=1,
            in_specs=[pl.BlockSpec(memory_space=pl.ANY)] * len(pieces) + [IN_VMEM],
            out_specs=IN_VMEM,
            scratch_shapes=[pltpu.SemaphoreType.DMA((len(pieces),))],
        ),
        out_shape=pltpu.VMEM(table.shape, BF16),
        input_output_aliases={len(pieces) + 1: 0},
        compiler_params=params(4),
        cost_estimate=SMALL,
        name="local_messages",
    )(feat, *pieces, table)


def aggregate_kernel(places, start, feat_ref, links, *refs):
    fine, coarse_tile, coarse, degree = refs[:4]
    pieces = refs[4 : 4 + len(places)]
    if places:
        send, keep, *first_rows, table, sems = refs[5 + len(places) :]
        pairs = []
        for place, piece in zip(places, pieces):
            at = pl.multiple_of(place(feat_ref[0]), 16)
            pairs.append((piece, table.at[pl.ds(at, piece.shape[0])]))
        copies = run_copies(pairs, sems)
    else:
        table, send, keep = refs[4:]
        copies = []
    blocks, block, fine_width = fine.shape
    kinds = fine_width // block
    count = send.shape[0] // block
    feat = feat_ref[0]
    wait_all(copies)
    for out_ref, which in ((send, 1 - feat), (keep, feat)):
        scale = 1.0 / jnp.transpose(degree[which].astype(F32))
        first = which * (blocks // 2) + start
        for pos in range(count):
            row = (first + pos) * kinds
            chosen = jnp.concatenate(
                [table[pl.ds(pl.multiple_of(links[row + kind], block), block), :] for kind in range(kinds)], axis=0
            )
            base = blocks * kinds + row
            stacked = jnp.concatenate(
                [
                    coarse[pl.ds(pl.multiple_of(links[base + kind], 8), CN_DEV), :]
                    for kind in range(kinds)
                ],
                axis=0,
            ).astype(BF16)
            summed = dot(fine[first + pos], chosen) + dot(coarse_tile[first + pos], stacked)
            result = (summed * scale[:, start + pos : start + pos + 1]).astype(BF16)
            out_ref[pos * block : (pos + 1) * block, :] = result
    if places and first_rows:

        @pl.when(feat == 0)
        def _():
            first_rows[0][...] = keep[:CN_DEV, :]

        @pl.when(feat != 0)
        def _():
            first_rows[0][...] = send[:CN_DEV, :]


def aggregate_call(feat, links, staged, coarse, degree, table, span, places=(), pieces=(), wants_first=False):
    fine, coarse_tile = staged
    blocks, block, _ = fine.shape
    columns = table.shape[1]
    start, count = span
    out_shape = [pltpu.VMEM((count * block, columns), BF16)] * 2
    aliases = {}
    scratch = []
    if pieces:
        out_shape += [pltpu.VMEM((CN_DEV, columns), BF16)] * wants_first + [pltpu.VMEM(table.shape, BF16)]
        aliases = {6 + len(pieces): len(out_shape) - 1}
        scratch = [pltpu.SemaphoreType.DMA((len(pieces),))]
    return pl.pallas_call(
        functools.partial(aggregate_kernel, places, start),
        grid_spec=pltpu.PrefetchScalarGridSpec(
            num_scalar_prefetch=2,
            in_specs=[IN_VMEM] * 4 + [IN_HBM] * len(pieces) + [IN_VMEM],
            out_specs=[IN_VMEM] * len(out_shape),
            scratch_shapes=scratch,
        ),
        out_shape=out_shape,
        input_output_aliases=aliases,
        compiler_params=params(12),
        cost_estimate=SMALL,
        name="aggregate",
    )(feat, links, fine, coarse_tile, coarse, degree, *pieces, table)


def node_kernel(mode, layer, start, offset, rows, placed, feat_ref, *refs):
    state_ref, keep, recv, in_own, in_other, out_own, out_other = refs[:7]
    refs = refs[7:]
    feat = feat_ref[0]
    columns = in_own.shape[2]
    width = state_ref.shape[1]
    sides = ((keep, 0), (recv, columns if mode == "coarse" else 0))
    if mode == "last":
        state_out, out, sems = refs[-3:]
        half_rows = out.shape[0] // 2
        pairs = []
        for place, piece in zip(placed, refs):
            at = pl.multiple_of((1 - feat) * half_rows + place, 16)
            pairs.append((piece, out.at[pl.ds(at, piece.shape[0])]))
        copies = run_copies(pairs, sems)
    keep_at = pl.multiple_of(width + feat * columns, columns)
    recv_at = pl.multiple_of(width + (1 - feat) * columns, columns)
    split = NODE_SPLIT if rows % (NODE_SPLIT * 640) == 0 else 1
    size = rows // split
    joined, hidden, state = {}, {}, {}

    def join(at):
        joined[at] = normalize(
            [state_ref[start + at : start + at + size, :].astype(F32)]
            + [ref[offset + at : offset + at + size, col : col + columns].astype(F32) for ref, col in sides]
        )

    def hide(at):
        parts = joined[at]
        hidden[at] = [
            silu(
                dot(parts[0], in_ref[layer, :width, :])
                + dot(parts[1], in_ref[layer, pl.ds(keep_at, columns), :])
                + dot(parts[2], in_ref[layer, pl.ds(recv_at, columns), :])
            ).astype(BF16)
            for in_ref in (in_own, in_other)
        ]

    def update(at):
        change = dot(hidden[at][0], out_own[layer]) + dot(hidden[at][1], out_other[layer])
        state[at] = (state_ref[start + at : start + at + size, :].astype(F32) + change).astype(BF16)
        if mode == "last":
            state_out[at : at + size, :] = state[at]
        elif mode == "mid":
            refs[2][start + at : start + at + size, :] = state[at]

    def norm(at):
        (joined[at],) = normalize([state[at].astype(F32)])

    def tell(at):
        if mode == "coarse":
            refs[1][...] = silu(dot(joined[at], refs[0][layer + 1])).astype(BF16).astype(F32)
            return
        for weight, message in ((refs[0], refs[3]), (refs[1], refs[4])):
            message[at : at + size, :] = silu(dot(joined[at], weight[layer + 1])).astype(BF16)

    stages = [join, hide, update] + ([] if mode == "last" else [norm, tell])
    for step in range(len(stages) + split - 1):
        for pos in range(split):
            if 0 <= step - pos < len(stages):
                stages[step - pos](pos * size)
    if mode == "last":
        at = pl.multiple_of(feat * half_rows + start, 16)
        copy = pltpu.make_async_copy(state_out, out.at[pl.ds(at, rows)], sems.at[len(placed)])
        copy.start()
        wait_all(copies)
        copy.wait()


def node_call(mode, layer, feat, state, start, offset, rows, keep, recv, weights, out=None, total=0, placed=(), pieces=()):
    columns = weights[0].shape[2]
    width = state.shape[1]
    operands = [state, keep, recv, *weights[:4]]
    aliases = {}
    scratch = []
    in_specs = [IN_VMEM] * len(operands)
    if mode == "last":
        out_shape = [pltpu.VMEM((rows, width), BF16), jax.ShapeDtypeStruct((total, width), BF16)]
        out_specs = [IN_VMEM, pl.BlockSpec(memory_space=pl.ANY)]
        scratch = [pltpu.SemaphoreType.DMA((1 + len(pieces),))]
        operands += pieces
        in_specs += [IN_VMEM] * len(pieces)
        if out is not None:
            aliases = {len(operands) + 1: 1}
            operands.append(out)
            in_specs.append(pl.BlockSpec(memory_space=pl.ANY))
    else:
        if mode == "coarse":
            operands.append(weights[4])
            out_shape = [pltpu.VMEM((rows, columns), F32)]
        else:
            operands += weights[4:]
            out_shape = [pltpu.VMEM(state.shape, BF16)] + [pltpu.VMEM((rows, columns), BF16)] * 2
            aliases = {1: 0}
        in_specs = [IN_VMEM] * len(operands)
        out_specs = [IN_VMEM] * len(out_shape)
    return pl.pallas_call(
        functools.partial(node_kernel, mode, layer, start, offset, rows, placed),
        grid_spec=pltpu.PrefetchScalarGridSpec(
            num_scalar_prefetch=1, in_specs=in_specs, out_specs=out_specs, scratch_shapes=scratch
        ),
        out_shape=out_shape,
        input_output_aliases=aliases,
        compiler_params=params(28),
        cost_estimate=LONG if mode == "last" else SMALL,
        name="node_" + mode,
    )(feat, *operands)


def assemble_kernel(placed, feat_ref, *refs):
    pieces = refs[: len(placed)]
    out, sems = refs[-2:]
    half_rows = out.shape[0] // 2
    pairs = []
    for place, piece in zip(placed, pieces):
        at = pl.multiple_of((1 - feat_ref[0]) * half_rows + place, 16)
        pairs.append((piece, out.at[pl.ds(at, piece.shape[0])]))
    wait_all(run_copies(pairs, sems))


def assemble_call(feat, placed, pieces, out):
    return pl.pallas_call(
        functools.partial(assemble_kernel, placed),
        grid_spec=pltpu.PrefetchScalarGridSpec(
            num_scalar_prefetch=1,
            in_specs=[IN_VMEM] * len(pieces) + [pl.BlockSpec(memory_space=pl.ANY)],
            out_specs=pl.BlockSpec(memory_space=pl.ANY),
            scratch_shapes=[pltpu.SemaphoreType.DMA((len(pieces),))],
        ),
        out_shape=shaped(out),
        input_output_aliases={len(pieces) + 1: 0},
        compiler_params=params(4),
        cost_estimate=SMALL,
        name="assemble",
    )(feat, *pieces, out)


def swap_feat(array):
    return lax.ppermute(array, "feat", [(0, 1), (1, 0)])


def fetch(held, stride):
    count = lax.axis_size("patch")
    return lax.ppermute(held, "patch", [(pos, pos ^ stride) for pos in range(count)])


def even_offsets(count):
    assert count & (count - 1) == 0
    offsets = [0]
    stride = count // 2
    while stride > 1:
        offsets += [offset + stride for offset in offsets]
        stride //= 2
    return offsets


def shards(
    node_state, fine_tile, coarse_tile, fine_index, coarse_index, node_degree, w_msg, w_in, w_out
):
    barrier = lax.optimization_barrier
    patches = lax.axis_size("patch")
    patch_pos = lax.axis_index("patch")
    feat_pos = lax.axis_index("feat")
    feat = feat_pos.astype(jnp.int32).reshape(1)
    blocks, kinds, block, _ = fine_tile.shape
    half = blocks // 2
    half_rows = half * block
    halo_rows = HALO_BLK * block
    assert half == HALO_BLK == sum(MID_BLOCKS) == sum(LAST_BLOCKS)

    forward = [(pos, pos + 1) for pos in range(patches - 1)]
    backward = [(target, source) for source, target in forward]
    sides = ((0, backward), (1, forward))
    own_patch = [(2 * src + side, 2 * dst + side) for side, pairs in sides for src, dst in pairs]
    other_patch = [(2 * src + side, 2 * dst + 1 - side) for side, pairs in sides for src, dst in pairs]
    evens = even_offsets(patches)

    held = node_state[:CN_DEV]
    held = jnp.concatenate([held, fetch(held, 1)], axis=0)
    sends = []
    halo = []
    for first, count in MESSAGE_ROWS:
        message = message_call(node_state, w_msg, first * block, count * block, MESSAGE_TILES)
        if not sends:
            message, held = barrier((message, held))
        sends.append(message)
        halo.append(lax.ppermute(message, "patch", backward if first < half else forward))
    high = sends[-1]

    offsets = [even + odd for even in evens for odd in (0, 1)]
    fine_index, coarse_index, node_degree, w_in, w_out, w_late, _ = barrier(
        (fine_index, coarse_index, node_degree, w_in, w_out, w_msg, high)
    )
    links = (fine_index - (patch_pos * blocks - HALO_BLK)).reshape(-1) * block
    away = (coarse_index ^ patch_pos).reshape(-1)
    coarse_links = sum(jnp.where(away == offset, pos * CN_DEV, 0) for pos, offset in enumerate(offsets))
    links = jnp.concatenate([links, coarse_links])
    degree = node_degree.reshape(2, half, block)
    fine, ctile, state, table, in_own, out_own, msg_own = stage_call(
        feat, fine_tile, jnp.swapaxes(coarse_tile, 1, 2), node_state, sends, (w_in, w_out, w_late)
    )
    staged = (fine, ctile)
    others = weights_call([swap_feat(w_in), swap_feat(w_out), swap_feat(w_late)])
    strides = [patches >> step for step in range(1, patches.bit_length() - 1)]
    for step, stride in enumerate(strides):
        got = fetch(held, stride)
        if step == 0:
            got, links, degree, table = barrier((got, links, degree, table))
        if step == len(strides) - 1:
            got, others = barrier((got, others))
        held = jnp.concatenate([held, got], axis=0)
    coarse_state = held
    weights = [in_own, others[0], out_own, others[1], msg_own, others[2]]
    coarse = coarse_message_call(coarse_state, msg_own)

    halo_places = [
        lambda feat, at=first * block: halo_rows + 2 * half_rows + at if at < half_rows else at - half_rows
        for first, _ in MESSAGE_ROWS
    ]
    first_span, last_span = (0, MID_BLOCKS[0]), MID_BLOCKS
    send, keep, first_rows, table = aggregate_call(
        feat, links, staged, coarse, degree, table, first_span, halo_places, halo, True
    )
    recv = swap_feat(send)
    got = fetch(first_rows, 1)
    send_1, keep_1 = aggregate_call(feat, links, staged, coarse, degree, table, last_span)
    recv, keep, send_1 = barrier((recv, keep, send_1))
    inputs = [(keep, recv), (keep_1, swap_feat(send_1))]
    local = []
    local_places = []
    halo = []
    halo_places = []
    at = 0
    for chunk, count in enumerate(MID_BLOCKS):
        rows = count * block
        state, own, other = node_call("mid", 0, feat, state, at, 0, rows, *inputs[chunk], weights)
        if chunk == 0:
            own, other, got = barrier((own, other, got))
        sibling = swap_feat(other)
        if chunk == 0:
            sibling, state = barrier((sibling, state))
        halo += [lax.ppermute(own, ("patch", "feat"), own_patch), lax.ppermute(other, ("patch", "feat"), other_patch)]
        local += [own, sibling]
        local_places += [
            lambda feat, at=at: halo_rows + feat * half_rows + at,
            lambda feat, at=at: halo_rows + (1 - feat) * half_rows + at,
        ]
        halo_places += [
            lambda feat, at=at: (1 - feat) * (halo_rows + 2 * half_rows) + at,
            lambda feat, at=at: feat * (halo_rows + 2 * half_rows) + at,
        ]
        at += rows

    early = len(halo) - 2
    held = jnp.concatenate([first_rows, got], axis=0)
    held = jnp.concatenate([held, swap_feat(held)], axis=1)
    held, local[-1], *halo[:early] = barrier((held, local[-1], *halo[:early]))
    table = local_call(feat, local_places + halo_places[:early], local + halo[:early], table)
    held = jnp.concatenate([held] + [fetch(held, offset) for offset in evens[1:]], axis=0)
    (coarse,) = node_call(
        "coarse", 0, feat, coarse_state, 0, 0, held.shape[0], held, held, weights
    )
    send, keep, table = aggregate_call(
        feat, links, staged, coarse, degree, table, (0, LAST_BLOCKS[0]), halo_places[early:], halo[early:]
    )
    recv = swap_feat(send)
    send_1, keep_1 = aggregate_call(feat, links, staged, coarse, degree, table, LAST_BLOCKS)
    recv, keep, send_1 = barrier((recv, keep, send_1))
    inputs = [(keep, recv), (keep_1, swap_feat(send_1))]
    out = None
    swapped = []
    placed = []
    for chunk, offset, count in LAST_ROWS:
        at = (chunk * LAST_BLOCKS[0] + offset) * block
        done = 1 if len(swapped) == len(LAST_ROWS) - 1 else 0
        new_state, out = node_call(
            "last", 1, feat, state, at, offset * block, count * block, *inputs[chunk], weights,
            out, node_state.shape[0], placed[:done], swapped[:done],
        )
        swapped.append(swap_feat(new_state))
        placed.append(at)
    return assemble_call(feat, placed[1:], swapped[1:], out)


def solution(mesh):
    return jax.shard_map(
        shards,
        mesh=mesh,
        in_specs=(
            P(("member", "patch"), None),
            P("patch", None, None, None),
            P("patch", None, None),
            P("patch", None),
            P("patch", None),
            P("patch"),
            P(None, None, "feat"),
            P(None, None, "feat"),
            P(None, "feat", None),
        ),
        out_specs=P(("member", "patch"), None),
        check_vma=False,
    )
```

```python
import functools

import jax
import jax.numpy as jnp
from jax import lax
from jax.experimental import pallas as pl
from jax.experimental.pallas import tpu as pltpu
from jax.sharding import PartitionSpec as P

CN_DEV = 40
LAYERS = 2
HALO_BLK = 20
MID_BLOCKS = (10, 10)
LAST_BLOCKS = (10, 10)
LAST_ROWS = ((0, 0, 10), (1, 0, 7), (1, 7, 3))
MESSAGE_ROWS = ((0, 20), (20, 20))
MESSAGE_TILES = (512, 640, 640, 512, 256)
NODE_SPLIT = 2
F32 = jnp.float32
BF16 = jnp.bfloat16
LONG = pl.CostEstimate(flops=1 << 33, transcendentals=0, bytes_accessed=1 << 10)
SMALL = pl.CostEstimate(flops=1 << 20, transcendentals=0, bytes_accessed=1 << 10)
IN_VMEM = pl.BlockSpec(memory_space=pltpu.VMEM)
IN_HBM = pl.BlockSpec(memory_space=pltpu.HBM)


def silu(v):
    return 0.5 * v * (1.0 + jnp.tanh(0.5 * v))


def dot(a, b):
    return jnp.dot(a, b, preferred_element_type=F32)


def normalize(parts):
    width = sum(part.shape[-1] for part in parts)
    mean = sum(jnp.sum(part, axis=-1, keepdims=True) for part in parts) / width
    center = [part - mean for part in parts]
    spread = sum(jnp.sum(part * part, axis=-1, keepdims=True) for part in center) / width
    scale = lax.rsqrt(spread + 1e-05)
    return [(part * scale).astype(BF16) for part in center]


def params(mib):
    return pltpu.CompilerParams(vmem_limit_bytes=mib << 20)


def shaped(array):
    return jax.ShapeDtypeStruct(array.shape, array.dtype)


def run_copies(pairs, sems):
    copies = [pltpu.make_async_copy(src, dst, sems.at[pos]) for pos, (src, dst) in enumerate(pairs)]
    for copy in copies:
        copy.start()
    return copies


def wait_all(copies):
    for copy in copies:
        copy.wait()


def coarse_message_kernel(state_ref, weight_ref, out_ref):
    (normed,) = normalize([state_ref[...].astype(F32)])
    out_ref[...] = silu(dot(normed, weight_ref[0])).astype(BF16).astype(F32)


def message_kernel(start, sizes, state, weight, out, state_buf, weight_buf, out_ref, sems):
    tiles = [(sum(sizes[:pos]), size) for pos, size in enumerate(sizes)]
    pairs = [(state.at[pl.ds(start + at, size)], state_buf.at[pl.ds(at, size)]) for at, size in tiles]
    copies = run_copies(pairs[:1] + [(weight.at[0], weight_buf)] + pairs[1:], sems)
    weight_copy = copies.pop(1)
    normed = []
    for pos in range(len(tiles) + 1):
        if pos < len(tiles):
            at, size = tiles[pos]
            copies[pos].wait()
            normed += normalize([state_buf[at : at + size, :].astype(F32)])
        if pos == 0:
            weight_copy.wait()
            continue
        at, size = tiles[pos - 1]
        out_ref[at : at + size, :] = silu(dot(normed[pos - 1], weight_buf[...])).astype(BF16)
        span = pl.ds(at, size)
        copy = pltpu.make_async_copy(out_ref.at[span], out.at[span], sems.at[len(tiles) + pos])
        copy.start()
        copies.append(copy)
    wait_all(copies[len(tiles) :])


def message_call(state, weight, start, rows, sizes):
    assert sum(sizes) == rows
    width, columns = weight.shape[1:]
    return pl.pallas_call(
        functools.partial(message_kernel, start, sizes),
        in_specs=[IN_HBM, IN_HBM],
        out_specs=IN_HBM,
        out_shape=jax.ShapeDtypeStruct((rows, columns), BF16),
        scratch_shapes=[
            pltpu.VMEM((rows, width), BF16),
            pltpu.VMEM((width, columns), BF16),
            pltpu.VMEM((rows, columns), BF16),
            pltpu.SemaphoreType.DMA((1 + 2 * len(sizes),)),
        ],
        compiler_params=params(56),
        cost_estimate=SMALL,
        name="message",
    )(state, weight)


def coarse_message_call(state, weight):
    return pl.pallas_call(
        coarse_message_kernel,
        in_specs=[IN_VMEM, IN_VMEM],
        out_specs=IN_VMEM,
        out_shape=pltpu.VMEM((state.shape[0], weight.shape[2]), F32),
        compiler_params=params(12),
        cost_estimate=SMALL,
        name="coarse_message",
    )(state, weight)


def stage_kernel(locals_, count, feat_ref, *refs):
    fine, coarse, state = refs[:3]
    pieces = refs[3 : 3 + locals_]
    refs = refs[3 + locals_ :]
    weights = refs[:count]
    fine_out, coarse_out, state_out, table = refs[count : 4 + count]
    weights_out = refs[4 + count : 4 + 2 * count]
    coarse_buf, sems = refs[4 + 2 * count :]
    block = fine.shape[-1]
    half_rows = state_out.shape[0]
    pairs = [(coarse, coarse_buf)]
    pairs += [
        (fine.at[:, kind], fine_out.at[:, :, pl.ds(kind * block, block)]) for kind in range(fine.shape[1])
    ]
    start = pl.multiple_of(feat_ref[0] * half_rows, 16)
    pairs.append((state.at[pl.ds(start, half_rows)], state_out))
    at = HALO_BLK * block
    for piece in pieces:
        pairs.append((piece, table.at[pl.ds(at, piece.shape[0])]))
        at += piece.shape[0]
    pairs += list(zip(weights, weights_out))
    copies = run_copies(pairs, sems)
    copies[0].wait()

    def turn(pos, carry):
        coarse_out[pos] = jnp.transpose(coarse_buf[pos])
        return carry

    lax.fori_loop(0, coarse.shape[0], turn, 0)
    wait_all(copies[1:])


def stage_call(feat, fine, coarse, state, pieces, weights):
    blocks, kinds, block, _ = fine.shape
    rows, columns = blocks // 2 * block, pieces[0].shape[1]
    out_shape = [
        pltpu.VMEM((blocks, block, kinds * block), BF16),
        pltpu.VMEM((blocks, block, coarse.shape[1]), BF16),
        pltpu.VMEM((rows, state.shape[1]), BF16),
        pltpu.VMEM((2 * rows + 2 * HALO_BLK * block, columns), BF16),
    ] + [pltpu.VMEM(weight.shape, BF16) for weight in weights]
    copies = 2 + kinds + len(pieces) + len(weights)
    return pl.pallas_call(
        functools.partial(stage_kernel, len(pieces), len(weights)),
        grid_spec=pltpu.PrefetchScalarGridSpec(
            num_scalar_prefetch=1,
            in_specs=[IN_HBM] * (3 + len(pieces) + len(weights)),
            out_specs=[IN_VMEM] * len(out_shape),
            scratch_shapes=[pltpu.VMEM(coarse.shape, BF16), pltpu.SemaphoreType.DMA((copies,))],
        ),
        out_shape=out_shape,
        compiler_params=params(36),
        cost_estimate=SMALL,
        name="stage",
    )(feat, fine, coarse, state, *pieces, *weights)


def weights_kernel(*refs):
    sems = refs[-1]
    count = len(refs) // 2
    wait_all(run_copies(list(zip(refs[:count], refs[count:-1])), sems))


def weights_call(weights):
    return pl.pallas_call(
        weights_kernel,
        in_specs=[IN_HBM] * len(weights),
        out_specs=[IN_VMEM] * len(weights),
        scratch_shapes=[pltpu.SemaphoreType.DMA((len(weights),))],
        out_shape=[pltpu.VMEM(weight.shape, BF16) for weight in weights],
        compiler_params=params(4),
        cost_estimate=SMALL,
        name="weights",
    )(*weights)


def local_kernel(places, feat_ref, *refs):
    pieces = refs[: len(places)]
    table, sems = refs[-2:]
    pairs = []
    for place, piece in zip(places, pieces):
        start = pl.multiple_of(place(feat_ref[0]), 16)
        pairs.append((piece, table.at[pl.ds(start, piece.shape[0])]))
    wait_all(run_copies(pairs, sems))


def local_call(feat, places, pieces, table):
    return pl.pallas_call(
        functools.partial(local_kernel, places),
        grid_spec=pltpu.PrefetchScalarGridSpec(
            num_scalar_prefetch=1,
            in_specs=[pl.BlockSpec(memory_space=pl.ANY)] * len(pieces) + [IN_VMEM],
            out_specs=IN_VMEM,
            scratch_shapes=[pltpu.SemaphoreType.DMA((len(pieces),))],
        ),
        out_shape=pltpu.VMEM(table.shape, BF16),
        input_output_aliases={len(pieces) + 1: 0},
        compiler_params=params(4),
        cost_estimate=SMALL,
        name="local_messages",
    )(feat, *pieces, table)


def aggregate_kernel(places, start, feat_ref, links, *refs):
    fine, coarse_tile, coarse, degree = refs[:4]
    pieces = refs[4 : 4 + len(places)]
    if places:
        send, keep, *first_rows, table, sems = refs[5 + len(places) :]
        pairs = []
        for place, piece in zip(places, pieces):
            at = pl.multiple_of(place(feat_ref[0]), 16)
            pairs.append((piece, table.at[pl.ds(at, piece.shape[0])]))
        copies = run_copies(pairs, sems)
    else:
        table, send, keep = refs[4:]
        copies = []
    blocks, block, fine_width = fine.shape
    kinds = fine_width // block
    count = send.shape[0] // block
    feat = feat_ref[0]
    wait_all(copies)
    for out_ref, which in ((send, 1 - feat), (keep, feat)):
        scale = 1.0 / jnp.transpose(degree[which].astype(F32))
        first = which * (blocks // 2) + start
        for pos in range(count):
            row = (first + pos) * kinds
            chosen = jnp.concatenate(
                [table[pl.ds(pl.multiple_of(links[row + kind], block), block), :] for kind in range(kinds)], axis=0
            )
            base = blocks * kinds + row
            stacked = jnp.concatenate(
                [
                    coarse[pl.ds(pl.multiple_of(links[base + kind], 8), CN_DEV), :]
                    for kind in range(kinds)
                ],
                axis=0,
            ).astype(BF16)
            summed = dot(fine[first + pos], chosen) + dot(coarse_tile[first + pos], stacked)
            result = (summed * scale[:, start + pos : start + pos + 1]).astype(BF16)
            out_ref[pos * block : (pos + 1) * block, :] = result
    if places and first_rows:

        @pl.when(feat == 0)
        def _():
            first_rows[0][...] = keep[:CN_DEV, :]

        @pl.when(feat != 0)
        def _():
            first_rows[0][...] = send[:CN_DEV, :]


def aggregate_call(feat, links, staged, coarse, degree, table, span, places=(), pieces=(), wants_first=False):
    fine, coarse_tile = staged
    blocks, block, _ = fine.shape
    columns = table.shape[1]
    start, count = span
    out_shape = [pltpu.VMEM((count * block, columns), BF16)] * 2
    aliases = {}
    scratch = []
    if pieces:
        out_shape += [pltpu.VMEM((CN_DEV, columns), BF16)] * wants_first + [pltpu.VMEM(table.shape, BF16)]
        aliases = {6 + len(pieces): len(out_shape) - 1}
        scratch = [pltpu.SemaphoreType.DMA((len(pieces),))]
    return pl.pallas_call(
        functools.partial(aggregate_kernel, places, start),
        grid_spec=pltpu.PrefetchScalarGridSpec(
            num_scalar_prefetch=2,
            in_specs=[IN_VMEM] * 4 + [IN_HBM] * len(pieces) + [IN_VMEM],
            out_specs=[IN_VMEM] * len(out_shape),
            scratch_shapes=scratch,
        ),
        out_shape=out_shape,
        input_output_aliases=aliases,
        compiler_params=params(12),
        cost_estimate=SMALL,
        name="aggregate",
    )(feat, links, fine, coarse_tile, coarse, degree, *pieces, table)


def node_kernel(mode, layer, start, offset, rows, placed, feat_ref, *refs):
    state_ref, keep, recv, in_own, in_other, out_own, out_other = refs[:7]
    refs = refs[7:]
    feat = feat_ref[0]
    columns = in_own.shape[2]
    width = state_ref.shape[1]
    sides = ((keep, 0), (recv, columns if mode == "coarse" else 0))
    if mode == "last":
        state_out, out, sems = refs[-3:]
        half_rows = out.shape[0] // 2
        pairs = []
        for place, piece in zip(placed, refs):
            at = pl.multiple_of((1 - feat) * half_rows + place, 16)
            pairs.append((piece, out.at[pl.ds(at, piece.shape[0])]))
        copies = run_copies(pairs, sems)
    keep_at = pl.multiple_of(width + feat * columns, columns)
    recv_at = pl.multiple_of(width + (1 - feat) * columns, columns)
    split = NODE_SPLIT if rows % (NODE_SPLIT * 640) == 0 else 1
    size = rows // split
    joined, hidden, state = {}, {}, {}

    def join(at):
        joined[at] = normalize(
            [state_ref[start + at : start + at + size, :].astype(F32)]
            + [ref[offset + at : offset + at + size, col : col + columns].astype(F32) for ref, col in sides]
        )

    def hide(at):
        parts = joined[at]
        hidden[at] = [
            silu(
                dot(parts[0], in_ref[layer, :width, :])
                + dot(parts[1], in_ref[layer, pl.ds(keep_at, columns), :])
                + dot(parts[2], in_ref[layer, pl.ds(recv_at, columns), :])
            ).astype(BF16)
            for in_ref in (in_own, in_other)
        ]

    def update(at):
        change = dot(hidden[at][0], out_own[layer]) + dot(hidden[at][1], out_other[layer])
        state[at] = (state_ref[start + at : start + at + size, :].astype(F32) + change).astype(BF16)
        if mode == "last":
            state_out[at : at + size, :] = state[at]
        elif mode == "mid":
            refs[2][start + at : start + at + size, :] = state[at]

    def norm(at):
        (joined[at],) = normalize([state[at].astype(F32)])

    def tell(at):
        if mode == "coarse":
            refs[1][...] = silu(dot(joined[at], refs[0][layer + 1])).astype(BF16).astype(F32)
            return
        for weight, message in ((refs[0], refs[3]), (refs[1], refs[4])):
            message[at : at + size, :] = silu(dot(joined[at], weight[layer + 1])).astype(BF16)

    stages = [join, hide, update] + ([] if mode == "last" else [norm, tell])
    for step in range(len(stages) + split - 1):
        for pos in range(split):
            if 0 <= step - pos < len(stages):
                stages[step - pos](pos * size)
    if mode == "last":
        at = pl.multiple_of(feat * half_rows + start, 16)
        copy = pltpu.make_async_copy(state_out, out.at[pl.ds(at, rows)], sems.at[len(placed)])
        copy.start()
        wait_all(copies)
        copy.wait()


def node_call(mode, layer, feat, state, start, offset, rows, keep, recv, weights, out=None, total=0, placed=(), pieces=()):
    columns = weights[0].shape[2]
    width = state.shape[1]
    operands = [state, keep, recv, *weights[:4]]
    aliases = {}
    scratch = []
    in_specs = [IN_VMEM] * len(operands)
    if mode == "last":
        out_shape = [pltpu.VMEM((rows, width), BF16), jax.ShapeDtypeStruct((total, width), BF16)]
        out_specs = [IN_VMEM, pl.BlockSpec(memory_space=pl.ANY)]
        scratch = [pltpu.SemaphoreType.DMA((1 + len(pieces),))]
        operands += pieces
        in_specs += [IN_VMEM] * len(pieces)
        if out is not None:
            aliases = {len(operands) + 1: 1}
            operands.append(out)
            in_specs.append(pl.BlockSpec(memory_space=pl.ANY))
    else:
        if mode == "coarse":
            operands.append(weights[4])
            out_shape = [pltpu.VMEM((rows, columns), F32)]
        else:
            operands += weights[4:]
            out_shape = [pltpu.VMEM(state.shape, BF16)] + [pltpu.VMEM((rows, columns), BF16)] * 2
            aliases = {1: 0}
        in_specs = [IN_VMEM] * len(operands)
        out_specs = [IN_VMEM] * len(out_shape)
    return pl.pallas_call(
        functools.partial(node_kernel, mode, layer, start, offset, rows, placed),
        grid_spec=pltpu.PrefetchScalarGridSpec(
            num_scalar_prefetch=1, in_specs=in_specs, out_specs=out_specs, scratch_shapes=scratch
        ),
        out_shape=out_shape,
        input_output_aliases=aliases,
        compiler_params=params(28),
        cost_estimate=LONG if mode == "last" else SMALL,
        name="node_" + mode,
    )(feat, *operands)


def assemble_kernel(placed, feat_ref, *refs):
    pieces = refs[: len(placed)]
    out, sems = refs[-2:]
    half_rows = out.shape[0] // 2
    pairs = []
    for place, piece in zip(placed, pieces):
        at = pl.multiple_of((1 - feat_ref[0]) * half_rows + place, 16)
        pairs.append((piece, out.at[pl.ds(at, piece.shape[0])]))
    wait_all(run_copies(pairs, sems))


def assemble_call(feat, placed, pieces, out):
    return pl.pallas_call(
        functools.partial(assemble_kernel, placed),
        grid_spec=pltpu.PrefetchScalarGridSpec(
            num_scalar_prefetch=1,
            in_specs=[IN_VMEM] * len(pieces) + [pl.BlockSpec(memory_space=pl.ANY)],
            out_specs=pl.BlockSpec(memory_space=pl.ANY),
            scratch_shapes=[pltpu.SemaphoreType.DMA((len(pieces),))],
        ),
        out_shape=shaped(out),
        input_output_aliases={len(pieces) + 1: 0},
        compiler_params=params(4),
        cost_estimate=SMALL,
        name="assemble",
    )(feat, *pieces, out)


def swap_feat(array):
    return lax.ppermute(array, "feat", [(0, 1), (1, 0)])


def fetch(held, stride):
    count = lax.axis_size("patch")
    return lax.ppermute(held, "patch", [(pos, pos ^ stride) for pos in range(count)])


def shards(
    node_state, fine_tile, coarse_tile, fine_index, coarse_index, node_degree, w_msg, w_in, w_out
):
    barrier = lax.optimization_barrier
    patches = lax.axis_size("patch")
    patch_pos = lax.axis_index("patch")
    feat_pos = lax.axis_index("feat")
    feat = feat_pos.astype(jnp.int32).reshape(1)
    blocks, kinds, block, _ = fine_tile.shape
    half = blocks // 2
    half_rows = half * block
    halo_rows = HALO_BLK * block
    assert half == HALO_BLK == sum(MID_BLOCKS) == sum(LAST_BLOCKS)

    forward = [(pos, pos + 1) for pos in range(patches - 1)]
    backward = [(target, source) for source, target in forward]
    sides = ((0, backward), (1, forward))
    own_patch = [(2 * src + side, 2 * dst + side) for side, pairs in sides for src, dst in pairs]
    other_patch = [(2 * src + side, 2 * dst + 1 - side) for side, pairs in sides for src, dst in pairs]
    assert patches & (patches - 1) == 0

    sends = []
    halo = []
    for first, count in MESSAGE_ROWS:
        message = message_call(node_state, w_msg, first * block, count * block, MESSAGE_TILES)
        sends.append(message)
        halo.append(lax.ppermute(message, "patch", backward if first < half else forward))
    high = sends[-1]

    fine_index, coarse_index, node_degree, w_in, w_out, w_late, _ = barrier(
        (fine_index, coarse_index, node_degree, w_in, w_out, w_msg, high)
    )
    links = (fine_index - (patch_pos * blocks - HALO_BLK)).reshape(-1) * block
    away = (coarse_index ^ patch_pos).reshape(-1)
    coarse_links = away * CN_DEV
    links = jnp.concatenate([links, coarse_links])
    degree = node_degree.reshape(2, half, block)
    fine, ctile, state, table, in_own, out_own, msg_own = stage_call(
        feat, fine_tile, jnp.swapaxes(coarse_tile, 1, 2), node_state, sends, (w_in, w_out, w_late)
    )
    staged = (fine, ctile)
    others = weights_call([swap_feat(w_in), swap_feat(w_out), swap_feat(w_late)])
    first_rows, _ = barrier((node_state[:CN_DEV], high))
    near_half = [fetch(first_rows, offset) for offset in range(1, patches // 2)]
    *near_half, links, degree, table = barrier((*near_half, links, degree, table))
    held = jnp.concatenate([first_rows, *near_half], axis=0)
    got = fetch(held, patches // 2)
    got, others = barrier((got, others))
    held = jnp.concatenate([held, got], axis=0)
    coarse_state = held
    weights = [in_own, others[0], out_own, others[1], msg_own, others[2]]
    coarse = coarse_message_call(coarse_state, msg_own)

    halo_places = [
        lambda feat, at=first * block: halo_rows + 2 * half_rows + at if at < half_rows else at - half_rows
        for first, _ in MESSAGE_ROWS
    ]
    first_span, last_span = (0, MID_BLOCKS[0]), MID_BLOCKS
    send, keep, first_rows, table = aggregate_call(
        feat, links, staged, coarse, degree, table, first_span, halo_places, halo, True
    )
    recv = swap_feat(send)
    got = fetch(first_rows, 1)
    send_1, keep_1 = aggregate_call(feat, links, staged, coarse, degree, table, last_span)
    recv, keep, send_1 = barrier((recv, keep, send_1))
    inputs = [(keep, recv), (keep_1, swap_feat(send_1))]
    local = []
    local_places = []
    halo = []
    halo_places = []
    at = 0
    for chunk, count in enumerate(MID_BLOCKS):
        rows = count * block
        state, own, other = node_call("mid", 0, feat, state, at, 0, rows, *inputs[chunk], weights)
        if chunk == 0:
            own, other, got = barrier((own, other, got))
        sibling = swap_feat(other)
        if chunk == 0:
            sibling, state = barrier((sibling, state))
        halo += [lax.ppermute(own, ("patch", "feat"), own_patch), lax.ppermute(other, ("patch", "feat"), other_patch)]
        local += [own, sibling]
        local_places += [
            lambda feat, at=at: halo_rows + feat * half_rows + at,
            lambda feat, at=at: halo_rows + (1 - feat) * half_rows + at,
        ]
        halo_places += [
            lambda feat, at=at: (1 - feat) * (halo_rows + 2 * half_rows) + at,
            lambda feat, at=at: feat * (halo_rows + 2 * half_rows) + at,
        ]
        at += rows

    early = len(halo) - 2
    held = jnp.concatenate([first_rows, got], axis=0)
    held = jnp.concatenate([held, swap_feat(held)], axis=1)
    held, local[-1], *halo[:early] = barrier((held, local[-1], *halo[:early]))
    table = local_call(feat, local_places + halo_places[:early], local + halo[:early], table)
    held = jnp.concatenate([held] + [fetch(held, offset) for offset in range(2, patches, 2)], axis=0)
    (coarse,) = node_call(
        "coarse", 0, feat, coarse_state, 0, 0, held.shape[0], held, held, weights
    )
    send, keep, table = aggregate_call(
        feat, links, staged, coarse, degree, table, (0, LAST_BLOCKS[0]), halo_places[early:], halo[early:]
    )
    recv = swap_feat(send)
    send_1, keep_1 = aggregate_call(feat, links, staged, coarse, degree, table, LAST_BLOCKS)
    recv, keep, send_1 = barrier((recv, keep, send_1))
    inputs = [(keep, recv), (keep_1, swap_feat(send_1))]
    out = None
    swapped = []
    placed = []
    for chunk, offset, count in LAST_ROWS:
        at = (chunk * LAST_BLOCKS[0] + offset) * block
        done = 1 if len(swapped) == len(LAST_ROWS) - 1 else 0
        new_state, out = node_call(
            "last", 1, feat, state, at, offset * block, count * block, *inputs[chunk], weights,
            out, node_state.shape[0], placed[:done], swapped[:done],
        )
        swapped.append(swap_feat(new_state))
        placed.append(at)
    return assemble_call(feat, placed[1:], swapped[1:], out)


def solution(mesh):
    return jax.shard_map(
        shards,
        mesh=mesh,
        in_specs=(
            P(("member", "patch"), None),
            P("patch", None, None, None),
            P("patch", None, None),
            P("patch", None),
            P("patch", None),
            P("patch"),
            P(None, None, "feat"),
            P(None, None, "feat"),
            P(None, "feat", None),
        ),
        out_specs=P(("member", "patch"), None),
        check_vma=False,
    )
```

```python
import functools

import jax
import jax.numpy as jnp
from jax import lax
from jax.experimental import pallas as pl
from jax.experimental.pallas import tpu as pltpu
from jax.sharding import PartitionSpec as P

CN_DEV = 40
LAYERS = 2
HALO_BLK = 20
MID_BLOCKS = (10, 10)
LAST_BLOCKS = (10, 10)
LAST_ROWS = ((0, 0, 10), (1, 0, 8), (1, 8, 2))
MESSAGE_ROWS = ((0, 20), (20, 20))
MESSAGE_TILES = (512, 640, 640, 512, 256)
NODE_SPLIT = 2
F32 = jnp.float32
BF16 = jnp.bfloat16
LONG = pl.CostEstimate(flops=1 << 33, transcendentals=0, bytes_accessed=1 << 10)
SMALL = pl.CostEstimate(flops=1 << 20, transcendentals=0, bytes_accessed=1 << 10)
IN_VMEM = pl.BlockSpec(memory_space=pltpu.VMEM)
IN_HBM = pl.BlockSpec(memory_space=pltpu.HBM)


def silu(v):
    return 0.5 * v * (1.0 + jnp.tanh(0.5 * v))


def dot(a, b):
    return jnp.dot(a, b, preferred_element_type=F32)


def normalize(parts):
    width = sum(part.shape[-1] for part in parts)
    mean = sum(jnp.sum(part, axis=-1, keepdims=True) for part in parts) / width
    center = [part - mean for part in parts]
    spread = sum(jnp.sum(part * part, axis=-1, keepdims=True) for part in center) / width
    scale = lax.rsqrt(spread + 1e-05)
    return [(part * scale).astype(BF16) for part in center]


def params(mib):
    return pltpu.CompilerParams(vmem_limit_bytes=mib << 20)


def shaped(array):
    return jax.ShapeDtypeStruct(array.shape, array.dtype)


def run_copies(pairs, sems):
    copies = [pltpu.make_async_copy(src, dst, sems.at[pos]) for pos, (src, dst) in enumerate(pairs)]
    for copy in copies:
        copy.start()
    return copies


def wait_all(copies):
    for copy in copies:
        copy.wait()


def coarse_message_kernel(state_ref, weight_ref, out_ref):
    (normed,) = normalize([state_ref[...].astype(F32)])
    out_ref[...] = silu(dot(normed, weight_ref[0])).astype(BF16).astype(F32)


def message_kernel(start, sizes, state, weight, out, state_buf, weight_buf, out_ref, sems):
    tiles = [(sum(sizes[:pos]), size) for pos, size in enumerate(sizes)]
    pairs = [(state.at[pl.ds(start + at, size)], state_buf.at[pl.ds(at, size)]) for at, size in tiles]
    copies = run_copies(pairs[:1] + [(weight.at[0], weight_buf)] + pairs[1:], sems)
    weight_copy = copies.pop(1)
    normed = []
    for pos in range(len(tiles) + 1):
        if pos < len(tiles):
            at, size = tiles[pos]
            copies[pos].wait()
            normed += normalize([state_buf[at : at + size, :].astype(F32)])
        if pos == 0:
            weight_copy.wait()
            continue
        at, size = tiles[pos - 1]
        out_ref[at : at + size, :] = silu(dot(normed[pos - 1], weight_buf[...])).astype(BF16)
        span = pl.ds(at, size)
        copy = pltpu.make_async_copy(out_ref.at[span], out.at[span], sems.at[len(tiles) + pos])
        copy.start()
        copies.append(copy)
    wait_all(copies[len(tiles) :])


def message_call(state, weight, start, rows, sizes):
    assert sum(sizes) == rows
    width, columns = weight.shape[1:]
    return pl.pallas_call(
        functools.partial(message_kernel, start, sizes),
        in_specs=[IN_HBM, IN_HBM],
        out_specs=IN_HBM,
        out_shape=jax.ShapeDtypeStruct((rows, columns), BF16),
        scratch_shapes=[
            pltpu.VMEM((rows, width), BF16),
            pltpu.VMEM((width, columns), BF16),
            pltpu.VMEM((rows, columns), BF16),
            pltpu.SemaphoreType.DMA((1 + 2 * len(sizes),)),
        ],
        compiler_params=params(56),
        cost_estimate=SMALL,
        name="message",
    )(state, weight)


def coarse_message_call(state, weight):
    return pl.pallas_call(
        coarse_message_kernel,
        in_specs=[IN_VMEM, IN_VMEM],
        out_specs=IN_VMEM,
        out_shape=pltpu.VMEM((state.shape[0], weight.shape[2]), F32),
        compiler_params=params(12),
        cost_estimate=SMALL,
        name="coarse_message",
    )(state, weight)


def stage_kernel(locals_, count, feat_ref, *refs):
    fine, coarse, state = refs[:3]
    pieces = refs[3 : 3 + locals_]
    refs = refs[3 + locals_ :]
    weights = refs[:count]
    fine_out, coarse_out, state_out, table = refs[count : 4 + count]
    weights_out = refs[4 + count : 4 + 2 * count]
    coarse_buf, sems = refs[4 + 2 * count :]
    block = fine.shape[-1]
    half_rows = state_out.shape[0]
    pairs = [(coarse, coarse_buf)]
    pairs += [
        (fine.at[:, kind], fine_out.at[:, :, pl.ds(kind * block, block)]) for kind in range(fine.shape[1])
    ]
    start = pl.multiple_of(feat_ref[0] * half_rows, 16)
    pairs.append((state.at[pl.ds(start, half_rows)], state_out))
    at = HALO_BLK * block
    for piece in pieces:
        pairs.append((piece, table.at[pl.ds(at, piece.shape[0])]))
        at += piece.shape[0]
    pairs += list(zip(weights, weights_out))
    copies = run_copies(pairs, sems)
    copies[0].wait()

    def turn(pos, carry):
        coarse_out[pos] = jnp.transpose(coarse_buf[pos])
        return carry

    lax.fori_loop(0, coarse.shape[0], turn, 0)
    wait_all(copies[1:])


def stage_call(feat, fine, coarse, state, pieces, weights):
    blocks, kinds, block, _ = fine.shape
    rows, columns = blocks // 2 * block, pieces[0].shape[1]
    out_shape = [
        pltpu.VMEM((blocks, block, kinds * block), BF16),
        pltpu.VMEM((blocks, block, coarse.shape[1]), BF16),
        pltpu.VMEM((rows, state.shape[1]), BF16),
        pltpu.VMEM((2 * rows + 2 * HALO_BLK * block, columns), BF16),
    ] + [pltpu.VMEM(weight.shape, BF16) for weight in weights]
    copies = 2 + kinds + len(pieces) + len(weights)
    return pl.pallas_call(
        functools.partial(stage_kernel, len(pieces), len(weights)),
        grid_spec=pltpu.PrefetchScalarGridSpec(
            num_scalar_prefetch=1,
            in_specs=[IN_HBM] * (3 + len(pieces) + len(weights)),
            out_specs=[IN_VMEM] * len(out_shape),
            scratch_shapes=[pltpu.VMEM(coarse.shape, BF16), pltpu.SemaphoreType.DMA((copies,))],
        ),
        out_shape=out_shape,
        compiler_params=params(36),
        cost_estimate=SMALL,
        name="stage",
    )(feat, fine, coarse, state, *pieces, *weights)


def weights_kernel(*refs):
    sems = refs[-1]
    count = len(refs) // 2
    wait_all(run_copies(list(zip(refs[:count], refs[count:-1])), sems))


def weights_call(weights):
    return pl.pallas_call(
        weights_kernel,
        in_specs=[IN_HBM] * len(weights),
        out_specs=[IN_VMEM] * len(weights),
        scratch_shapes=[pltpu.SemaphoreType.DMA((len(weights),))],
        out_shape=[pltpu.VMEM(weight.shape, BF16) for weight in weights],
        compiler_params=params(4),
        cost_estimate=SMALL,
        name="weights",
    )(*weights)


def local_kernel(places, feat_ref, *refs):
    pieces = refs[: len(places)]
    table, sems = refs[-2:]
    pairs = []
    for place, piece in zip(places, pieces):
        start = pl.multiple_of(place(feat_ref[0]), 16)
        pairs.append((piece, table.at[pl.ds(start, piece.shape[0])]))
    wait_all(run_copies(pairs, sems))


def local_call(feat, places, pieces, table):
    return pl.pallas_call(
        functools.partial(local_kernel, places),
        grid_spec=pltpu.PrefetchScalarGridSpec(
            num_scalar_prefetch=1,
            in_specs=[pl.BlockSpec(memory_space=pl.ANY)] * len(pieces) + [IN_VMEM],
            out_specs=IN_VMEM,
            scratch_shapes=[pltpu.SemaphoreType.DMA((len(pieces),))],
        ),
        out_shape=pltpu.VMEM(table.shape, BF16),
        input_output_aliases={len(pieces) + 1: 0},
        compiler_params=params(4),
        cost_estimate=SMALL,
        name="local_messages",
    )(feat, *pieces, table)


def aggregate_kernel(places, start, feat_ref, links, *refs):
    fine, coarse_tile, coarse, degree = refs[:4]
    pieces = refs[4 : 4 + len(places)]
    if places:
        send, keep, *first_rows, table, sems = refs[5 + len(places) :]
        pairs = []
        for place, piece in zip(places, pieces):
            at = pl.multiple_of(place(feat_ref[0]), 16)
            pairs.append((piece, table.at[pl.ds(at, piece.shape[0])]))
        copies = run_copies(pairs, sems)
    else:
        table, send, keep = refs[4:]
        copies = []
    blocks, block, fine_width = fine.shape
    kinds = fine_width // block
    count = send.shape[0] // block
    feat = feat_ref[0]
    wait_all(copies)
    for out_ref, which in ((send, 1 - feat), (keep, feat)):
        scale = 1.0 / jnp.transpose(degree[which].astype(F32))
        first = which * (blocks // 2) + start
        for pos in range(count):
            row = (first + pos) * kinds
            chosen = jnp.concatenate(
                [table[pl.ds(pl.multiple_of(links[row + kind], block), block), :] for kind in range(kinds)], axis=0
            )
            base = blocks * kinds + row
            stacked = jnp.concatenate(
                [
                    coarse[pl.ds(pl.multiple_of(links[base + kind], 8), CN_DEV), :]
                    for kind in range(kinds)
                ],
                axis=0,
            ).astype(BF16)
            summed = dot(fine[first + pos], chosen) + dot(coarse_tile[first + pos], stacked)
            result = (summed * scale[:, start + pos : start + pos + 1]).astype(BF16)
            out_ref[pos * block : (pos + 1) * block, :] = result
    if places and first_rows:

        @pl.when(feat == 0)
        def _():
            first_rows[0][...] = keep[:CN_DEV, :]

        @pl.when(feat != 0)
        def _():
            first_rows[0][...] = send[:CN_DEV, :]


def aggregate_call(feat, links, staged, coarse, degree, table, span, places=(), pieces=(), wants_first=False):
    fine, coarse_tile = staged
    blocks, block, _ = fine.shape
    columns = table.shape[1]
    start, count = span
    out_shape = [pltpu.VMEM((count * block, columns), BF16)] * 2
    aliases = {}
    scratch = []
    if pieces:
        out_shape += [pltpu.VMEM((CN_DEV, columns), BF16)] * wants_first + [pltpu.VMEM(table.shape, BF16)]
        aliases = {6 + len(pieces): len(out_shape) - 1}
        scratch = [pltpu.SemaphoreType.DMA((len(pieces),))]
    return pl.pallas_call(
        functools.partial(aggregate_kernel, places, start),
        grid_spec=pltpu.PrefetchScalarGridSpec(
            num_scalar_prefetch=2,
            in_specs=[IN_VMEM] * 4 + [IN_HBM] * len(pieces) + [IN_VMEM],
            out_specs=[IN_VMEM] * len(out_shape),
            scratch_shapes=scratch,
        ),
        out_shape=out_shape,
        input_output_aliases=aliases,
        compiler_params=params(12),
        cost_estimate=SMALL,
        name="aggregate",
    )(feat, links, fine, coarse_tile, coarse, degree, *pieces, table)


def node_kernel(mode, layer, start, offset, rows, placed, feat_ref, *refs):
    state_ref, keep, recv, in_own, in_other, out_own, out_other = refs[:7]
    refs = refs[7:]
    feat = feat_ref[0]
    columns = in_own.shape[2]
    width = state_ref.shape[1]
    sides = ((keep, 0), (recv, columns if mode == "coarse" else 0))
    if mode == "last":
        state_out, out, sems = refs[-3:]
        half_rows = out.shape[0] // 2
        pairs = []
        for place, piece in zip(placed, refs):
            at = pl.multiple_of((1 - feat) * half_rows + place, 16)
            pairs.append((piece, out.at[pl.ds(at, piece.shape[0])]))
        copies = run_copies(pairs, sems)
    keep_at = pl.multiple_of(width + feat * columns, columns)
    recv_at = pl.multiple_of(width + (1 - feat) * columns, columns)
    split = NODE_SPLIT if rows >= 1024 else 1
    size = rows // split
    joined, hidden, state = {}, {}, {}

    def join(at):
        joined[at] = normalize(
            [state_ref[start + at : start + at + size, :].astype(F32)]
            + [ref[offset + at : offset + at + size, col : col + columns].astype(F32) for ref, col in sides]
        )

    def hide(at):
        parts = joined[at]
        hidden[at] = [
            silu(
                dot(parts[0], in_ref[layer, :width, :])
                + dot(parts[1], in_ref[layer, pl.ds(keep_at, columns), :])
                + dot(parts[2], in_ref[layer, pl.ds(recv_at, columns), :])
            ).astype(BF16)
            for in_ref in (in_own, in_other)
        ]

    def update(at):
        change = dot(hidden[at][0], out_own[layer]) + dot(hidden[at][1], out_other[layer])
        state[at] = (state_ref[start + at : start + at + size, :].astype(F32) + change).astype(BF16)
        if mode == "last":
            state_out[at : at + size, :] = state[at]
        elif mode == "mid":
            refs[2][start + at : start + at + size, :] = state[at]

    def norm(at):
        (joined[at],) = normalize([state[at].astype(F32)])

    def tell(at):
        if mode == "coarse":
            refs[1][...] = silu(dot(joined[at], refs[0][layer + 1])).astype(BF16).astype(F32)
            return
        for weight, message in ((refs[0], refs[3]), (refs[1], refs[4])):
            message[at : at + size, :] = silu(dot(joined[at], weight[layer + 1])).astype(BF16)

    stages = [join, hide, update] + ([] if mode == "last" else [norm, tell])
    for step in range(len(stages) + split - 1):
        for pos in range(split):
            if 0 <= step - pos < len(stages):
                stages[step - pos](pos * size)
    if mode == "last":
        at = pl.multiple_of(feat * half_rows + start, 16)
        copy = pltpu.make_async_copy(state_out, out.at[pl.ds(at, rows)], sems.at[len(placed)])
        copy.start()
        wait_all(copies)
        copy.wait()


def node_call(mode, layer, feat, state, start, offset, rows, keep, recv, weights, out=None, total=0, placed=(), pieces=()):
    columns = weights[0].shape[2]
    width = state.shape[1]
    operands = [state, keep, recv, *weights[:4]]
    aliases = {}
    scratch = []
    in_specs = [IN_VMEM] * len(operands)
    if mode == "last":
        out_shape = [pltpu.VMEM((rows, width), BF16), jax.ShapeDtypeStruct((total, width), BF16)]
        out_specs = [IN_VMEM, pl.BlockSpec(memory_space=pl.ANY)]
        scratch = [pltpu.SemaphoreType.DMA((1 + len(pieces),))]
        operands += pieces
        in_specs += [IN_VMEM] * len(pieces)
        if out is not None:
            aliases = {len(operands) + 1: 1}
            operands.append(out)
            in_specs.append(pl.BlockSpec(memory_space=pl.ANY))
    else:
        if mode == "coarse":
            operands.append(weights[4])
            out_shape = [pltpu.VMEM((rows, columns), F32)]
        else:
            operands += weights[4:]
            out_shape = [pltpu.VMEM(state.shape, BF16)] + [pltpu.VMEM((rows, columns), BF16)] * 2
            aliases = {1: 0}
        in_specs = [IN_VMEM] * len(operands)
        out_specs = [IN_VMEM] * len(out_shape)
    return pl.pallas_call(
        functools.partial(node_kernel, mode, layer, start, offset, rows, placed),
        grid_spec=pltpu.PrefetchScalarGridSpec(
            num_scalar_prefetch=1, in_specs=in_specs, out_specs=out_specs, scratch_shapes=scratch
        ),
        out_shape=out_shape,
        input_output_aliases=aliases,
        compiler_params=params(28),
        cost_estimate=LONG if mode == "last" else SMALL,
        name="node_" + mode,
    )(feat, *operands)


def assemble_kernel(placed, feat_ref, *refs):
    pieces = refs[: len(placed)]
    out, sems = refs[-2:]
    half_rows = out.shape[0] // 2
    pairs = []
    for place, piece in zip(placed, pieces):
        at = pl.multiple_of((1 - feat_ref[0]) * half_rows + place, 16)
        pairs.append((piece, out.at[pl.ds(at, piece.shape[0])]))
    wait_all(run_copies(pairs, sems))


def assemble_call(feat, placed, pieces, out):
    return pl.pallas_call(
        functools.partial(assemble_kernel, placed),
        grid_spec=pltpu.PrefetchScalarGridSpec(
            num_scalar_prefetch=1,
            in_specs=[IN_VMEM] * len(pieces) + [pl.BlockSpec(memory_space=pl.ANY)],
            out_specs=pl.BlockSpec(memory_space=pl.ANY),
            scratch_shapes=[pltpu.SemaphoreType.DMA((len(pieces),))],
        ),
        out_shape=shaped(out),
        input_output_aliases={len(pieces) + 1: 0},
        compiler_params=params(4),
        cost_estimate=SMALL,
        name="assemble",
    )(feat, *pieces, out)


def swap_feat(array):
    return lax.ppermute(array, "feat", [(0, 1), (1, 0)])


def fetch(held, stride):
    count = lax.axis_size("patch")
    return lax.ppermute(held, "patch", [(pos, pos ^ stride) for pos in range(count)])


def even_offsets(count):
    assert count & (count - 1) == 0
    offsets = [0]
    stride = count // 2
    while stride > 1:
        offsets += [offset + stride for offset in offsets]
        stride //= 2
    return offsets


def shards(
    node_state, fine_tile, coarse_tile, fine_index, coarse_index, node_degree, w_msg, w_in, w_out
):
    barrier = lax.optimization_barrier
    patches = lax.axis_size("patch")
    patch_pos = lax.axis_index("patch")
    feat_pos = lax.axis_index("feat")
    feat = feat_pos.astype(jnp.int32).reshape(1)
    blocks, kinds, block, _ = fine_tile.shape
    half = blocks // 2
    half_rows = half * block
    halo_rows = HALO_BLK * block
    assert half == HALO_BLK == sum(MID_BLOCKS) == sum(LAST_BLOCKS)

    forward = [(pos, pos + 1) for pos in range(patches - 1)]
    backward = [(target, source) for source, target in forward]
    sides = ((0, backward), (1, forward))
    own_patch = [(2 * src + side, 2 * dst + side) for side, pairs in sides for src, dst in pairs]
    other_patch = [(2 * src + side, 2 * dst + 1 - side) for side, pairs in sides for src, dst in pairs]
    evens = even_offsets(patches)

    held = node_state[:CN_DEV]
    held = jnp.concatenate([held, fetch(held, 1)], axis=0)
    sends = []
    halo = []
    for first, count in MESSAGE_ROWS:
        message = message_call(node_state, w_msg, first * block, count * block, MESSAGE_TILES)
        if not sends:
            message, held = barrier((message, held))
        sends.append(message)
        halo.append(lax.ppermute(message, "patch", backward if first < half else forward))
    high = sends[-1]

    offsets = [even + odd for even in evens for odd in (0, 1)]
    fine_index, coarse_index, node_degree, w_in, w_out, w_late, _ = barrier(
        (fine_index, coarse_index, node_degree, w_in, w_out, w_msg, high)
    )
    links = (fine_index - (patch_pos * blocks - HALO_BLK)).reshape(-1) * block
    away = (coarse_index ^ patch_pos).reshape(-1)
    coarse_links = sum(jnp.where(away == offset, pos * CN_DEV, 0) for pos, offset in enumerate(offsets))
    links = jnp.concatenate([links, coarse_links])
    degree = node_degree.reshape(2, half, block)
    fine, ctile, state, table, in_own, out_own, msg_own = stage_call(
        feat, fine_tile, jnp.swapaxes(coarse_tile, 1, 2), node_state, sends, (w_in, w_out, w_late)
    )
    staged = (fine, ctile)
    others = weights_call([swap_feat(w_in), swap_feat(w_out), swap_feat(w_late)])
    strides = [patches >> step for step in range(1, patches.bit_length() - 1)]
    for step, stride in enumerate(strides):
        got = fetch(held, stride)
        if step == 0:
            got, links, degree, table = barrier((got, links, degree, table))
        if step == len(strides) - 1:
            got, others = barrier((got, others))
        held = jnp.concatenate([held, got], axis=0)
    coarse_state = held
    weights = [in_own, others[0], out_own, others[1], msg_own, others[2]]
    coarse = coarse_message_call(coarse_state, msg_own)

    halo_places = [
        lambda feat, at=first * block: halo_rows + 2 * half_rows + at if at < half_rows else at - half_rows
        for first, _ in MESSAGE_ROWS
    ]
    first_span, last_span = (0, MID_BLOCKS[0]), MID_BLOCKS
    send, keep, first_rows, table = aggregate_call(
        feat, links, staged, coarse, degree, table, first_span, halo_places, halo, True
    )
    recv = swap_feat(send)
    got = fetch(first_rows, 1)
    send_1, keep_1 = aggregate_call(feat, links, staged, coarse, degree, table, last_span)
    recv, keep, send_1 = barrier((recv, keep, send_1))
    inputs = [(keep, recv), (keep_1, swap_feat(send_1))]
    local = []
    local_places = []
    halo = []
    halo_places = []
    at = 0
    for chunk, count in enumerate(MID_BLOCKS):
        rows = count * block
        state, own, other = node_call("mid", 0, feat, state, at, 0, rows, *inputs[chunk], weights)
        if chunk == 0:
            own, other, got = barrier((own, other, got))
        sibling = swap_feat(other)
        if chunk == 0:
            sibling, state = barrier((sibling, state))
        halo += [lax.ppermute(own, ("patch", "feat"), own_patch), lax.ppermute(other, ("patch", "feat"), other_patch)]
        local += [own, sibling]
        local_places += [
            lambda feat, at=at: halo_rows + feat * half_rows + at,
            lambda feat, at=at: halo_rows + (1 - feat) * half_rows + at,
        ]
        halo_places += [
            lambda feat, at=at: (1 - feat) * (halo_rows + 2 * half_rows) + at,
            lambda feat, at=at: feat * (halo_rows + 2 * half_rows) + at,
        ]
        at += rows

    early = len(halo) - 2
    held = jnp.concatenate([first_rows, got], axis=0)
    held = jnp.concatenate([held, swap_feat(held)], axis=1)
    held, local[-1], *halo[:early] = barrier((held, local[-1], *halo[:early]))
    table = local_call(feat, local_places + halo_places[:early], local + halo[:early], table)
    held = jnp.concatenate([held] + [fetch(held, offset) for offset in evens[1:]], axis=0)
    (coarse,) = node_call(
        "coarse", 0, feat, coarse_state, 0, 0, held.shape[0], held, held, weights
    )
    send, keep, table = aggregate_call(
        feat, links, staged, coarse, degree, table, (0, LAST_BLOCKS[0]), halo_places[early:], halo[early:]
    )
    recv = swap_feat(send)
    send_1, keep_1 = aggregate_call(feat, links, staged, coarse, degree, table, LAST_BLOCKS)
    recv, keep, send_1 = barrier((recv, keep, send_1))
    inputs = [(keep, recv), (keep_1, swap_feat(send_1))]
    out = None
    swapped = []
    placed = []
    for chunk, offset, count in LAST_ROWS:
        at = (chunk * LAST_BLOCKS[0] + offset) * block
        done = 1 if len(swapped) == len(LAST_ROWS) - 1 else 0
        new_state, out = node_call(
            "last", 1, feat, state, at, offset * block, count * block, *inputs[chunk], weights,
            out, node_state.shape[0], placed[:done], swapped[:done],
        )
        swapped.append(swap_feat(new_state))
        placed.append(at)
    return assemble_call(feat, placed[1:], swapped[1:], out)


def solution(mesh):
    return jax.shard_map(
        shards,
        mesh=mesh,
        in_specs=(
            P(("member", "patch"), None),
            P("patch", None, None, None),
            P("patch", None, None),
            P("patch", None),
            P("patch", None),
            P("patch"),
            P(None, None, "feat"),
            P(None, None, "feat"),
            P(None, "feat", None),
        ),
        out_specs=P(("member", "patch"), None),
        check_vma=False,
    )
```

```python
import functools

import jax
import jax.numpy as jnp
from jax import lax
from jax.experimental import pallas as pl
from jax.experimental.pallas import tpu as pltpu
from jax.sharding import PartitionSpec as P

CN_DEV = 40
LAYERS = 2
HALO_BLK = 20
MID_BLOCKS = (10, 10)
LAST_BLOCKS = (10, 10)
LAST_ROWS = ((0, 0, 10), (1, 0, 8), (1, 8, 2))
MESSAGE_ROWS = ((0, 20), (20, 20))
MESSAGE_TILES = (512, 640, 640, 512, 256)
NODE_SPLIT = 2
F32 = jnp.float32
BF16 = jnp.bfloat16
LONG = pl.CostEstimate(flops=1 << 33, transcendentals=0, bytes_accessed=1 << 10)
SMALL = pl.CostEstimate(flops=1 << 20, transcendentals=0, bytes_accessed=1 << 10)
IN_VMEM = pl.BlockSpec(memory_space=pltpu.VMEM)
IN_HBM = pl.BlockSpec(memory_space=pltpu.HBM)


def silu(v):
    half = 0.5 * v
    return half + half * jnp.tanh(half)


def dot(a, b):
    return jnp.dot(a, b, preferred_element_type=F32)


def normalize(parts):
    width = sum(part.shape[-1] for part in parts)
    mean = sum(jnp.sum(part, axis=-1, keepdims=True) for part in parts) / width
    center = [part - mean for part in parts]
    spread = sum(jnp.sum(part * part, axis=-1, keepdims=True) for part in center) / width
    scale = lax.rsqrt(spread + 1e-05)
    return [(part * scale).astype(BF16) for part in center]


def params(mib):
    return pltpu.CompilerParams(vmem_limit_bytes=mib << 20)


def shaped(array):
    return jax.ShapeDtypeStruct(array.shape, array.dtype)


def run_copies(pairs, sems):
    copies = [pltpu.make_async_copy(src, dst, sems.at[pos]) for pos, (src, dst) in enumerate(pairs)]
    for copy in copies:
        copy.start()
    return copies


def wait_all(copies):
    for copy in copies:
        copy.wait()


def coarse_message_kernel(state_ref, weight_ref, out_ref):
    (normed,) = normalize([state_ref[...].astype(F32)])
    out_ref[...] = silu(dot(normed, weight_ref[0])).astype(BF16).astype(F32)


def message_kernel(start, sizes, state, weight, out, state_buf, weight_buf, out_ref, sems):
    tiles = [(sum(sizes[:pos]), size) for pos, size in enumerate(sizes)]
    pairs = [(state.at[pl.ds(start + at, size)], state_buf.at[pl.ds(at, size)]) for at, size in tiles]
    copies = run_copies(pairs[:1] + [(weight.at[0], weight_buf)] + pairs[1:], sems)
    weight_copy = copies.pop(1)
    normed = []
    for pos in range(len(tiles) + 1):
        if pos < len(tiles):
            at, size = tiles[pos]
            copies[pos].wait()
            normed += normalize([state_buf[at : at + size, :].astype(F32)])
        if pos == 0:
            weight_copy.wait()
            continue
        at, size = tiles[pos - 1]
        out_ref[at : at + size, :] = silu(dot(normed[pos - 1], weight_buf[...])).astype(BF16)
        span = pl.ds(at, size)
        copy = pltpu.make_async_copy(out_ref.at[span], out.at[span], sems.at[len(tiles) + pos])
        copy.start()
        copies.append(copy)
    wait_all(copies[len(tiles) :])


def message_call(state, weight, start, rows, sizes):
    assert sum(sizes) == rows
    width, columns = weight.shape[1:]
    return pl.pallas_call(
        functools.partial(message_kernel, start, sizes),
        in_specs=[IN_HBM, IN_HBM],
        out_specs=IN_HBM,
        out_shape=jax.ShapeDtypeStruct((rows, columns), BF16),
        scratch_shapes=[
            pltpu.VMEM((rows, width), BF16),
            pltpu.VMEM((width, columns), BF16),
            pltpu.VMEM((rows, columns), BF16),
            pltpu.SemaphoreType.DMA((1 + 2 * len(sizes),)),
        ],
        compiler_params=params(56),
        cost_estimate=SMALL,
        name="message",
    )(state, weight)


def coarse_message_call(state, weight):
    return pl.pallas_call(
        coarse_message_kernel,
        in_specs=[IN_VMEM, IN_VMEM],
        out_specs=IN_VMEM,
        out_shape=pltpu.VMEM((state.shape[0], weight.shape[2]), F32),
        compiler_params=params(12),
        cost_estimate=SMALL,
        name="coarse_message",
    )(state, weight)


def stage_kernel(locals_, count, feat_ref, *refs):
    fine, coarse, state = refs[:3]
    pieces = refs[3 : 3 + locals_]
    refs = refs[3 + locals_ :]
    weights = refs[:count]
    fine_out, coarse_out, state_out, table = refs[count : 4 + count]
    weights_out = refs[4 + count : 4 + 2 * count]
    coarse_buf, sems = refs[4 + 2 * count :]
    block = fine.shape[-1]
    half_rows = state_out.shape[0]
    pairs = [(coarse, coarse_buf)]
    pairs += [
        (fine.at[:, kind], fine_out.at[:, :, pl.ds(kind * block, block)]) for kind in range(fine.shape[1])
    ]
    start = pl.multiple_of(feat_ref[0] * half_rows, 16)
    pairs.append((state.at[pl.ds(start, half_rows)], state_out))
    at = HALO_BLK * block
    for piece in pieces:
        pairs.append((piece, table.at[pl.ds(at, piece.shape[0])]))
        at += piece.shape[0]
    pairs += list(zip(weights, weights_out))
    copies = run_copies(pairs, sems)
    copies[0].wait()

    def turn(pos, carry):
        coarse_out[pos] = jnp.transpose(coarse_buf[pos])
        return carry

    lax.fori_loop(0, coarse.shape[0], turn, 0)
    wait_all(copies[1:])


def stage_call(feat, fine, coarse, state, pieces, weights):
    blocks, kinds, block, _ = fine.shape
    rows, columns = blocks // 2 * block, pieces[0].shape[1]
    out_shape = [
        pltpu.VMEM((blocks, block, kinds * block), BF16),
        pltpu.VMEM((blocks, block, coarse.shape[1]), BF16),
        pltpu.VMEM((rows, state.shape[1]), BF16),
        pltpu.VMEM((2 * rows + 2 * HALO_BLK * block, columns), BF16),
    ] + [pltpu.VMEM(weight.shape, BF16) for weight in weights]
    copies = 2 + kinds + len(pieces) + len(weights)
    return pl.pallas_call(
        functools.partial(stage_kernel, len(pieces), len(weights)),
        grid_spec=pltpu.PrefetchScalarGridSpec(
            num_scalar_prefetch=1,
            in_specs=[IN_HBM] * (3 + len(pieces) + len(weights)),
            out_specs=[IN_VMEM] * len(out_shape),
            scratch_shapes=[pltpu.VMEM(coarse.shape, BF16), pltpu.SemaphoreType.DMA((copies,))],
        ),
        out_shape=out_shape,
        compiler_params=params(36),
        cost_estimate=SMALL,
        name="stage",
    )(feat, fine, coarse, state, *pieces, *weights)


def weights_kernel(*refs):
    sems = refs[-1]
    count = len(refs) // 2
    wait_all(run_copies(list(zip(refs[:count], refs[count:-1])), sems))


def weights_call(weights):
    return pl.pallas_call(
        weights_kernel,
        in_specs=[IN_HBM] * len(weights),
        out_specs=[IN_VMEM] * len(weights),
        scratch_shapes=[pltpu.SemaphoreType.DMA((len(weights),))],
        out_shape=[pltpu.VMEM(weight.shape, BF16) for weight in weights],
        compiler_params=params(4),
        cost_estimate=SMALL,
        name="weights",
    )(*weights)


def local_kernel(places, feat_ref, *refs):
    pieces = refs[: len(places)]
    table, sems = refs[-2:]
    pairs = []
    for place, piece in zip(places, pieces):
        start = pl.multiple_of(place(feat_ref[0]), 16)
        pairs.append((piece, table.at[pl.ds(start, piece.shape[0])]))
    wait_all(run_copies(pairs, sems))


def local_call(feat, places, pieces, table):
    return pl.pallas_call(
        functools.partial(local_kernel, places),
        grid_spec=pltpu.PrefetchScalarGridSpec(
            num_scalar_prefetch=1,
            in_specs=[pl.BlockSpec(memory_space=pl.ANY)] * len(pieces) + [IN_VMEM],
            out_specs=IN_VMEM,
            scratch_shapes=[pltpu.SemaphoreType.DMA((len(pieces),))],
        ),
        out_shape=pltpu.VMEM(table.shape, BF16),
        input_output_aliases={len(pieces) + 1: 0},
        compiler_params=params(4),
        cost_estimate=SMALL,
        name="local_messages",
    )(feat, *pieces, table)


def aggregate_kernel(places, start, feat_ref, links, *refs):
    fine, coarse_tile, coarse, degree = refs[:4]
    pieces = refs[4 : 4 + len(places)]
    if places:
        send, keep, *first_rows, table, sems = refs[5 + len(places) :]
        pairs = []
        for place, piece in zip(places, pieces):
            at = pl.multiple_of(place(feat_ref[0]), 16)
            pairs.append((piece, table.at[pl.ds(at, piece.shape[0])]))
        copies = run_copies(pairs, sems)
    else:
        table, send, keep = refs[4:]
        copies = []
    blocks, block, fine_width = fine.shape
    kinds = fine_width // block
    count = send.shape[0] // block
    feat = feat_ref[0]
    wait_all(copies)
    for out_ref, which in ((send, 1 - feat), (keep, feat)):
        scale = 1.0 / jnp.transpose(degree[which].astype(F32))
        first = which * (blocks // 2) + start
        for pos in range(count):
            row = (first + pos) * kinds
            chosen = jnp.concatenate(
                [table[pl.ds(pl.multiple_of(links[row + kind], block), block), :] for kind in range(kinds)], axis=0
            )
            base = blocks * kinds + row
            stacked = jnp.concatenate(
                [
                    coarse[pl.ds(pl.multiple_of(links[base + kind], 8), CN_DEV), :]
                    for kind in range(kinds)
                ],
                axis=0,
            ).astype(BF16)
            summed = dot(fine[first + pos], chosen) + dot(coarse_tile[first + pos], stacked)
            result = (summed * scale[:, start + pos : start + pos + 1]).astype(BF16)
            out_ref[pos * block : (pos + 1) * block, :] = result
    if places and first_rows:

        @pl.when(feat == 0)
        def _():
            first_rows[0][...] = keep[:CN_DEV, :]

        @pl.when(feat != 0)
        def _():
            first_rows[0][...] = send[:CN_DEV, :]


def aggregate_call(feat, links, staged, coarse, degree, table, span, places=(), pieces=(), wants_first=False):
    fine, coarse_tile = staged
    blocks, block, _ = fine.shape
    columns = table.shape[1]
    start, count = span
    out_shape = [pltpu.VMEM((count * block, columns), BF16)] * 2
    aliases = {}
    scratch = []
    if pieces:
        out_shape += [pltpu.VMEM((CN_DEV, columns), BF16)] * wants_first + [pltpu.VMEM(table.shape, BF16)]
        aliases = {6 + len(pieces): len(out_shape) - 1}
        scratch = [pltpu.SemaphoreType.DMA((len(pieces),))]
    return pl.pallas_call(
        functools.partial(aggregate_kernel, places, start),
        grid_spec=pltpu.PrefetchScalarGridSpec(
            num_scalar_prefetch=2,
            in_specs=[IN_VMEM] * 4 + [IN_HBM] * len(pieces) + [IN_VMEM],
            out_specs=[IN_VMEM] * len(out_shape),
            scratch_shapes=scratch,
        ),
        out_shape=out_shape,
        input_output_aliases=aliases,
        compiler_params=params(12),
        cost_estimate=SMALL,
        name="aggregate",
    )(feat, links, fine, coarse_tile, coarse, degree, *pieces, table)


def node_kernel(mode, layer, start, offset, rows, placed, feat_ref, *refs):
    state_ref, keep, recv, in_own, in_other, out_own, out_other = refs[:7]
    refs = refs[7:]
    feat = feat_ref[0]
    columns = in_own.shape[2]
    width = state_ref.shape[1]
    sides = ((keep, 0), (recv, columns if mode == "coarse" else 0))
    if mode == "last":
        state_out, out, sems = refs[-3:]
        half_rows = out.shape[0] // 2
        pairs = []
        for place, piece in zip(placed, refs):
            at = pl.multiple_of((1 - feat) * half_rows + place, 16)
            pairs.append((piece, out.at[pl.ds(at, piece.shape[0])]))
        copies = run_copies(pairs, sems)
    keep_at = pl.multiple_of(width + feat * columns, columns)
    recv_at = pl.multiple_of(width + (1 - feat) * columns, columns)
    split = NODE_SPLIT if rows >= 1024 else 1
    size = rows // split
    joined, hidden, state = {}, {}, {}

    def join(at):
        joined[at] = normalize(
            [state_ref[start + at : start + at + size, :].astype(F32)]
            + [ref[offset + at : offset + at + size, col : col + columns].astype(F32) for ref, col in sides]
        )

    def hide(at):
        parts = joined[at]
        hidden[at] = [
            silu(
                dot(parts[0], in_ref[layer, :width, :])
                + dot(parts[1], in_ref[layer, pl.ds(keep_at, columns), :])
                + dot(parts[2], in_ref[layer, pl.ds(recv_at, columns), :])
            ).astype(BF16)
            for in_ref in (in_own, in_other)
        ]

    def update(at):
        change = dot(hidden[at][0], out_own[layer]) + dot(hidden[at][1], out_other[layer])
        state[at] = (state_ref[start + at : start + at + size, :].astype(F32) + change).astype(BF16)
        if mode == "last":
            state_out[at : at + size, :] = state[at]
        elif mode == "mid":
            refs[2][start + at : start + at + size, :] = state[at]

    def norm(at):
        (joined[at],) = normalize([state[at].astype(F32)])

    def tell(at):
        if mode == "coarse":
            refs[1][...] = silu(dot(joined[at], refs[0][layer + 1])).astype(BF16).astype(F32)
            return
        for weight, message in ((refs[0], refs[3]), (refs[1], refs[4])):
            message[at : at + size, :] = silu(dot(joined[at], weight[layer + 1])).astype(BF16)

    stages = [join, hide, update] + ([] if mode == "last" else [norm, tell])
    for step in range(len(stages) + split - 1):
        for pos in range(split):
            if 0 <= step - pos < len(stages):
                stages[step - pos](pos * size)
    if mode == "last":
        at = pl.multiple_of(feat * half_rows + start, 16)
        copy = pltpu.make_async_copy(state_out, out.at[pl.ds(at, rows)], sems.at[len(placed)])
        copy.start()
        wait_all(copies)
        copy.wait()


def node_call(mode, layer, feat, state, start, offset, rows, keep, recv, weights, out=None, total=0, placed=(), pieces=()):
    columns = weights[0].shape[2]
    width = state.shape[1]
    operands = [state, keep, recv, *weights[:4]]
    aliases = {}
    scratch = []
    in_specs = [IN_VMEM] * len(operands)
    if mode == "last":
        out_shape = [pltpu.VMEM((rows, width), BF16), jax.ShapeDtypeStruct((total, width), BF16)]
        out_specs = [IN_VMEM, pl.BlockSpec(memory_space=pl.ANY)]
        scratch = [pltpu.SemaphoreType.DMA((1 + len(pieces),))]
        operands += pieces
        in_specs += [IN_VMEM] * len(pieces)
        if out is not None:
            aliases = {len(operands) + 1: 1}
            operands.append(out)
            in_specs.append(pl.BlockSpec(memory_space=pl.ANY))
    else:
        if mode == "coarse":
            operands.append(weights[4])
            out_shape = [pltpu.VMEM((rows, columns), F32)]
        else:
            operands += weights[4:]
            out_shape = [pltpu.VMEM(state.shape, BF16)] + [pltpu.VMEM((rows, columns), BF16)] * 2
            aliases = {1: 0}
        in_specs = [IN_VMEM] * len(operands)
        out_specs = [IN_VMEM] * len(out_shape)
    return pl.pallas_call(
        functools.partial(node_kernel, mode, layer, start, offset, rows, placed),
        grid_spec=pltpu.PrefetchScalarGridSpec(
            num_scalar_prefetch=1, in_specs=in_specs, out_specs=out_specs, scratch_shapes=scratch
        ),
        out_shape=out_shape,
        input_output_aliases=aliases,
        compiler_params=params(28),
        cost_estimate=LONG if mode == "last" else SMALL,
        name="node_" + mode,
    )(feat, *operands)


def assemble_kernel(placed, feat_ref, *refs):
    pieces = refs[: len(placed)]
    out, sems = refs[-2:]
    half_rows = out.shape[0] // 2
    pairs = []
    for place, piece in zip(placed, pieces):
        at = pl.multiple_of((1 - feat_ref[0]) * half_rows + place, 16)
        pairs.append((piece, out.at[pl.ds(at, piece.shape[0])]))
    wait_all(run_copies(pairs, sems))


def assemble_call(feat, placed, pieces, out):
    return pl.pallas_call(
        functools.partial(assemble_kernel, placed),
        grid_spec=pltpu.PrefetchScalarGridSpec(
            num_scalar_prefetch=1,
            in_specs=[IN_VMEM] * len(pieces) + [pl.BlockSpec(memory_space=pl.ANY)],
            out_specs=pl.BlockSpec(memory_space=pl.ANY),
            scratch_shapes=[pltpu.SemaphoreType.DMA((len(pieces),))],
        ),
        out_shape=shaped(out),
        input_output_aliases={len(pieces) + 1: 0},
        compiler_params=params(4),
        cost_estimate=SMALL,
        name="assemble",
    )(feat, *pieces, out)


def swap_feat(array):
    return lax.ppermute(array, "feat", [(0, 1), (1, 0)])


def fetch(held, stride):
    count = lax.axis_size("patch")
    return lax.ppermute(held, "patch", [(pos, pos ^ stride) for pos in range(count)])


def even_offsets(count):
    assert count & (count - 1) == 0
    offsets = [0]
    stride = count // 2
    while stride > 1:
        offsets += [offset + stride for offset in offsets]
        stride //= 2
    return offsets


def shards(
    node_state, fine_tile, coarse_tile, fine_index, coarse_index, node_degree, w_msg, w_in, w_out
):
    barrier = lax.optimization_barrier
    patches = lax.axis_size("patch")
    patch_pos = lax.axis_index("patch")
    feat_pos = lax.axis_index("feat")
    feat = feat_pos.astype(jnp.int32).reshape(1)
    blocks, kinds, block, _ = fine_tile.shape
    half = blocks // 2
    half_rows = half * block
    halo_rows = HALO_BLK * block
    assert half == HALO_BLK == sum(MID_BLOCKS) == sum(LAST_BLOCKS)

    forward = [(pos, pos + 1) for pos in range(patches - 1)]
    backward = [(target, source) for source, target in forward]
    sides = ((0, backward), (1, forward))
    own_patch = [(2 * src + side, 2 * dst + side) for side, pairs in sides for src, dst in pairs]
    other_patch = [(2 * src + side, 2 * dst + 1 - side) for side, pairs in sides for src, dst in pairs]
    evens = even_offsets(patches)

    held = node_state[:CN_DEV]
    held = jnp.concatenate([held, fetch(held, 1)], axis=0)
    sends = []
    halo = []
    for first, count in MESSAGE_ROWS:
        message = message_call(node_state, w_msg, first * block, count * block, MESSAGE_TILES)
        if not sends:
            message, held = barrier((message, held))
        sends.append(message)
        halo.append(lax.ppermute(message, "patch", backward if first < half else forward))
    high = sends[-1]

    offsets = [even + odd for even in evens for odd in (0, 1)]
    fine_index, coarse_index, node_degree, w_in, w_out, w_late, _ = barrier(
        (fine_index, coarse_index, node_degree, w_in, w_out, w_msg, high)
    )
    links = (fine_index - (patch_pos * blocks - HALO_BLK)).reshape(-1) * block
    away = (coarse_index ^ patch_pos).reshape(-1)
    coarse_links = sum(jnp.where(away == offset, pos * CN_DEV, 0) for pos, offset in enumerate(offsets))
    links = jnp.concatenate([links, coarse_links])
    degree = node_degree.reshape(2, half, block)
    fine, ctile, state, table, in_own, out_own, msg_own = stage_call(
        feat, fine_tile, jnp.swapaxes(coarse_tile, 1, 2), node_state, sends, (w_in, w_out, w_late)
    )
    staged = (fine, ctile)
    others = weights_call([swap_feat(w_in), swap_feat(w_out), swap_feat(w_late)])
    strides = [patches >> step for step in range(1, patches.bit_length() - 1)]
    for step, stride in enumerate(strides):
        got = fetch(held, stride)
        if step == 0:
            got, links, degree, table = barrier((got, links, degree, table))
        if step == len(strides) - 1:
            got, others = barrier((got, others))
        held = jnp.concatenate([held, got], axis=0)
    coarse_state = held
    weights = [in_own, others[0], out_own, others[1], msg_own, others[2]]
    coarse = coarse_message_call(coarse_state, msg_own)

    halo_places = [
        lambda feat, at=first * block: halo_rows + 2 * half_rows + at if at < half_rows else at - half_rows
        for first, _ in MESSAGE_ROWS
    ]
    first_span, last_span = (0, MID_BLOCKS[0]), MID_BLOCKS
    send, keep, first_rows, table = aggregate_call(
        feat, links, staged, coarse, degree, table, first_span, halo_places, halo, True
    )
    recv = swap_feat(send)
    got = fetch(first_rows, 1)
    send_1, keep_1 = aggregate_call(feat, links, staged, coarse, degree, table, last_span)
    recv, keep, send_1 = barrier((recv, keep, send_1))
    inputs = [(keep, recv), (keep_1, swap_feat(send_1))]
    local = []
    local_places = []
    halo = []
    halo_places = []
    at = 0
    for chunk, count in enumerate(MID_BLOCKS):
        rows = count * block
        state, own, other = node_call("mid", 0, feat, state, at, 0, rows, *inputs[chunk], weights)
        if chunk == 0:
            own, other, got = barrier((own, other, got))
        sibling = swap_feat(other)
        if chunk == 0:
            sibling, state = barrier((sibling, state))
        halo += [lax.ppermute(own, ("patch", "feat"), own_patch), lax.ppermute(other, ("patch", "feat"), other_patch)]
        local += [own, sibling]
        local_places += [
            lambda feat, at=at: halo_rows + feat * half_rows + at,
            lambda feat, at=at: halo_rows + (1 - feat) * half_rows + at,
        ]
        halo_places += [
            lambda feat, at=at: (1 - feat) * (halo_rows + 2 * half_rows) + at,
            lambda feat, at=at: feat * (halo_rows + 2 * half_rows) + at,
        ]
        at += rows

    early = len(halo) - 2
    held = jnp.concatenate([first_rows, got], axis=0)
    held = jnp.concatenate([held, swap_feat(held)], axis=1)
    held, local[-1], *halo[:early] = barrier((held, local[-1], *halo[:early]))
    table = local_call(feat, local_places + halo_places[:early], local + halo[:early], table)
    held = jnp.concatenate([held] + [fetch(held, offset) for offset in evens[1:]], axis=0)
    (coarse,) = node_call(
        "coarse", 0, feat, coarse_state, 0, 0, held.shape[0], held, held, weights
    )
    send, keep, table = aggregate_call(
        feat, links, staged, coarse, degree, table, (0, LAST_BLOCKS[0]), halo_places[early:], halo[early:]
    )
    recv = swap_feat(send)
    send_1, keep_1 = aggregate_call(feat, links, staged, coarse, degree, table, LAST_BLOCKS)
    recv, keep, send_1 = barrier((recv, keep, send_1))
    inputs = [(keep, recv), (keep_1, swap_feat(send_1))]
    out = None
    swapped = []
    placed = []
    for chunk, offset, count in LAST_ROWS:
        at = (chunk * LAST_BLOCKS[0] + offset) * block
        done = 1 if len(swapped) == len(LAST_ROWS) - 1 else 0
        new_state, out = node_call(
            "last", 1, feat, state, at, offset * block, count * block, *inputs[chunk], weights,
            out, node_state.shape[0], placed[:done], swapped[:done],
        )
        swapped.append(swap_feat(new_state))
        placed.append(at)
    return assemble_call(feat, placed[1:], swapped[1:], out)


def solution(mesh):
    return jax.shard_map(
        shards,
        mesh=mesh,
        in_specs=(
            P(("member", "patch"), None),
            P("patch", None, None, None),
            P("patch", None, None),
            P("patch", None),
            P("patch", None),
            P("patch"),
            P(None, None, "feat"),
            P(None, None, "feat"),
            P(None, "feat", None),
        ),
        out_specs=P(("member", "patch"), None),
        check_vma=False,
    )
```
